32 devices in a mesh: dp: 8 (over y, x, core), mp: 4 (over z).
Axes of the slice: x: 2, y: 2, z: 4, core: 2. Of those that a mesh axis runs over, the one named last changes fastest.
Arguments:
- patches: bfloat16 [16384, 1024], P(('dp', 'mp')), may hold values from -6 to 6
- cotangent: bfloat16 [16384, 1024], P(('dp', 'mp')), may hold values from -6 to 6
- lengths: int32 [16384], P(('dp', 'mp')), may hold values from 1 to 64, as said below
- hashes: int32 [16384], P(('dp', 'mp')), may hold values from 0 to 500001
- segments: int32 [8, 2048], P('dp'), may hold values from 0 to 3, never falling along the last dimension, each value on 1 to 1024 neighbouring positions
- attend_master: float32 [3, 256, 64, 64], P(None, ('dp', 'mp')), may hold values from -0.1875 to 0.1875
- output_master: float32 [256, 64, 64], P(('dp', 'mp')), may hold values from -2 to 2
- expand_master: float32 [2, 256, 64, 176], P(None, ('dp', 'mp')), may hold values from -0.1875 to 0.1875
- reduce_master: float32 [256, 176, 64], P(('dp', 'mp')), may hold values from -0.109375 to 0.109375
- gains: float32 [2, 1024], replicated, may hold values from 0.5 to 1.5
- attend_left: float32 [3, 256, 64, 64], P(None, ('dp', 'mp')), as said below
- attend_right: float32 [3, 256, 64, 64], P(None, ('dp', 'mp')), as said below
- output_left: float32 [256, 64, 64], P(('dp', 'mp')), as said below
- output_right: float32 [256, 64, 64], P(('dp', 'mp')), as said below
- expand_left: float32 [2, 256, 64, 64], P(None, ('dp', 'mp')), as said below
- expand_right: float32 [2, 256, 176, 176], P(None, ('dp', 'mp')), as said below
- reduce_left: float32 [256, 176, 176], P(('dp', 'mp')), as said below
- reduce_right: float32 [256, 64, 64], P(('dp', 'mp')), as said below
- gains_left: float32 [2, 2], replicated, as said below
- gains_right: float32 [1024], replicated, may hold values from 2 to 8
Outputs:
- activations: bfloat16 [16384, 1024], P(('dp', 'mp'))
- input_grad: float32 [16384, 1024], P(('dp', 'mp'))
- attend_grad: float32 [3, 256, 64, 64], P(None, ('dp', 'mp'))
- attend_weight: float32 [3, 256, 64, 64], P(None, ('dp', 'mp'))
- left_attend: float32 [3, 256, 64, 64], P(None, ('dp', 'mp'))
- right_attend: float32 [3, 256, 64, 64], P(None, ('dp', 'mp'))
- output_grad: float32 [256, 64, 64], P(('dp', 'mp'))
- output_weight: float32 [256, 64, 64], P(('dp', 'mp'))
- left_output: float32 [256, 64, 64], P(('dp', 'mp'))
- right_output: float32 [256, 64, 64], P(('dp', 'mp'))
- expand_grad: float32 [2, 256, 64, 176], P(None, ('dp', 'mp'))
- expand_weight: float32 [2, 256, 64, 176], P(None, ('dp', 'mp'))
- left_expand: float32 [2, 256, 64, 64], P(None, ('dp', 'mp'))
- right_expand: float32 [2, 256, 176, 176], P(None, ('dp', 'mp'))
- reduce_grad: float32 [256, 176, 64], P(('dp', 'mp'))
- reduce_weight: float32 [256, 176, 64], P(('dp', 'mp'))
- left_reduce: float32 [256, 176, 176], P(('dp', 'mp'))
- right_reduce: float32 [256, 64, 64], P(('dp', 'mp'))
- gains_grad: float32 [2, 1024], replicated
- gains_weight: float32 [2, 1024], replicated
- left_gains: float32 [2, 2], replicated
- right_gains: float32 [1024], replicated
The draws below stay inside these ranges and needn't reach their ends.
Inputs may be any that keep to these rules, and one draw needn't show every extreme that they name: `lengths`: the last patch has 64 bytes. `attend_left`: each matrix is symmetric; every diagonal entry is positive and larger than the sum of the magnitudes of the other entries of its row. `attend_right`: each matrix is symmetric; every diagonal entry is positive and larger than the sum of the magnitudes of the other entries of its row. `output_left`: each matrix is symmetric; every diagonal entry is positive and larger than the sum of the magnitudes of the other entries of its row. `output_right`: each matrix is symmetric; every diagonal entry is positive and larger than the sum of the magnitudes of the other entries of its row. `expand_left`: each matrix is symmetric; every diagonal entry is positive and larger than the sum of the magnitudes of the other entries of its row. `expand_right`: each matrix is symmetric; every diagonal entry is positive and larger than the sum of the magnitudes of the other entries of its row. `reduce_left`: each matrix is symmetric; every diagonal entry is positive and larger than the sum of the magnitudes of the other entries of its row. `reduce_right`: each matrix is symmetric; every diagonal entry is positive and larger than the sum of the magnitudes of the other entries of its row. `gains_left`: symmetric; each diagonal entry is positive and larger than the magnitude of the other entry of its row.
All inputs are finite; a program needn't handle non-finite values.
Results may differ from the reference program's by a relative error of at most 0.015.
The reference program's roundings to bfloat16 on the way count: a program that leaves them out, or rounds other values in their place, can miss the bound.
Values may be sent and summed in bfloat16 or wider, within the bound.
No kernel may reach another device: no remote copies, remote signals or barrier semaphores. Data moves between devices by JAX's collectives and lax.ppermute only.
A program may use at most 192 MiB of HBM per device.

```python
import math
import jax
import jax.numpy as jnp
import numpy as np
from jax import lax

D = 1024
HEADS = 16
HD = 64
FF = 2816
L = 2048
BLK = 64
FBLK = 176
HASH_B = 500002
ROOTS = 6
PATCHES = 16384
ROWS = 8
QB_ALL = 256
FB_ALL = 256
OUT_FAN = 8
N_DP = 8
N_MP = 4


def draw_lengths(key, part):
    position = jnp.arange(PATCHES, dtype=jnp.int32)
    upper_bound = 17 + 48 * position // PATCHES
    values = jax.random.randint(key, (PATCHES,), 1, upper_bound, dtype=jnp.int32)
    return jnp.where(position == PATCHES - 1, 64, values).astype(jnp.int32)


def draw_statistic(key, leading, matrix_size, level):
    diagonal_key, spread_key, sign_key = jax.random.split(key, 3)
    diagonal = level * jnp.exp(jax.random.uniform(diagonal_key, leading + (matrix_size,), jnp.float32, 0.0, math.log(4.0)))
    magnitude = jax.random.uniform(spread_key, leading + (matrix_size, matrix_size), jnp.float32, 0.7, 1.0)
    flips = jax.random.bernoulli(sign_key, 0.5, leading + (matrix_size, matrix_size))
    entries = jnp.where(flips, magnitude, -magnitude)
    places = jnp.arange(matrix_size, dtype=jnp.int32)
    upper = places[:, None] < places[None, :]
    entries = jnp.where(upper, entries, jnp.swapaxes(entries, -1, -2))
    spread = entries * (0.9 * level / max(matrix_size - 1, 1))
    identity = jnp.eye(matrix_size, dtype=jnp.float32)
    return (spread * (1.0 - identity) + identity * diagonal[..., None]).astype(jnp.float32)


def draw_attend_left(key, part):
    return draw_statistic(jax.random.fold_in(key, 11), (3, QB_ALL), BLK, BLK * 0.125)


def draw_attend_right(key, part):
    return draw_statistic(jax.random.fold_in(key, 12), (3, QB_ALL), BLK, BLK * 0.125)


def draw_output_left(key, part):
    return draw_statistic(jax.random.fold_in(key, 13), (QB_ALL,), BLK, BLK * 36.0 / L)


def draw_output_right(key, part):
    return draw_statistic(jax.random.fold_in(key, 14), (QB_ALL,), BLK, BLK * 36.0 / L)


def draw_expand_left(key, part):
    return draw_statistic(jax.random.fold_in(key, 15), (2, FB_ALL), BLK, FBLK * 0.25)


def draw_expand_right(key, part):
    return draw_statistic(jax.random.fold_in(key, 16), (2, FB_ALL), FBLK, BLK * 0.25)


def draw_reduce_left(key, part):
    return draw_statistic(jax.random.fold_in(key, 17), (FB_ALL,), FBLK, BLK * 0.5)


def draw_reduce_right(key, part):
    return draw_statistic(jax.random.fold_in(key, 18), (FB_ALL,), BLK, FBLK * 0.5)


def draw_gains_left(key, part):
    return draw_statistic(jax.random.fold_in(key, 19), (), 2, D * 1.0)


def place_ends(array, rng, low, high):
    place = [jax.random.randint(jax.random.fold_in(rng, axis), (), 0, length) for axis, length in enumerate(array.shape)]
    main_axis = array.shape.index(max(array.shape))
    beside = place[:main_axis] + [(place[main_axis] + 1) % array.shape[main_axis]] + place[main_axis + 1:]
    return array.at[tuple(place)].set(low).at[tuple(beside)].set(high)


def steps_of(own_key, shape, shards, low, largest):
    level = 1.0
    for dim, shards_of in shards:
        steps = jax.random.uniform(jax.random.fold_in(jax.random.fold_in(own_key, 6), dim), (shards_of,), jnp.float32, low / len(shards), largest / len(shards))
        level = level * jnp.repeat(jnp.exp(steps), shape[dim] // shards_of).reshape((-1,) + (1,) * (len(shape) - 1 - dim))
    return level


def skewed_wide(rng, dims, number_of, lean):
    weights = [min(1 << octave, number_of + 1 - (1 << octave)) * (1 << 20) // math.isqrt((1 << octave) ** lean) + 1 for octave in range((number_of + 1).bit_length()) if 1 << octave <= number_of]
    scale = 1 + sum(weights) // (1 << 30)
    table = np.cumsum(np.array([max(1, weight // scale) for weight in weights]))
    lot = jax.random.randint(jax.random.fold_in(rng, 1), dims, 0, int(table[len(weights) - 1]))
    start = jnp.left_shift(1, jnp.searchsorted(jnp.asarray(table, jnp.int32), lot, side="right").astype(jnp.int32))
    rank = start - 1 + jax.random.randint(jax.random.fold_in(rng, 4), dims, 0, 1 << 30) % jnp.minimum(start, number_of + 1 - start)
    return jax.random.permutation(jax.random.fold_in(rng, 2), number_of)[rank].astype(jnp.int32)


def length_profile(amount, total, most, slope):
    loads = [(1 << 20) // math.isqrt(standing ** slope) + 1 for standing in range(2, amount + 1)]
    surplus, given = total - most - (amount - 1), [1] * (amount - 1)
    while surplus > 0:
        free = [i for i in range(amount - 1) if given[i] < most]
        pool, left = sum([loads[i] for i in free]), surplus
        for i in free:
            addition = min(most - given[i], max(1, left * loads[i] // pool), surplus)
            given[i] = given[i] + addition
            surplus = surplus - addition
    return np.array([most] + given)


def ragged_sizes(own_key, amount, total, most, slope):
    if amount == 2:
        one = jax.random.randint(own_key, (), max(1, total - most), min(most, total - 1) + 1)
        return jnp.stack([one, total - one])
    tallies = jnp.asarray(length_profile(amount, total, most, slope), jnp.int32)
    twos = (amount - 1) // 2
    giver, sink = tallies[1:1 + 2 * twos:2], tallies[2:2 + 2 * twos:2]
    slack = jnp.minimum(giver - 1, most - sink)
    shifted = jax.random.randint(jax.random.fold_in(own_key, 1), (twos,), 0, 1 << 20) % (slack + 1)
    tallies = tallies.at[1:1 + 2 * twos:2].set(giver - shifted).at[2:2 + 2 * twos:2].set(sink + shifted)
    return tallies[jax.random.permutation(jax.random.fold_in(own_key, 2), amount)]


def bell_draw(own_key, extent, scale, limit, pieces=(), held_as=jnp.bfloat16):
    gain = steps_of(own_key, extent, pieces, -0.22, 0.18) if pieces else 1.0
    values = jax.random.normal(own_key, extent, jnp.float32) * scale * gain
    return jnp.minimum(jnp.maximum(values, -limit), limit).astype(held_as)


def setup_inputs(seed: int = 0) -> dict:
    key_list = jax.random.split(jax.random.key(seed), 21)
    return {
        "patches": bell_draw(key_list[0], (PATCHES, D), 1.0, 6.0, ((0, 32),)),
        "cotangent": bell_draw(key_list[1], (PATCHES, D), 1.0, 6.0, ((0, 32),)),
        "lengths": draw_lengths(jax.random.fold_in(key_list[20], 71), 0),
        "hashes": place_ends(skewed_wide(key_list[3], (PATCHES,), HASH_B, 1), jax.random.fold_in(key_list[3], 3), 0, HASH_B - 1).astype(jnp.int32),
        "segments": jax.vmap(lambda own: jnp.searchsorted(jnp.cumsum(ragged_sizes(own, 4, L, L // 2, 1)), jnp.arange(L), side="right"))(jax.random.split(key_list[4], ROWS)).reshape((ROWS, L)).astype(jnp.int32),
        "attend_master": bell_draw(key_list[5], (3, QB_ALL, BLK, BLK), D ** -0.5, 0.1875, ((1, 32),), jnp.float32),
        "output_master": bell_draw(key_list[6], (QB_ALL, BLK, BLK), OUT_FAN ** -0.5, 2.0, ((0, 32),), jnp.float32),
        "expand_master": bell_draw(key_list[7], (2, FB_ALL, BLK, FBLK), D ** -0.5, 0.1875, ((1, 32),), jnp.float32),
        "reduce_master": bell_draw(key_list[8], (FB_ALL, FBLK, BLK), FF ** -0.5, 0.109375, ((0, 32),), jnp.float32),
        "gains": jnp.clip(1.0 + 0.1 * jax.random.normal(key_list[9], (2, D), jnp.float32), 0.5, 1.5),
        "attend_left": draw_attend_left(jax.random.fold_in(key_list[20], 71), 0),
        "attend_right": draw_attend_right(jax.random.fold_in(key_list[20], 71), 0),
        "output_left": draw_output_left(jax.random.fold_in(key_list[20], 71), 0),
        "output_right": draw_output_right(jax.random.fold_in(key_list[20], 71), 0),
        "expand_left": draw_expand_left(jax.random.fold_in(key_list[20], 71), 0),
        "expand_right": draw_expand_right(jax.random.fold_in(key_list[20], 71), 0),
        "reduce_left": draw_reduce_left(jax.random.fold_in(key_list[20], 71), 0),
        "reduce_right": draw_reduce_right(jax.random.fold_in(key_list[20], 71), 0),
        "gains_left": draw_gains_left(jax.random.fold_in(key_list[20], 71), 0),
        "gains_right": jnp.clip(jnp.exp(jax.random.uniform(key_list[19], (D,), jnp.float32, math.log(2.0), math.log(8.0))), 2.0, 8.0),
    }


EPSILON = 1e-05
STEP_RATE = 16.0
GAIN_RATE = 2.0
HIGHEST = lax.Precision.HIGHEST
MASKED = -1e+30

@jax.custom_vjp
def low(v):
    return lax.optimization_barrier(v.astype(jnp.bfloat16)).astype(jnp.float32)

@jax.custom_vjp
def low_back(v):
    return v

def low_keep(v):
    return (low(v), None)

def low_pass(kept, grad):
    return (grad,)

def back_keep(v):
    return (v, None)

def back_low(kept, grad):
    return (low(grad),)
low.defvjp(low_keep, low_pass)
low_back.defvjp(back_keep, back_low)

def gather_blocks(blocked, row_count, by_columns):
    leading = blocked.shape[:-3]
    block_count, height, width = blocked.shape[-3:]
    per_owner = block_count // (N_DP * N_MP)
    grid = blocked.reshape(leading + (N_DP, N_MP, per_owner, height, width))
    grid = jnp.swapaxes(grid, -5, -4)
    row_blocks = row_count // height
    column_blocks = N_DP * per_owner // row_blocks
    grid = grid.reshape(leading + (N_MP, row_blocks, column_blocks, height, width))
    grid = jnp.swapaxes(grid, -3, -2)
    shard_view = grid.reshape(leading + (N_MP, row_blocks * height, column_blocks * width))
    if by_columns:
        shard_view = jnp.swapaxes(shard_view, -3, -2)
        return shard_view.reshape(leading + (row_blocks * height, N_MP * column_blocks * width))
    return shard_view.reshape(leading + (N_MP * row_blocks * height, column_blocks * width))

def scatter_blocks(matrix, row_count, height, width, by_columns):
    leading = matrix.shape[:-2]
    if by_columns:
        shard_view = matrix.reshape(leading + (row_count, N_MP, matrix.shape[-1] // N_MP))
        shard_view = jnp.swapaxes(shard_view, -3, -2)
    else:
        shard_view = matrix.reshape(leading + (N_MP, row_count, matrix.shape[-1]))
    column_count = shard_view.shape[-1]
    row_blocks = row_count // height
    column_blocks = column_count // width
    grid = shard_view.reshape(leading + (N_MP, row_blocks, height, column_blocks, width))
    grid = jnp.swapaxes(grid, -3, -2)
    per_owner = row_blocks * column_blocks // N_DP
    grid = grid.reshape(leading + (N_MP, N_DP, per_owner, height, width))
    grid = jnp.swapaxes(grid, -5, -4)
    return grid.reshape(leading + (N_DP * N_MP * per_owner, height, width))

def product(first, second):
    return jnp.einsum('...ij,...jk->...ik', first, second, precision=HIGHEST)

def quarter_root(statistic):
    matrix_size = statistic.shape[-1]
    identity = jnp.eye(matrix_size, dtype=jnp.float32)
    frobenius = jnp.sqrt(lax.optimization_barrier(jnp.sum(statistic * statistic, axis=(-2, -1), keepdims=True)) + 1e-06)
    matrix = statistic / frobenius
    estimate = jnp.broadcast_to(identity, statistic.shape)
    for iteration in range(ROOTS):
        update = (5.0 * identity - matrix) * 0.25
        estimate = product(estimate, update)
        squared = product(update, update)
        matrix = product(product(squared, squared), matrix)
    return estimate * lax.rsqrt(jnp.sqrt(frobenius))

def shampoo(gradient, master, left_old, right_old, step_size):
    left_new = 0.5 * left_old + 0.5 * jnp.einsum('...ij,...kj->...ik', gradient, gradient, precision=HIGHEST)
    right_new = 0.5 * right_old + 0.5 * jnp.einsum('...ji,...jk->...ik', gradient, gradient, precision=HIGHEST)
    direction = product(product(quarter_root(left_new), gradient), quarter_root(right_new))
    return (master - step_size * direction, left_new, right_new)

def gain_update(gradient, gain_rows, left_old, right_old):
    left_new = 0.5 * left_old + 0.5 * jnp.einsum('id,jd->ij', gradient, gradient, precision=HIGHEST)
    right_new = 0.5 * right_old + 0.5 * lax.optimization_barrier(jnp.sum(gradient * gradient, axis=0))
    direction = jnp.einsum('ij,jd->id', quarter_root(left_new), gradient, precision=HIGHEST) * lax.rsqrt(jnp.sqrt(right_new))
    return (gain_rows - GAIN_RATE * direction, left_new, right_new)

def attend_row(parts):
    queries, key_rows, values, labels = parts
    positions = jnp.arange(L, dtype=jnp.int32)
    scores = low_back(jnp.einsum('qhd,khd->hqk', queries, key_rows, precision=HIGHEST) * HD ** (-0.5))
    allowed = (labels[:, None] == labels[None, :]) & (positions[:, None] >= positions[None, :])
    scores = jnp.where(allowed[None], scores, MASKED)
    maximum = lax.optimization_barrier(jnp.max(scores, axis=2, keepdims=True))
    powers = jnp.exp(scores - maximum)
    attention = low(powers / lax.optimization_barrier(jnp.sum(powers, axis=2, keepdims=True)))
    return jnp.einsum('hqk,khd->qhd', attention, values, precision=HIGHEST)

def block_layer(stream, w_query, w_key, w_value, w_out, w_gate, w_up, w_down, gain_rows, segments):
    first_hat = stream * lax.rsqrt(lax.optimization_barrier(jnp.mean(stream * stream, axis=1, keepdims=True)) + EPSILON)
    first_normed = low(first_hat * gain_rows[0])
    queries = low_back(low(jnp.dot(first_normed, w_query, precision=HIGHEST)))
    key_rows = low_back(low(jnp.dot(first_normed, w_key, precision=HIGHEST)))
    values = low_back(low(jnp.dot(first_normed, w_value, precision=HIGHEST)))
    shape_rows = (stream.shape[0] // L, L, HEADS, HD)
    context = lax.map(jax.checkpoint(attend_row), (queries.reshape(shape_rows), key_rows.reshape(shape_rows), values.reshape(shape_rows), segments))
    context = low_back(low(context.reshape(stream.shape[0], HEADS * HD)))
    middle = stream + low_back(jnp.dot(context, w_out, precision=HIGHEST))
    second_hat = middle * lax.rsqrt(lax.optimization_barrier(jnp.mean(middle * middle, axis=1, keepdims=True)) + EPSILON)
    second_normed = low(second_hat * gain_rows[1])
    gate_pre = low_back(jnp.dot(second_normed, w_gate, precision=HIGHEST))
    up_pre = low_back(jnp.dot(second_normed, w_up, precision=HIGHEST))
    hidden = low(jax.nn.silu(gate_pre) * up_pre)
    return middle + low_back(jnp.dot(hidden, w_down, precision=HIGHEST))

def reference(patches, cotangent, lengths, hashes, segments, attend_master, output_master, expand_master, reduce_master, gains, attend_left, attend_right, output_left, output_right, expand_left, expand_right, reduce_left, reduce_right, gains_left, gains_right):
    counts = jnp.zeros((HASH_B,), jnp.int32).at[hashes].add(1)
    raw_weight = lengths.astype(jnp.float32) * lax.rsqrt(counts[hashes].astype(jnp.float32))
    patch_weight = raw_weight / jnp.mean(raw_weight)
    grad_out = cotangent.astype(jnp.float32) * patch_weight[:, None]
    head_width = HEADS * HD // N_MP
    hidden_width = FF // N_MP
    attend_full = low(gather_blocks(attend_master, D, True))
    output_full = low(gather_blocks(output_master, head_width, False))
    expand_full = low(gather_blocks(expand_master, D, True))
    reduce_full = low(gather_blocks(reduce_master, hidden_width, False))

    def forward(stream, w_query, w_key, w_value, w_out, w_gate, w_up, w_down, gain_rows):
        return block_layer(stream, w_query, w_key, w_value, w_out, w_gate, w_up, w_down, gain_rows, segments)
    result, pull = jax.vjp(forward, patches.astype(jnp.float32), attend_full[0], attend_full[1], attend_full[2], output_full, expand_full[0], expand_full[1], reduce_full, gains)
    grads = pull(grad_out)
    grad_scale = lax.rsqrt(jnp.asarray(PATCHES, jnp.float32))
    attend_grad = scatter_blocks(jnp.stack([grads[1], grads[2], grads[3]]) * grad_scale, D, BLK, BLK, True)
    output_grad = scatter_blocks(grads[4] * grad_scale, head_width, BLK, BLK, False)
    expand_grad = scatter_blocks(jnp.stack([grads[5], grads[6]]) * grad_scale, D, BLK, FBLK, True)
    reduce_grad = scatter_blocks(grads[7] * grad_scale, hidden_width, FBLK, BLK, False)
    gains_grad = grads[8] * grad_scale
    attend_weight, left_attend, right_attend = shampoo(attend_grad, attend_master, attend_left, attend_right, STEP_RATE * D ** (-0.5))
    output_weight, left_output, right_output = shampoo(output_grad, output_master, output_left, output_right, STEP_RATE * OUT_FAN ** (-0.5))
    expand_weight, left_expand, right_expand = shampoo(expand_grad, expand_master, expand_left, expand_right, STEP_RATE * D ** (-0.5))
    reduce_weight, left_reduce, right_reduce = shampoo(reduce_grad, reduce_master, reduce_left, reduce_right, STEP_RATE * FF ** (-0.5))
    gains_weight, left_gains, right_gains = gain_update(gains_grad, gains, gains_left, gains_right)
    return (result.astype(jnp.bfloat16), grads[0], attend_grad, attend_weight, left_attend, right_attend, output_grad, output_weight, left_output, right_output, expand_grad, expand_weight, left_expand, right_expand, reduce_grad, reduce_weight, left_reduce, right_reduce, gains_grad, gains_weight, left_gains, right_gains)
```

```python
import functools

import jax
import jax.numpy as jnp
from jax import lax
from jax.experimental import pallas as pl
from jax.experimental.pallas import tpu as pltpu
from jax.sharding import PartitionSpec as P

D = 1024
HEADS = 16
HD = 64
FF = 2816
BLK = 64
FBLK = 176
ROOTS = 6
OUT_FAN = 8
SPAN = 1024

EPSILON = 1e-05
STEP_RATE = 16.0
GAIN_RATE = 2.0
MASKED = -1e30
F32 = jnp.float32
BF16 = jnp.bfloat16
PAIR = 2 * HD


def piece_shape(blocked_shape, group_rows, dp_size):
    per_owner, height, width = blocked_shape[-3:]
    column_blocks = dp_size * per_owner // (group_rows // height)
    if per_owner % column_blocks == 0:
        rows, columns = per_owner // column_blocks, column_blocks
    else:
        rows, columns = 1, per_owner
    grid_columns = column_blocks // columns
    return rows, columns, dp_size // grid_columns, grid_columns


def to_piece(blocked, rows, columns):
    leading = blocked.shape[:-3]
    height, width = blocked.shape[-2:]
    grid = blocked.reshape(leading + (rows, columns, height, width))
    return jnp.swapaxes(grid, -3, -2).reshape(leading + (rows * height, columns * width))


def from_piece(piece, rows, columns):
    leading = piece.shape[:-2]
    height, width = piece.shape[-2] // rows, piece.shape[-1] // columns
    grid = piece.reshape(leading + (rows, height, columns, width))
    return jnp.swapaxes(grid, -3, -2).reshape(leading + (rows * columns, height, width))


def gather_all(piece):
    return lax.all_gather(lax.all_gather(piece, "mp"), "dp")


def scatter_all(parts):
    reduced = lax.psum_scatter(parts, "dp", scatter_dimension=0, tiled=False)
    return lax.psum_scatter(reduced, "mp", scatter_dimension=0, tiled=False)


def weight_by_columns(master, dp_size):
    rows, columns, grid_rows, grid_columns = piece_shape(master.shape, D, dp_size)
    gathered = gather_all(to_piece(master.astype(BF16), rows, columns))
    dp, mp, members, height, width = gathered.shape
    grid = gathered.reshape(grid_rows, grid_columns, mp, members, height, width)
    grid = jnp.transpose(grid, (3, 0, 4, 2, 1, 5))
    return grid.reshape(members, grid_rows * height, mp * grid_columns * width)


def weight_by_rows(master, group_rows, dp_size):
    rows, columns, grid_rows, grid_columns = piece_shape(master.shape, group_rows, dp_size)
    gathered = gather_all(to_piece(master.astype(BF16), rows, columns))
    dp, mp, height, width = gathered.shape
    grid = gathered.reshape(grid_rows, grid_columns, mp, height, width)
    grid = jnp.transpose(grid, (2, 0, 3, 1, 4))
    return grid.reshape(mp * grid_rows * height, grid_columns * width)


def grad_by_columns(matrix, master, dp_size, mp_size):
    rows, columns, grid_rows, grid_columns = piece_shape(master.shape, D, dp_size)
    members = matrix.shape[0]
    height, width = rows * master.shape[-2], columns * master.shape[-1]
    grid = matrix.reshape(members, grid_rows, height, mp_size, grid_columns, width)
    grid = jnp.transpose(grid, (1, 4, 3, 0, 2, 5))
    parts = grid.reshape(dp_size, mp_size, members, height, width)
    return from_piece(scatter_all(parts).astype(F32), rows, columns)


def grad_by_rows(matrix, master, group_rows, dp_size, mp_size):
    rows, columns, grid_rows, grid_columns = piece_shape(master.shape, group_rows, dp_size)
    height, width = rows * master.shape[-2], columns * master.shape[-1]
    grid = matrix.reshape(mp_size, grid_rows, height, grid_columns, width)
    grid = jnp.transpose(grid, (1, 3, 0, 2, 4))
    parts = grid.reshape(dp_size, mp_size, height, width)
    return from_piece(scatter_all(parts).astype(F32), rows, columns)


def exchanges():
    for axis in ("dp", "mp"):
        size = lax.axis_size(axis)
        step = 1
        while step < size:
            yield axis, [(i, i ^ step) for i in range(size)]
            step *= 2


def gather_small(values):
    for axis, pairs in exchanges():
        values = jnp.concatenate([values, lax.ppermute(values, axis, pairs)], axis=0)
    return values


def sum_small(values):
    for axis, pairs in exchanges():
        values = values + lax.ppermute(values, axis, pairs)
    return values


def fill_bias(bias_ref, query_labels, key_labels, tile, tile_count, history):
    for t in range(tile_count):
        span = SPAN + tile
        key_pos = lax.broadcasted_iota(jnp.int32, (span, tile), 0) + (history - SPAN + t * tile)
        query_pos = lax.broadcasted_iota(jnp.int32, (span, tile), 1) + (history + t * tile)
        same = key_labels[pl.ds(history - SPAN + t * tile, span), :] == query_labels[:, pl.ds(t * tile, tile)]
        bias_ref[t] = jnp.where(same & (key_pos <= query_pos), 0.0, MASKED)


def head_rows(values, head):
    row = lax.broadcasted_iota(jnp.int32, values.shape, 0)
    return jnp.where((row >= head * HD) & (row < (head + 1) * HD), values, jnp.zeros_like(values))


def head_lanes(values, head):
    lane = lax.broadcasted_iota(jnp.int32, values.shape, 1)
    return jnp.where((lane >= head * HD) & (lane < (head + 1) * HD), values, jnp.zeros_like(values))


def attend_kernel(tile, history, query_labels, key_labels, q_ref, k_ref, v_ref, o_ref, lse_ref, bias_ref, vt_ref):
    tile_count = q_ref.shape[0] // tile
    span = SPAN + tile

    @pl.when(pl.program_id(0) == 0)
    def _():
        fill_bias(bias_ref, query_labels, key_labels, tile, tile_count, history)

    vt_ref[...] = v_ref[...].T
    for t in range(tile_count):
        base = history - SPAN + t * tile
        queries = (q_ref[pl.ds(t * tile, tile), :] * HD ** (-0.5)).astype(BF16).T
        keys = k_ref[pl.ds(base, span), :]
        outputs = []
        for head in range(2):
            scores = (
                jnp.dot(keys, head_rows(queries, head), preferred_element_type=F32) + bias_ref[t]
            )
            maximum = jnp.max(scores, axis=0, keepdims=True)
            powers = jnp.exp(scores - maximum)
            total = jnp.sum(powers, axis=0, keepdims=True)
            attention = (powers * (1.0 / total)).astype(BF16)
            outputs.append(
                jnp.dot(
                    vt_ref[pl.ds(head * HD, HD), pl.ds(base, span)],
                    attention,
                    preferred_element_type=F32,
                )
            )
            lse_ref[0, pl.ds(head, 1), pl.ds(t * tile, tile)] = maximum + jnp.log(total)
        o_ref[pl.ds(t * tile, tile), :] = jnp.concatenate(outputs, axis=0).T.astype(BF16)


def attend_back_kernel(
    tile, history, query_labels, key_labels, q_ref, k_ref, v_ref, o_ref, do_ref, lse_ref,
    dq_ref, dk_ref, dv_ref, bias_ref, kt_ref, dk_acc, dv_acc,
):
    tile_count = q_ref.shape[0] // tile
    span = SPAN + tile

    @pl.when(pl.program_id(0) == 0)
    def _():
        fill_bias(bias_ref, query_labels, key_labels, tile, tile_count, history)

    kt_ref[...] = k_ref[...].T
    dk_acc[...] = jnp.zeros_like(dk_acc)
    dv_acc[...] = jnp.zeros_like(dv_acc)
    for t in range(tile_count):
        base = history - SPAN + t * tile
        scaled = (q_ref[pl.ds(t * tile, tile), :] * HD ** (-0.5)).astype(BF16)
        grads = do_ref[pl.ds(t * tile, tile), :]
        scaled_t, grads_t = scaled.T, grads.T
        product_t = grads_t.astype(F32) * o_ref[pl.ds(t * tile, tile), :].T.astype(F32)
        keys = k_ref[pl.ds(base, span), :]
        values = v_ref[pl.ds(base, span), :]
        grad_queries = []
        for head in range(2):
            scores = (
                jnp.dot(keys, head_rows(scaled_t, head), preferred_element_type=F32) + bias_ref[t]
            )
            attention = jnp.exp(scores - lse_ref[0, pl.ds(head, 1), pl.ds(t * tile, tile)])
            row_terms = jnp.sum(product_t[head * HD : (head + 1) * HD], axis=0, keepdims=True)
            grad_attention = jnp.dot(values, head_rows(grads_t, head), preferred_element_type=F32)
            grad_scores = (attention * (grad_attention - row_terms)).astype(BF16)
            dv_acc[pl.ds(base, span), :] += jnp.dot(
                attention.astype(BF16), head_lanes(grads, head), preferred_element_type=F32
            )
            dk_acc[pl.ds(base, span), :] += jnp.dot(
                grad_scores, head_lanes(scaled, head), preferred_element_type=F32
            )
            grad_queries.append(
                jnp.dot(
                    kt_ref[pl.ds(head * HD, HD), pl.ds(base, span)],
                    grad_scores,
                    preferred_element_type=F32,
                )
            )
        dq_ref[pl.ds(t * tile, tile), :] = (
            jnp.concatenate(grad_queries, axis=0).T * HD ** (-0.5)
        ).astype(BF16)
    dk_ref[...] = dk_acc[...].astype(BF16)
    dv_ref[...] = dv_acc[...].astype(BF16)


def attention_specs(count, window):
    whole = lambda shape: pl.BlockSpec(shape, lambda h: (0,) * len(shape))
    own = pl.BlockSpec((count, PAIR), lambda h: (0, h))
    seen = pl.BlockSpec((window, PAIR), lambda h: (0, h))
    sums = pl.BlockSpec((1, 2, count), lambda h: (h, 0, 0))
    labels = [whole((1, count)), whole((window, 1))]
    return labels, own, seen, sums


def attend(queries, keys, values, query_labels, key_labels, tile):
    count, width = queries.shape
    window = keys.shape[0]
    pairs = width // PAIR
    labels, own, seen, sums = attention_specs(count, window)
    work = 2 * count * (SPAN + tile) * width
    return pl.pallas_call(
        functools.partial(attend_kernel, tile, window - count),
        grid=(pairs,),
        in_specs=labels + [own, seen, seen],
        out_specs=[own, sums],
        out_shape=[
            jax.ShapeDtypeStruct((count, width), BF16),
            jax.ShapeDtypeStruct((pairs, 2, count), F32),
        ],
        scratch_shapes=[
            pltpu.VMEM((count // tile, SPAN + tile, tile), F32),
            pltpu.VMEM((PAIR, window), BF16),
        ],
        cost_estimate=pl.CostEstimate(
            flops=2 * work, bytes_accessed=4 * (window + count) * width, transcendentals=0
        ),
        name="attend",
    )(query_labels, key_labels, queries, keys, values)


def attend_back(queries, keys, values, context, grads, sums_in, query_labels, key_labels, tile):
    count, width = queries.shape
    window = keys.shape[0]
    pairs = width // PAIR
    labels, own, seen, sums = attention_specs(count, window)
    work = 2 * count * (SPAN + tile) * width
    return pl.pallas_call(
        functools.partial(attend_back_kernel, tile, window - count),
        grid=(pairs,),
        in_specs=labels + [own, seen, seen, own, own, sums],
        out_specs=[own, seen, seen],
        out_shape=[
            jax.ShapeDtypeStruct((count, width), BF16),
            jax.ShapeDtypeStruct((window, width), BF16),
            jax.ShapeDtypeStruct((window, width), BF16),
        ],
        scratch_shapes=[
            pltpu.VMEM((count // tile, SPAN + tile, tile), F32),
            pltpu.VMEM((PAIR, window), BF16),
            pltpu.VMEM((window, PAIR), F32),
            pltpu.VMEM((window, PAIR), F32),
        ],
        cost_estimate=pl.CostEstimate(
            flops=5 * work, bytes_accessed=8 * (window + count) * width, transcendentals=0
        ),
        name="attend_back",
    )(query_labels, key_labels, queries, keys, values, context, grads, sums_in)


def product(first, second):
    return jnp.einsum("...ij,...jk->...ik", first, second, precision=lax.Precision.HIGH)


def quarter_root(statistic):
    matrix_size = statistic.shape[-1]
    identity = jnp.eye(matrix_size, dtype=F32)
    frobenius = jnp.sqrt(jnp.sum(statistic * statistic, axis=(-2, -1), keepdims=True) + 1e-06)
    matrix = statistic / frobenius
    estimate = None
    for iteration in range(ROOTS):
        update = (5.0 * identity - matrix) * 0.25
        estimate = update if estimate is None else product(estimate, update)
        if iteration < ROOTS - 1:
            squared = product(update, update)
            matrix = product(product(squared, squared), matrix)
    return estimate * lax.rsqrt(jnp.sqrt(frobenius))


def shampoo(gradient, master, left_old, right_old, step_size):
    highest = lax.Precision.HIGH
    left_new = 0.5 * left_old + 0.5 * jnp.einsum(
        "...ij,...kj->...ik", gradient, gradient, precision=highest
    )
    right_new = 0.5 * right_old + 0.5 * jnp.einsum(
        "...ji,...jk->...ik", gradient, gradient, precision=highest
    )
    direction = product(product(quarter_root(left_new), gradient), quarter_root(right_new))
    return (master - step_size * direction, left_new, right_new)


def two_by_two(first, second):
    (a, b), (c, d) = first
    (e, f), (g, h) = second
    return ((a * e + b * g, a * f + b * h), (c * e + d * g, c * f + d * h))


def quarter_root_pair(statistic):
    entries = tuple(tuple(statistic[i, j] for j in range(2)) for i in range(2))
    frobenius = jnp.sqrt(sum(v * v for row in entries for v in row) + 1e-06)
    matrix = tuple(tuple(v / frobenius for v in row) for row in entries)
    estimate = ((1.0, 0.0), (0.0, 1.0))
    for iteration in range(ROOTS):
        (a, b), (c, d) = matrix
        update = (((5.0 - a) * 0.25, -b * 0.25), (-c * 0.25, (5.0 - d) * 0.25))
        estimate = two_by_two(estimate, update)
        squared = two_by_two(update, update)
        matrix = two_by_two(two_by_two(squared, squared), matrix)
    scale = lax.rsqrt(jnp.sqrt(frobenius))
    return tuple(tuple(v * scale for v in row) for row in estimate)


def gain_update(gradient, gain_rows, left_old, right_old):
    outer = jnp.sum(gradient[:, None, :] * gradient[None, :, :], axis=2)
    left_new = 0.5 * left_old + 0.5 * outer
    right_new = 0.5 * right_old + 0.5 * jnp.sum(gradient * gradient, axis=0)
    (a, b), (c, d) = quarter_root_pair(left_new)
    first, second = gradient[0], gradient[1]
    mixed = jnp.stack([a * first + b * second, c * first + d * second])
    direction = mixed * lax.rsqrt(jnp.sqrt(right_new))
    return (gain_rows - GAIN_RATE * direction, left_new, right_new)


def dot(first, second):
    return jnp.dot(first, second, preferred_element_type=F32)


def dot_back(first, second):
    return lax.dot_general(first, second, (((1,), (1,)), ((), ())), preferred_element_type=F32)


def dot_weight(first, second):
    return lax.dot_general(first, second, (((0,), (0,)), ((), ())), preferred_element_type=F32)


def body(
    patches,
    cotangent,
    lengths,
    hashes,
    segments,
    attend_master,
    output_master,
    expand_master,
    reduce_master,
    gains,
    attend_left,
    attend_right,
    output_left,
    output_right,
    expand_left,
    expand_right,
    reduce_left,
    reduce_right,
    gains_left,
    gains_right,
):
    dp_size, mp_size = lax.axis_size("dp"), lax.axis_size("mp")
    mp_index = lax.axis_index("mp")
    count = patches.shape[0]
    head_width, hidden_width = D // mp_size, FF // mp_size
    total_patches = count * dp_size * mp_size
    earlier = -(-(SPAN - 1) // count)
    history = earlier * count
    tile = min(256, count)

    attend_w = weight_by_columns(attend_master, dp_size)
    output_w = weight_by_rows(output_master, head_width, dp_size)
    expand_w = weight_by_columns(expand_master, dp_size)
    reduce_w = weight_by_rows(reduce_master, hidden_width, dp_size)

    stream = patches.astype(F32)
    first_rms = lax.rsqrt(jnp.mean(stream * stream, axis=1, keepdims=True) + EPSILON)
    first_hat = stream * first_rms
    first_normed = (first_hat * gains[0]).astype(BF16)
    up_one = [(i, i + 1) for i in range(mp_size - 1)]
    down_one = [(i + 1, i) for i in range(mp_size - 1)]
    shards = [first_normed]
    for _ in range(earlier):
        shards.insert(0, lax.ppermute(shards[0], "mp", up_one))
    window = jnp.concatenate(shards, axis=0)

    row_labels = segments.reshape(-1)
    padded = jnp.concatenate([jnp.full((history,), -1, jnp.int32), row_labels])
    key_labels = lax.dynamic_slice_in_dim(padded, mp_index * count, history + count, 0)
    query_labels = key_labels[history:].reshape(1, count)
    key_labels = key_labels.reshape(-1, 1)

    all_hashes = gather_small(hashes)
    own_counts = jnp.sum((hashes[:, None] == all_hashes[None, :]).astype(F32), axis=1)
    raw_weight = lengths.astype(F32) * lax.rsqrt(own_counts)
    raw_total = sum_small(jnp.sum(raw_weight).reshape(1, 1))
    patch_weight = raw_weight * (total_patches / raw_total[0, 0])
    grad_out = cotangent.astype(F32) * patch_weight[:, None]
    grad_low = grad_out.astype(BF16)

    queries = dot(first_normed, attend_w[0]).astype(BF16)
    keys = dot(window, attend_w[1]).astype(BF16)
    values = dot(window, attend_w[2]).astype(BF16)
    context, log_sums = attend(queries, keys, values, query_labels, key_labels, tile)
    middle = stream + dot(context, output_w)

    second_rms = lax.rsqrt(jnp.mean(middle * middle, axis=1, keepdims=True) + EPSILON)
    second_hat = middle * second_rms
    second_normed = (second_hat * gains[1]).astype(BF16)
    gate_pre = dot(second_normed, expand_w[0])
    up_pre = dot(second_normed, expand_w[1])
    gate_sig = jax.nn.sigmoid(gate_pre)
    hidden = (gate_pre * gate_sig * up_pre).astype(BF16)
    activations = (middle + dot(hidden, reduce_w)).astype(BF16)

    grad_hidden = dot_back(grad_low, reduce_w)
    grad_up = (grad_hidden * gate_pre * gate_sig).astype(BF16)
    grad_gate = (grad_hidden * up_pre * gate_sig * (1.0 + gate_pre * (1.0 - gate_sig))).astype(BF16)
    reduce_local = dot_weight(hidden, grad_low).astype(BF16)
    expand_local = jnp.stack(
        [dot_weight(second_normed, grad_gate), dot_weight(second_normed, grad_up)]
    ).astype(BF16)
    reduce_sum = grad_by_rows(reduce_local, reduce_master, hidden_width, dp_size, mp_size)
    expand_sum = grad_by_columns(expand_local, expand_master, dp_size, mp_size)

    second_back = dot_back(grad_gate, expand_w[0]) + dot_back(grad_up, expand_w[1])
    second_scaled = second_back * gains[1]
    gain_second = jnp.sum(second_back * second_hat, axis=0)
    middle_grad = grad_out + second_rms * (
        second_scaled - second_hat * jnp.mean(second_scaled * second_hat, axis=1, keepdims=True)
    )
    middle_low = middle_grad.astype(BF16)
    output_local = dot_weight(context, middle_low).astype(BF16)
    grad_context = dot_back(middle_low, output_w).astype(BF16)
    output_sum = grad_by_rows(output_local, output_master, head_width, dp_size, mp_size)

    grad_queries, grad_keys, grad_values = attend_back(
        queries, keys, values, context, grad_context, log_sums, query_labels, key_labels, tile
    )
    attend_local = jnp.stack(
        [
            dot_weight(first_normed, grad_queries),
            dot_weight(window, grad_keys),
            dot_weight(window, grad_values),
        ]
    ).astype(BF16)
    attend_sum = grad_by_columns(attend_local, attend_master, dp_size, mp_size)
    window_back = dot_back(grad_keys, attend_w[1]) + dot_back(grad_values, attend_w[2])
    own_back = window_back[history:] + dot_back(grad_queries, attend_w[0])
    gain_first = (
        jnp.sum(own_back * first_normed.astype(F32), axis=0)
        + jnp.sum(window_back[:history] * window[:history].astype(F32), axis=0)
    ) / gains[0]
    carried = None
    for k in range(earlier):
        share = window_back[k * count : (k + 1) * count]
        share = share if carried is None else share + carried
        carried = lax.ppermute(share.astype(BF16), "mp", down_one).astype(F32)
    first_back = own_back + carried
    first_scaled = first_back * gains[0]
    input_grad = middle_grad + first_rms * (
        first_scaled - first_hat * jnp.mean(first_scaled * first_hat, axis=1, keepdims=True)
    )

    grad_scale = total_patches ** (-0.5)
    gains_grad = sum_small(jnp.stack([gain_first, gain_second])) * grad_scale
    attend_grad = attend_sum * grad_scale
    output_grad = output_sum * grad_scale
    expand_grad = expand_sum * grad_scale
    reduce_grad = reduce_sum * grad_scale
    reduce_weight, left_reduce, right_reduce = shampoo(
        reduce_grad, reduce_master, reduce_left, reduce_right, STEP_RATE * FF ** (-0.5)
    )
    expand_weight, left_expand, right_expand = shampoo(
        expand_grad, expand_master, expand_left, expand_right, STEP_RATE * D ** (-0.5)
    )
    output_weight, left_output, right_output = shampoo(
        output_grad, output_master, output_left, output_right, STEP_RATE * OUT_FAN ** (-0.5)
    )
    attend_weight, left_attend, right_attend = shampoo(
        attend_grad, attend_master, attend_left, attend_right, STEP_RATE * D ** (-0.5)
    )
    gains_weight, left_gains, right_gains = gain_update(gains_grad, gains, gains_left, gains_right)
    return (
        activations,
        input_grad,
        attend_grad,
        attend_weight,
        left_attend,
        right_attend,
        output_grad,
        output_weight,
        left_output,
        right_output,
        expand_grad,
        expand_weight,
        left_expand,
        right_expand,
        reduce_grad,
        reduce_weight,
        left_reduce,
        right_reduce,
        gains_grad,
        gains_weight,
        left_gains,
        right_gains,
    )


def solution(mesh):
    rows = P(("dp", "mp"), None)
    single = P(("dp", "mp"), None, None)
    stacked = P(None, ("dp", "mp"), None, None)
    return jax.shard_map(
        body,
        mesh=mesh,
        in_specs=(
            rows,
            rows,
            P(("dp", "mp")),
            P(("dp", "mp")),
            P("dp", None),
            stacked,
            single,
            stacked,
            single,
            P(),
            stacked,
            stacked,
            single,
            single,
            stacked,
            stacked,
            single,
            single,
            P(),
            P(),
        ),
        out_specs=(
            rows,
            rows,
            stacked,
            stacked,
            stacked,
            stacked,
            single,
            single,
            single,
            single,
            stacked,
            stacked,
            stacked,
            stacked,
            single,
            single,
            single,
            single,
            P(),
            P(),
            P(),
            P(),
        ),
        check_vma=False,
    )
```

```python
import functools

import jax
import jax.numpy as jnp
from jax import lax
from jax.experimental import pallas as pl
from jax.experimental.pallas import tpu as pltpu
from jax.sharding import PartitionSpec as P

D = 1024
HEADS = 16
HD = 64
FF = 2816
BLK = 64
FBLK = 176
ROOTS = 6
OUT_FAN = 8
SPAN = 1024

EPSILON = 1e-05
STEP_RATE = 16.0
GAIN_RATE = 2.0
MASKED = -1e30
F32 = jnp.float32
BF16 = jnp.bfloat16
PAIR = 2 * HD


CHIPS = 4
LANES = 128


def piece_shape(blocked_shape, group_rows, dp_size):
    per_owner, height, width = blocked_shape[-3:]
    column_blocks = dp_size * per_owner // (group_rows // height)
    if per_owner % column_blocks == 0:
        rows, columns = per_owner // column_blocks, column_blocks
    else:
        rows, columns = 1, per_owner
    grid_columns = column_blocks // columns
    return rows, columns, dp_size // grid_columns, grid_columns


def to_piece(blocked, rows, columns):
    leading = blocked.shape[:-3]
    height, width = blocked.shape[-2:]
    grid = blocked.reshape(leading + (rows, columns, height, width))
    return jnp.swapaxes(grid, -3, -2).reshape(leading + (rows * height, columns * width))


def from_piece(piece, rows, columns):
    leading = piece.shape[:-2]
    height, width = piece.shape[-2] // rows, piece.shape[-1] // columns
    grid = piece.reshape(leading + (rows, height, columns, width))
    return jnp.swapaxes(grid, -3, -2).reshape(leading + (rows * columns, height, width))


def rows_of_columns(piece):
    return jnp.swapaxes(piece, -1, -2).reshape(-1, LANES)


def columns_of_rows(rows, members):
    return jnp.swapaxes(rows.reshape(members, -1, LANES), -1, -2)


def rows_of_rows(piece):
    height, width = piece.shape
    return jnp.swapaxes(piece.reshape(height, width // LANES, LANES), 0, 1).reshape(-1, LANES)


def rows_to_rows(rows, blocks):
    grid = jnp.swapaxes(rows.reshape(blocks, -1, LANES), 0, 1)
    return grid.reshape(grid.shape[0], blocks * LANES)


def together(*values):
    return lax.optimization_barrier(values)


def pairwise(values, axis, step):
    return lax.ppermute(values, axis, [(i, i ^ step) for i in range(lax.axis_size(axis))])


def gather_sides(slices):
    return pairwise(slices, "dp", 2), pairwise(slices, "dp", 4), pairwise(slices, "dp", 1)


def gather_corner(across_x, across_y, other):
    half = across_x.shape[1] // 2
    return (
        pairwise(across_y[:, :half], "dp", 2),
        pairwise(across_x[:, half:], "dp", 4),
        pairwise(across_x, "dp", 1),
        pairwise(across_y, "dp", 1),
    )


def gather_end(slices, across_x, across_y, other, corner_x, corner_y, other_x, other_y):
    corner = jnp.concatenate([corner_x, corner_y], axis=1)
    return (
        slices, across_x, across_y, corner, other, other_x, other_y, pairwise(corner, "dp", 1)
    )


def part_sum(own_core, received, chip, low, high):
    return own_core[chip, :, low:high].astype(F32) + received[chip, :, low:high].astype(F32)


def reduce_chips_corner(own_core, received):
    half = own_core.shape[2] // 2
    corner_x = pairwise(part_sum(own_core, received, 3, 0, half).astype(BF16), "dp", 2)
    corner_y = pairwise(part_sum(own_core, received, 3, half, None).astype(BF16), "dp", 4)
    return corner_x, corner_y


def reduce_chips_sides(own_core, received, corner_x, corner_y):
    half = own_core.shape[2] // 2
    to_y = jnp.concatenate(
        [
            part_sum(own_core, received, 2, 0, half) + corner_x.astype(F32),
            part_sum(own_core, received, 2, half, None),
        ],
        axis=1,
    ).astype(BF16)
    to_x = jnp.concatenate(
        [
            part_sum(own_core, received, 1, 0, half),
            part_sum(own_core, received, 1, half, None) + corner_y.astype(F32),
        ],
        axis=1,
    ).astype(BF16)
    return pairwise(to_x, "dp", 2), pairwise(to_y, "dp", 4)


def reduce_chips_own(own_core, received, from_x, from_y):
    return part_sum(own_core, received, 0, 0, None) + from_x.astype(F32) + from_y.astype(F32)


def coordinate(fast):
    return lax.axis_index("dp").astype(jnp.int32).reshape(1) if fast else jnp.zeros((1,), jnp.int32)


def gather_all(piece):
    return lax.all_gather(lax.all_gather(piece, "mp"), "dp")


def scatter_all(parts):
    reduced = lax.psum_scatter(parts, "dp", scatter_dimension=0, tiled=False)
    return lax.psum_scatter(reduced, "mp", scatter_dimension=0, tiled=False)


def weight_by_columns(master, dp_size):
    rows, columns, grid_rows, grid_columns = piece_shape(master.shape, D, dp_size)
    gathered = gather_all(to_piece(master.astype(BF16), rows, columns))
    mp, members, height, width = gathered.shape[1:]
    grid = gathered.reshape(grid_rows, grid_columns, mp, members, height, width)
    grid = jnp.transpose(grid, (3, 0, 4, 2, 1, 5))
    return grid.reshape(members, grid_rows * height, mp * grid_columns * width)


def weight_by_rows(master, group_rows, dp_size):
    rows, columns, grid_rows, grid_columns = piece_shape(master.shape, group_rows, dp_size)
    gathered = gather_all(to_piece(master.astype(BF16), rows, columns))
    mp, height, width = gathered.shape[1:]
    grid = gathered.reshape(grid_rows, grid_columns, mp, height, width)
    grid = jnp.transpose(grid, (2, 0, 3, 1, 4))
    return grid.reshape(mp * grid_rows * height, grid_columns * width)


def grad_by_columns(matrix, master, dp_size, mp_size):
    rows, columns, grid_rows, grid_columns = piece_shape(master.shape, D, dp_size)
    members = matrix.shape[0]
    height, width = rows * master.shape[-2], columns * master.shape[-1]
    grid = matrix.reshape(members, grid_rows, height, mp_size, grid_columns, width)
    grid = jnp.transpose(grid, (1, 4, 3, 0, 2, 5))
    parts = grid.reshape(dp_size, mp_size, members, height, width)
    return from_piece(scatter_all(parts).astype(F32), rows, columns)


def grad_by_rows(matrix, master, group_rows, dp_size, mp_size):
    rows, columns, grid_rows, grid_columns = piece_shape(master.shape, group_rows, dp_size)
    height, width = rows * master.shape[-2], columns * master.shape[-1]
    grid = matrix.reshape(mp_size, grid_rows, height, grid_columns, width)
    grid = jnp.transpose(grid, (1, 3, 0, 2, 4))
    parts = grid.reshape(dp_size, mp_size, height, width)
    return from_piece(scatter_all(parts).astype(F32), rows, columns)


def cut_columns(matrices, mp_size):
    members, _, width = matrices.shape
    grid = matrices.reshape(members, CHIPS, 2, LANES, mp_size, width // mp_size)
    return jnp.transpose(grid, (1, 2, 4, 0, 5, 3)).reshape(CHIPS, 2, mp_size, -1, LANES)


def join_columns(pieces, members):
    grid = pieces.reshape(pieces.shape[:3] + (members, -1, LANES))
    return jnp.transpose(grid, (3, 0, 1, 5, 2, 4)).reshape(members, D, -1)


def cut_rows(matrix, mp_size):
    grid = matrix.reshape(mp_size, CHIPS, matrix.shape[0] // (mp_size * CHIPS), 2, D // (2 * LANES), LANES)
    return jnp.transpose(grid, (1, 3, 0, 4, 2, 5)).reshape(CHIPS, 2, mp_size, -1, LANES)


def join_rows(pieces):
    grid = pieces.reshape(pieces.shape[:3] + (D // (2 * LANES), -1, LANES))
    return jnp.transpose(grid, (2, 0, 4, 1, 3, 5)).reshape(-1, D)


def lanes_of(device, relative):
    return pl.ds(pl.multiple_of((device ^ relative) * LANES, LANES), LANES)


def half_lanes(device, core, block):
    start = ((device & 1) ^ core) * (D // 2) + block * LANES
    return pl.ds(pl.multiple_of(start, LANES), LANES)


def rows_at(device, chip, height):
    return pl.ds(pl.multiple_of(((device >> 1) ^ chip) * height, 16), height)


def join_attend_kernel(device_ref, *refs):
    device = device_ref[0]
    attend_ref, output_ref = refs[2 * CHIPS :]
    height = attend_ref.shape[1]
    for core in range(2):
        for chip in range(CHIPS):
            piece = refs[core * CHIPS + chip]
            lanes = lanes_of(device, 2 * chip + core)
            for member in range(3):
                attend_ref[member, :, lanes] = piece[0, pl.ds(member * height, height), :]
            rows = rows_at(device, chip, height // CHIPS)
            for block in range(D // (2 * LANES)):
                output_ref[rows, half_lanes(device, core, block)] = piece[
                    0, pl.ds(3 * height + block * (height // CHIPS), height // CHIPS), :
                ]


def cut_attend_kernel(device_ref, query, key, value, output, first, second):
    device = device_ref[0]
    height = query.shape[0]
    for core, pieces in enumerate((first, second)):
        for chip in range(CHIPS):
            lanes = lanes_of(device, 2 * chip + core)
            for member, matrix in enumerate((query, key, value)):
                pieces[chip, 0, pl.ds(member * height, height), :] = matrix[:, lanes]
            rows = rows_at(device, chip, height // CHIPS)
            for block in range(D // (2 * LANES)):
                pieces[chip, 0, pl.ds(3 * height + block * (height // CHIPS), height // CHIPS), :] = (
                    output[rows, half_lanes(device, core, block)]
                )


def grid_call(
    kernel, grid, in_specs, out_specs, out_shape, name, scratch=(), cost=None, aliases=None
):
    return pl.pallas_call(
        kernel,
        grid_spec=pltpu.PrefetchScalarGridSpec(
            num_scalar_prefetch=1,
            grid=grid,
            in_specs=in_specs,
            out_specs=out_specs,
            scratch_shapes=scratch,
        ),
        out_shape=out_shape,
        input_output_aliases=aliases or {},
        cost_estimate=cost,
        name=name,
    )


def moved(count):
    return pl.CostEstimate(flops=0, bytes_accessed=2 * count, transcendentals=0)


def join_attend(device, pieces):
    slices = pieces[0].shape[0]
    height = D // slices
    piece = pl.BlockSpec((1, 4 * height, LANES), lambda k, d: (k, 0, 0))
    return grid_call(
        join_attend_kernel,
        (slices,),
        [piece] * (2 * CHIPS),
        [
            pl.BlockSpec((3, height, D), lambda k, d: (0, k, 0)),
            pl.BlockSpec((height, D), lambda k, d: (k, 0)),
        ],
        [jax.ShapeDtypeStruct((3, D, D), BF16), jax.ShapeDtypeStruct((D, D), BF16)],
        "join_attend",
        cost=moved(8 * D * D),
    )(device, *pieces)


def cut_attend(device, matrices, slices):
    height = matrices[0].shape[0] // slices
    matrix = pl.BlockSpec((height, D), lambda k, d: (k, 0))
    piece = pl.BlockSpec((CHIPS, 1, 4 * height, LANES), lambda k, d: (0, k, 0, 0))
    shape = jax.ShapeDtypeStruct((CHIPS, slices, 4 * height, LANES), BF16)
    return grid_call(
        cut_attend_kernel,
        (slices,),
        [matrix] * 4,
        [piece, piece],
        [shape, shape],
        "cut_attend",
        cost=moved(8 * slices * height * D),
    )(device, *matrices)


def hidden_kernel(
    kept, device_ref, normed_ref, grads_ref, *refs
):
    parts = refs[: 6 * CHIPS]
    result_ref, back_ref, first, second = refs[6 * CHIPS + kept : 6 * CHIPS + kept + 4]
    (
        normed_t, grads_t, w_gate, w_up, w_down, hidden_t, dgate_t, dup_t, moved_ref
    ) = refs[6 * CHIPS + kept + 4 :]
    device = device_ref[0]
    width = w_gate.shape[0]
    height = width // CHIPS
    blocks = D // (2 * LANES)

    @pl.when(pl.program_id(0) == 0)
    def _():
        normed_t[...] = normed_ref[...].T
        grads_t[...] = grads_ref[...].T
        result_ref[...] = jnp.zeros_like(result_ref)
        back_ref[...] = jnp.zeros_like(back_ref)

    for core in range(2):
        for chip in range(CHIPS):
            gate, up, down = parts[3 * (core * CHIPS + chip) : 3 * (core * CHIPS + chip + 1)]
            lanes = lanes_of(device, 2 * chip + core)
            w_gate[:, lanes] = gate[0]
            w_up[:, lanes] = up[0]
            for block in range(blocks):
                w_down[rows_at(device, chip, height), half_lanes(device, core, block)] = down[
                    0, pl.ds(block * height, height), :
                ]

    @pl.loop(0, CHIPS)
    def _(j):
        start = pl.multiple_of(j * height, 16)
        rows = pl.ds(start, height)
        gate_pre = jnp.dot(w_gate[rows, :], normed_t[...], preferred_element_type=F32)
        up_pre = jnp.dot(w_up[rows, :], normed_t[...], preferred_element_type=F32)
        grad_hidden = jnp.dot(w_down[rows, :], grads_t[...], preferred_element_type=F32)
        sig = jax.nn.sigmoid(gate_pre)
        silu = gate_pre * sig
        hidden = (silu * up_pre).astype(BF16)
        dup = (grad_hidden * silu).astype(BF16)
        dgate = (grad_hidden * up_pre * sig * (1.0 + gate_pre * (1.0 - sig))).astype(BF16)
        hidden_t[rows, :] = hidden
        dup_t[rows, :] = dup
        dgate_t[rows, :] = dgate

        moved_ref[...] = jnp.dot(hidden, grads_ref[...], preferred_element_type=F32).astype(BF16)
        chip = (device >> 1) ^ j
        for core, pieces in enumerate((first, second)):
            for block in range(blocks):
                pieces[chip, 0, pl.ds(2 * width + block * height, height), :] = moved_ref[
                    :, half_lanes(device, core, block)
                ]
        for member, values in enumerate((dgate, dup)):
            moved_ref[...] = jnp.dot(values, normed_ref[...], preferred_element_type=F32).astype(BF16)
            target = pl.ds(pl.multiple_of(member * width + start, 16), height)
            for core, pieces in enumerate((first, second)):
                for chip in range(CHIPS):
                    pieces[chip, 0, target, :] = moved_ref[:, lanes_of(device, 2 * chip + core)]

    tile = min(256, normed_ref.shape[0])
    for t in range(normed_ref.shape[0] // tile):
        rows = pl.ds(t * tile, tile)
        result_ref[rows, :] += jnp.dot(
            hidden_t[:, rows].T, w_down[...], preferred_element_type=F32
        )
        back_ref[rows, :] += jnp.dot(
            dgate_t[:, rows].T, w_gate[...], preferred_element_type=F32
        ) + jnp.dot(dup_t[:, rows].T, w_up[...], preferred_element_type=F32)


def hidden_layer(device, normed, grads, pieces, width, start, slices, earlier=()):
    count = normed.shape[0]
    whole = pl.BlockSpec((count, D), lambda k, d: (0, 0))
    piece = lambda part: pl.BlockSpec((1, width, LANES), lambda k, d: (start + k, part, 0))
    out_piece = pl.BlockSpec((CHIPS, 1, 3 * width, LANES), lambda k, d: (0, start + k, 0, 0))
    shape = jax.ShapeDtypeStruct((CHIPS, pieces[0].shape[0], 3 * width, LANES), BF16)
    total = jax.ShapeDtypeStruct((count, D), F32)
    first_kept = 3 + 6 * CHIPS
    return grid_call(
        functools.partial(hidden_kernel, len(earlier)),
        (slices,),
        [whole, whole]
        + [piece(part) for part in range(3)] * (2 * CHIPS)
        + [pl.BlockSpec(memory_space=pl.ANY)] * len(earlier),
        [whole, whole, out_piece, out_piece],
        [total, total, shape, shape],
        "hidden_layer",
        scratch=[
            pltpu.VMEM((D, count), BF16),
            pltpu.VMEM((D, count), BF16),
            pltpu.VMEM((width, D), BF16),
            pltpu.VMEM((width, D), BF16),
            pltpu.VMEM((width, D), BF16),
            pltpu.VMEM((width, count), BF16),
            pltpu.VMEM((width, count), BF16),
            pltpu.VMEM((width, count), BF16),
            pltpu.VMEM((width // CHIPS, D), BF16),
        ],
        cost=pl.CostEstimate(
            flops=18 * slices * width * D * count,
            bytes_accessed=12 * slices * width * D,
            transcendentals=0,
        ),
        aliases={first_kept + i: 2 + i for i in range(len(earlier))},
    )(device, normed, grads, *[piece for piece in pieces for _ in range(3)], *earlier)


def exchanges():
    for axis in ("dp", "mp"):
        size = lax.axis_size(axis)
        step = 1
        while step < size:
            yield axis, [(i, i ^ step) for i in range(size)]
            step *= 2


def hash_rows(hashes):
    digits = jnp.stack([hashes >> 14, (hashes >> 7) & 127, hashes & 127])
    rows = digits.astype(BF16).reshape(-1, LANES)
    return jnp.pad(rows, ((0, -rows.shape[0] % 32), (0, 0)))


def rows_hash(rows, count):
    used = 3 * count // LANES
    digits = rows[..., :used, :].reshape(-1, 3, count).astype(F32)
    return ((digits[:, 0] * 128.0 + digits[:, 1]) * 128.0 + digits[:, 2]).reshape(-1)


def gather_small(values):
    for axis, pairs in exchanges():
        values = jnp.concatenate([values, lax.ppermute(values, axis, pairs)], axis=0)
    return values


def sum_small(values):
    for axis, pairs in exchanges():
        values = values + lax.ppermute(values, axis, pairs)
    return values


def fill_bias(bias_ref, query_labels, key_labels, tile, tile_count, history):
    for t in range(tile_count):
        span = SPAN + tile
        key_pos = lax.broadcasted_iota(jnp.int32, (span, tile), 0) + (history - SPAN + t * tile)
        query_pos = lax.broadcasted_iota(jnp.int32, (span, tile), 1) + (history + t * tile)
        same = key_labels[pl.ds(history - SPAN + t * tile, span), :] == query_labels[:, pl.ds(t * tile, tile)]
        bias_ref[t] = jnp.where(same & (key_pos <= query_pos), 0.0, MASKED)


def head_rows(values, head):
    row = lax.broadcasted_iota(jnp.int32, values.shape, 0)
    return jnp.where((row >= head * HD) & (row < (head + 1) * HD), values, jnp.zeros_like(values))


def head_lanes(values, head):
    lane = lax.broadcasted_iota(jnp.int32, values.shape, 1)
    return jnp.where((lane >= head * HD) & (lane < (head + 1) * HD), values, jnp.zeros_like(values))


def attend_kernel(
    tile, history, query_labels, key_labels, q_ref, k_ref, v_ref, o_ref, lse_ref, bias_ref, vt_ref
):
    tile_count = q_ref.shape[0] // tile
    span = SPAN + tile

    @pl.when(pl.program_id(0) == 0)
    def _():
        fill_bias(bias_ref, query_labels, key_labels, tile, tile_count, history)

    vt_ref[...] = v_ref[...].T
    for t in range(tile_count):
        base = history - SPAN + t * tile
        queries = (q_ref[pl.ds(t * tile, tile), :] * HD ** (-0.5)).astype(BF16).T
        keys = k_ref[pl.ds(base, span), :]
        outputs = []
        for head in range(2):
            scores = (
                jnp.dot(keys, head_rows(queries, head), preferred_element_type=F32) + bias_ref[t]
            )
            maximum = jnp.max(scores, axis=0, keepdims=True)
            powers = jnp.exp(scores - maximum)
            total = jnp.sum(powers, axis=0, keepdims=True)
            attention = (powers * (1.0 / total)).astype(BF16)
            outputs.append(
                jnp.dot(
                    vt_ref[pl.ds(head * HD, HD), pl.ds(base, span)],
                    attention,
                    preferred_element_type=F32,
                )
            )
            lse_ref[0, pl.ds(head, 1), pl.ds(t * tile, tile)] = maximum + jnp.log(total)
        o_ref[pl.ds(t * tile, tile), :] = jnp.concatenate(outputs, axis=0).T.astype(BF16)


def attend_back_kernel(
    tile, history, query_labels, key_labels, q_ref, k_ref, v_ref, o_ref, do_ref, lse_ref,
    dq_ref, dk_ref, dv_ref, bias_ref, kt_ref, dk_acc, dv_acc,
):
    tile_count = q_ref.shape[0] // tile
    span = SPAN + tile

    @pl.when(pl.program_id(0) == 0)
    def _():
        fill_bias(bias_ref, query_labels, key_labels, tile, tile_count, history)

    kt_ref[...] = k_ref[...].T
    dk_acc[...] = jnp.zeros_like(dk_acc)
    dv_acc[...] = jnp.zeros_like(dv_acc)
    for t in range(tile_count):
        base = history - SPAN + t * tile
        scaled = (q_ref[pl.ds(t * tile, tile), :] * HD ** (-0.5)).astype(BF16)
        grads = do_ref[pl.ds(t * tile, tile), :]
        scaled_t, grads_t = scaled.T, grads.T
        product_t = grads_t.astype(F32) * o_ref[pl.ds(t * tile, tile), :].T.astype(F32)
        keys = k_ref[pl.ds(base, span), :]
        values = v_ref[pl.ds(base, span), :]
        grad_queries = []
        for head in range(2):
            scores = (
                jnp.dot(keys, head_rows(scaled_t, head), preferred_element_type=F32) + bias_ref[t]
            )
            attention = jnp.exp(scores - lse_ref[0, pl.ds(head, 1), pl.ds(t * tile, tile)])
            row_terms = jnp.sum(product_t[head * HD : (head + 1) * HD], axis=0, keepdims=True)
            grad_attention = jnp.dot(values, head_rows(grads_t, head), preferred_element_type=F32)
            grad_scores = (attention * (grad_attention - row_terms)).astype(BF16)
            dv_acc[pl.ds(base, span), :] += jnp.dot(
                attention.astype(BF16), head_lanes(grads, head), preferred_element_type=F32
            )
            dk_acc[pl.ds(base, span), :] += jnp.dot(
                grad_scores, head_lanes(scaled, head), preferred_element_type=F32
            )
            grad_queries.append(
                jnp.dot(
                    kt_ref[pl.ds(head * HD, HD), pl.ds(base, span)],
                    grad_scores,
                    preferred_element_type=F32,
                )
            )
        dq_ref[pl.ds(t * tile, tile), :] = (
            jnp.concatenate(grad_queries, axis=0).T * HD ** (-0.5)
        ).astype(BF16)
    dk_ref[...] = dk_acc[...].astype(BF16)
    dv_ref[...] = dv_acc[...].astype(BF16)


def attention_specs(count, window, start):
    whole = lambda shape: pl.BlockSpec(shape, lambda h: (0,) * len(shape))
    specs = []
    for first in (start, 0):
        own = pl.BlockSpec((count, PAIR), lambda h, first=first: (0, first + h))
        seen = pl.BlockSpec((window, PAIR), lambda h, first=first: (0, first + h))
        specs.append((own, seen))
    sums = pl.BlockSpec((1, 2, count), lambda h: (h, 0, 0))
    labels = [whole((1, count)), whole((window, 1))]
    return labels, specs[0], specs[1], sums


def attend(inputs, tile, start, pairs):
    _, _, queries, keys, _ = inputs
    count, window = queries.shape[0], keys.shape[0]
    labels, (own, seen), (own_out, _), sums = attention_specs(count, window, start)
    work = 2 * count * (SPAN + tile) * PAIR * pairs
    return pl.pallas_call(
        functools.partial(attend_kernel, tile, window - count),
        grid=(pairs,),
        in_specs=labels + [own, seen, seen],
        out_specs=[own_out, sums],
        out_shape=[
            jax.ShapeDtypeStruct((count, pairs * PAIR), BF16),
            jax.ShapeDtypeStruct((pairs, 2, count), F32),
        ],
        scratch_shapes=[
            pltpu.VMEM((count // tile, SPAN + tile, tile), F32),
            pltpu.VMEM((PAIR, window), BF16),
        ],
        cost_estimate=pl.CostEstimate(
            flops=4 * work, bytes_accessed=4 * (window + count) * PAIR * pairs, transcendentals=0
        ),
        name="attend",
    )(*inputs)


def attend_back(inputs, context, grads, log_sums, tile, start, pairs):
    _, _, queries, keys, _ = inputs
    count, window = queries.shape[0], keys.shape[0]
    labels, (own, seen), (own_out, seen_out), sums = attention_specs(count, window, start)
    work = 2 * count * (SPAN + tile) * PAIR * pairs
    return pl.pallas_call(
        functools.partial(attend_back_kernel, tile, window - count),
        grid=(pairs,),
        in_specs=labels + [own, seen, seen, own_out, own, sums],
        out_specs=[own_out, seen_out, seen_out],
        out_shape=[
            jax.ShapeDtypeStruct((count, pairs * PAIR), BF16),
            jax.ShapeDtypeStruct((window, pairs * PAIR), BF16),
            jax.ShapeDtypeStruct((window, pairs * PAIR), BF16),
        ],
        scratch_shapes=[
            pltpu.VMEM((count // tile, SPAN + tile, tile), F32),
            pltpu.VMEM((PAIR, window), BF16),
            pltpu.VMEM((window, PAIR), F32),
            pltpu.VMEM((window, PAIR), F32),
        ],
        cost_estimate=pl.CostEstimate(
            flops=10 * work, bytes_accessed=8 * (window + count) * PAIR * pairs, transcendentals=0
        ),
        name="attend_back",
    )(*inputs, context, grads, log_sums)


def project_back_kernel(first_own, *refs):
    queries, keys, values = refs[0:2], refs[2:4], refs[4:6]
    weights, normed, back_ref, gain_ref = refs[6:]
    half = queries[0].shape[1]
    tile = pl.program_id(0)
    back = None
    for member, parts in ((1, keys), (2, values)):
        for i, part in enumerate(parts):
            term = mxu(part[...], weights[member, pl.ds(i * half, half), :])
            back = term if back is None else back + term
    back_ref[...] = back

    @pl.when(tile >= first_own)
    def _():
        back_ref[...] += mxu(queries[0][...], weights[0, pl.ds(0, half), :]) + mxu(
            queries[1][...], weights[0, pl.ds(half, half), :]
        )

    @pl.when(tile == 0)
    def _():
        gain_ref[...] = jnp.zeros_like(gain_ref)

    gain_ref[...] += jnp.sum(back_ref[...] * normed[...].astype(F32), axis=0, keepdims=True)


def project_back(first, second, weights, window):
    count, half = first[0].shape
    rows = window.shape[0]
    tile = min(256, count)
    first_own = (rows - count) // tile
    own = pl.BlockSpec((tile, half), lambda i: (jnp.maximum(i - first_own, 0), 0))
    seen = pl.BlockSpec((tile, half), lambda i: (i, 0))
    wide = pl.BlockSpec((tile, D), lambda i: (i, 0))
    return pl.pallas_call(
        functools.partial(project_back_kernel, first_own),
        grid=(rows // tile,),
        in_specs=[own, own, seen, seen, seen, seen, pl.BlockSpec((3, D, D), lambda i: (0, 0, 0)), wide],
        out_specs=[wide, pl.BlockSpec((1, D), lambda i: (0, 0))],
        out_shape=[jax.ShapeDtypeStruct((rows, D), F32), jax.ShapeDtypeStruct((1, D), F32)],
        cost_estimate=pl.CostEstimate(
            flops=2 * D * D * (2 * rows + count), bytes_accessed=12 * rows * D, transcendentals=0
        ),
        name="project_back",
    )(first[0], second[0], first[1], second[1], first[2], second[2], weights, window)


def split(values):
    high = values.astype(BF16)
    return high, (values - high.astype(F32)).astype(BF16)


def dot_split(first, second, contract):
    dims = ((contract, contract), ((), ()))
    (a, b), (c, d) = split(first), split(second)
    multiply = lambda x, y: lax.dot_general(x, y, dims, preferred_element_type=F32)
    return multiply(a, c) + multiply(b, c) + multiply(a, d)


def total_of(values):
    return jnp.sum(jnp.sum(values, axis=0, keepdims=True), axis=1, keepdims=True)


def mxu(first, second):
    return jnp.dot(first, second, preferred_element_type=F32)


class Chain:
    def __init__(self, matrix, rows, spread):
        self.matrix, self.rows, self.spread = matrix, rows, spread

    def square(self):
        self.low = self.matrix.astype(BF16)
        height = self.rows.shape[0]
        stacked = jnp.concatenate([self.rows.astype(BF16), self.low], axis=0)
        both = mxu(stacked, self.spread(self.low))
        self.rows = 1.25 * self.rows - 0.25 * both[:height]
        self.rest = (0.0625 * both[height:] - 0.625 * self.low.astype(F32)).astype(BF16)

    def half(self):
        self.right = self.spread(self.rest)
        self.matrix = 1.5625 * self.matrix + mxu(self.low, self.right)

    def whole(self):
        self.matrix = 1.5625 * self.matrix + mxu(self.matrix.astype(BF16), self.right)

    def last(self):
        self.rows = 1.25 * self.rows - 0.25 * mxu(
            self.rows.astype(BF16), self.spread(self.matrix.astype(BF16))
        )


def run_chains(chains):
    for _ in range(ROOTS - 1):
        for chain in chains:
            chain.square()
        for chain in chains:
            chain.half()
        for chain in chains:
            chain.whole()
    for chain in chains:
        chain.last()


def quarter(norm):
    return lax.rsqrt(jnp.sqrt(norm))


def shampoo_kernel(
    step_size, pack, grad_ref, master_ref, short_ref, long_ref, weight_ref, short_out, long_out
):
    blocks, short, width = grad_ref.shape
    side = pack * short
    row = lax.broadcasted_iota(jnp.int32, (side, side), 0)
    lane = lax.broadcasted_iota(jnp.int32, (side, side), 1)
    mask = jnp.where(lax.div(row, short) == lax.div(lane, short), 1.0, 0.0).astype(BF16)
    eye = jnp.where(
        lax.broadcasted_iota(jnp.int32, (short, side), 0)
        == lax.rem(lax.broadcasted_iota(jnp.int32, (short, side), 1), short),
        1.0,
        0.0,
    )
    spread = lambda values: jnp.concatenate([values] * pack, axis=0) * mask
    beside = lambda values: jnp.concatenate(values, axis=1)
    alone = lambda values: values
    packed_long = width == short

    shorts, longs, rows, scales = [], [], [], []
    for b in range(blocks):
        grad = grad_ref[b]
        short_new = 0.5 * short_ref[b] + 0.5 * dot_split(grad, grad, (1,))
        grad_t = grad.T
        long_new = 0.5 * long_ref[b] + 0.5 * dot_split(grad_t, grad_t, (1,))
        short_out[b] = short_new
        long_out[b] = long_new
        short_norm = jnp.sqrt(total_of(short_new * short_new) + 1e-06)
        long_norm = jnp.sqrt(total_of(long_new * long_new) + 1e-06)
        shorts.append(short_new / short_norm)
        longs.append(long_new / long_norm)
        rows.append(grad)
        scales.append(step_size * quarter(short_norm) * quarter(long_norm))
    groups = [range(i, i + pack) for i in range(0, blocks, pack)]
    left = [Chain(beside([shorts[b] for b in g]), eye, spread) for g in groups]
    if packed_long:
        right = [
            Chain(beside([longs[b] for b in g]), beside([rows[b] for b in g]), spread) for g in groups
        ]
    else:
        right = [Chain(longs[b], rows[b], alone) for b in range(blocks)]
    run_chains(left + right)
    for i, g in enumerate(groups):
        high, low = split(left[i].rows)
        if packed_long:
            second, second_low = split(right[i].rows)
            second, second_low = spread(second), spread(second_low)
            steps = mxu(high, second) + mxu(low, second) + mxu(high, second_low)
            steps = [steps[:, j * short : (j + 1) * short] for j in range(pack)]
        else:
            second, second_low = split(jnp.concatenate([right[b].rows for b in g], axis=0))
            high, low = spread(high), spread(low)
            steps = mxu(high, second) + mxu(low, second) + mxu(high, second_low)
            steps = [steps[j * short : (j + 1) * short] for j in range(pack)]
        for b, step in zip(g, steps):
            weight_ref[b] = master_ref[b] - scales[b] * step


def shampoo(gradient, master, short_old, long_old, step_size, blocks):
    count, short, width = gradient.shape
    blocks = min(blocks, count)
    pack = min(4, blocks)
    spec = lambda *shape: pl.BlockSpec((blocks,) + shape, lambda i: (i, 0, 0))
    specs = [spec(short, width), spec(short, short), spec(width, width)]
    shape = lambda *dims: jax.ShapeDtypeStruct((count,) + dims, F32)
    return pl.pallas_call(
        functools.partial(shampoo_kernel, step_size, pack),
        grid=(count // blocks,),
        in_specs=specs[:1] + specs,
        out_specs=specs,
        out_shape=[shape(short, width), shape(short, short), shape(width, width)],
        cost_estimate=pl.CostEstimate(
            flops=40 * count * width * width * width,
            bytes_accessed=8 * count * (width * width + short * short + 2 * short * width),
            transcendentals=0,
        ),
        name="shampoo",
    )(gradient, master, short_old, long_old)
def step_rows(gradient, master, left, right, step_size, blocks):
    flat = lambda values: values.reshape((-1,) + values.shape[-2:])
    outs = shampoo(flat(gradient), flat(master), flat(left), flat(right), step_size, blocks)
    return tuple(v.reshape(gradient.shape[:-2] + v.shape[-2:]) for v in outs)


def step_columns(gradient, master, left, right, step_size, blocks):
    turn = lambda values: jnp.swapaxes(values, -1, -2)
    weight, right, left = shampoo(turn(gradient), turn(master), right, left, step_size, blocks)
    return turn(weight), left, right


def two_by_two(first, second):
    (a, b), (c, d) = first
    (e, f), (g, h) = second
    return ((a * e + b * g, a * f + b * h), (c * e + d * g, c * f + d * h))


def quarter_root_pair(statistic):
    entries = tuple(tuple(statistic[i, j] for j in range(2)) for i in range(2))
    frobenius = jnp.sqrt(sum(v * v for row in entries for v in row) + 1e-06)
    matrix = tuple(tuple(v / frobenius for v in row) for row in entries)
    estimate = ((1.0, 0.0), (0.0, 1.0))
    for iteration in range(ROOTS):
        (a, b), (c, d) = matrix
        update = (((5.0 - a) * 0.25, -b * 0.25), (-c * 0.25, (5.0 - d) * 0.25))
        estimate = two_by_two(estimate, update)
        squared = two_by_two(update, update)
        matrix = two_by_two(two_by_two(squared, squared), matrix)
    scale = lax.rsqrt(jnp.sqrt(frobenius))
    return tuple(tuple(v * scale for v in row) for row in estimate)


def gain_update(gradient, gain_rows, left_old, right_old):
    outer = jnp.sum(gradient[:, None, :] * gradient[None, :, :], axis=2)
    left_new = 0.5 * left_old + 0.5 * outer
    right_new = 0.5 * right_old + 0.5 * jnp.sum(gradient * gradient, axis=0)
    (a, b), (c, d) = quarter_root_pair(left_new)
    first, second = gradient[0], gradient[1]
    mixed = jnp.stack([a * first + b * second, c * first + d * second])
    direction = mixed * lax.rsqrt(jnp.sqrt(right_new))
    return (gain_rows - GAIN_RATE * direction, left_new, right_new)


def dot(first, second):
    return jnp.dot(first, second, preferred_element_type=F32)


def dot_back(first, second):
    return lax.dot_general(first, second, (((1,), (1,)), ((), ())), preferred_element_type=F32)


def dot_weight(first, second):
    return lax.dot_general(first, second, (((0,), (0,)), ((), ())), preferred_element_type=F32)


def body(
    patches,
    cotangent,
    lengths,
    hashes,
    segments,
    attend_master,
    output_master,
    expand_master,
    reduce_master,
    gains,
    attend_left,
    attend_right,
    output_left,
    output_right,
    expand_left,
    expand_right,
    reduce_left,
    reduce_right,
    gains_left,
    gains_right,
):
    dp_size, mp_size = lax.axis_size("dp"), lax.axis_size("mp")
    mp_index = lax.axis_index("mp")
    count = patches.shape[0]
    head_width, hidden_width = D // mp_size, FF // mp_size
    head_rows_width = head_width // CHIPS
    total_patches = count * dp_size * mp_size
    earlier = -(-(SPAN - 1) // count)
    history = earlier * count
    tile = min(256, count)
    fast = dp_size == 2 * CHIPS and mp_size == 4
    device = coordinate(fast)
    grids = {
        name: piece_shape(master.shape, rows, dp_size)
        for name, master, rows in (
            ("attend", attend_master, D),
            ("output", output_master, head_width),
            ("expand", expand_master, D),
            ("reduce", reduce_master, hidden_width),
        )
    }

    stream = patches.astype(F32)
    first_rms = lax.rsqrt(jnp.mean(stream * stream, axis=1, keepdims=True) + EPSILON)
    first_hat = stream * first_rms
    first_normed = (first_hat * gains[0]).astype(BF16)

    row_labels = segments.reshape(-1)
    padded = jnp.concatenate([jnp.full((history,), -1, jnp.int32), row_labels])
    key_labels = lax.dynamic_slice_in_dim(padded, mp_index * count, history + count, 0)
    query_labels = key_labels[history:].reshape(1, count)
    key_labels = key_labels.reshape(-1, 1)
    up_one = [(i, i + 1) for i in range(mp_size - 1)]
    down_one = [(i + 1, i) for i in range(mp_size - 1)]
    half_pairs = HEADS * HD // PAIR // 2

    def count_own(all_hashes):
        own = hashes.astype(F32)
        return jnp.sum((own[:, None] == all_hashes[None, :]).astype(F32), axis=1)

    def halo(values):
        return lax.ppermute(values, "mp", up_one)

    if fast:
        attend_rows = jnp.concatenate(
            [
                rows_of_columns(to_piece(attend_master.astype(BF16), *grids["attend"][:2])),
                rows_of_rows(to_piece(output_master.astype(BF16), *grids["output"][:2])),
                hash_rows(hashes),
            ]
        )
        slice_two = pairwise(attend_rows, "mp", 2)
        slice_one = pairwise(attend_rows, "mp", 1)
        halo_source, slice_two = together(first_normed, slice_two)
        slice_three = pairwise(slice_two, "mp", 1)
        near_halo = halo(halo_source)
        attend_slices = jnp.stack([attend_rows, slice_one, slice_two, slice_three])
        sides = gather_sides(attend_slices)
        near_halo, sides = together(near_halo, sides)
        corners = gather_corner(*sides)
        shards = [near_halo, first_normed]
        for _ in range(earlier - 1):
            shards.insert(0, halo(shards[0]))
        shards[0], corners = together(shards[0], corners)
        attend_pieces = gather_end(attend_slices, *sides, *corners)
        window = jnp.concatenate(shards, axis=0)
        all_hashes = jnp.concatenate(
            [rows_hash(piece[:, 4 * head_width :], count) for piece in attend_pieces]
        )
    else:
        attend_cut = jnp.concatenate(
            [
                cut_columns(weight_by_columns(attend_master, dp_size), mp_size),
                cut_rows(weight_by_rows(output_master, head_width, dp_size), mp_size),
            ],
            axis=3,
        )
        attend_pieces = [attend_cut[chip, core] for core in range(2) for chip in range(CHIPS)]
        hidden_cut = jnp.concatenate(
            [
                cut_columns(weight_by_columns(expand_master, dp_size), mp_size),
                cut_rows(weight_by_rows(reduce_master, hidden_width, dp_size), mp_size),
            ],
            axis=3,
        )
        near_pieces, far_pieces = (
            [hidden_cut[chip, core, k : k + 2] for core in range(2) for chip in range(CHIPS)]
            for k in (0, 2)
        )
        shards = [first_normed]
        for _ in range(earlier):
            shards.insert(0, halo(shards[0]))
        window = jnp.concatenate(shards, axis=0)
        all_hashes = gather_small(hashes).astype(F32)

    raw_weight = lengths.astype(F32) * lax.rsqrt(count_own(all_hashes))
    raw_total = jnp.sum(raw_weight).reshape(1, 1)
    steps = list(exchanges())
    grad_out = cotangent.astype(F32) * raw_weight[:, None]
    grad_low = grad_out.astype(BF16)

    if fast:
        hidden_rows = jnp.concatenate(
            [
                rows_of_columns(to_piece(expand_master.astype(BF16), *grids["expand"][:2])),
                rows_of_rows(to_piece(reduce_master.astype(BF16), *grids["reduce"][:2])),
            ]
        )
        window, hidden_rows = together(window, hidden_rows)
        slice_one = pairwise(hidden_rows, "mp", 1)
        slice_two = pairwise(hidden_rows, "mp", 2)
    attend_w, output_w = join_attend(device, attend_pieces)
    queries = dot_back(first_normed, attend_w[0]).astype(BF16)
    keys = dot_back(window, attend_w[1]).astype(BF16)
    values = dot_back(window, attend_w[2]).astype(BF16)
    labels = (query_labels, key_labels)
    if fast:
        queries, slice_one = together(queries, slice_one)
        near = jnp.stack([hidden_rows, slice_one])
        sides = gather_sides(near)
    inputs = labels + (queries, keys, values)
    context_a, sums_a = attend(inputs, tile, 0, half_pairs)
    if fast:
        queries, context_a, sides, slice_two = together(queries, context_a, sides, slice_two)
        inputs = labels + (queries, keys, values)
        corners = gather_corner(*sides)
        slice_three = pairwise(slice_two, "mp", 1)
        moved = lax.ppermute(raw_total, *steps[0])
    context_b, sums_b = attend(inputs, tile, half_pairs, half_pairs)
    if fast:
        context_b, corners, slice_three, moved = together(context_b, corners, slice_three, moved)
        raw_total = raw_total + moved
        moved = lax.ppermute(raw_total, *steps[1])
        near_pieces = gather_end(near, *sides, *corners)
        far = jnp.stack([slice_two, slice_three])
        sides = gather_sides(far)
    half = context_a.shape[1]
    middle = stream + dot(context_a, output_w[:half]) + dot(context_b, output_w[half:])

    second_rms = lax.rsqrt(jnp.mean(middle * middle, axis=1, keepdims=True) + EPSILON)
    second_hat = middle * second_rms
    second_normed = (second_hat * gains[1]).astype(BF16)
    if fast:
        second_normed, near_pieces, moved = together(second_normed, near_pieces, moved)
        raw_total = raw_total + moved
        moved = lax.ppermute(raw_total, *steps[2])
        share_a = hidden_layer(device, second_normed, grad_low, near_pieces, hidden_width, 0, 1)
        share_a, sides, moved = together(share_a, sides, moved)
        raw_total = raw_total + moved
        moved = lax.ppermute(raw_total, *steps[3])
        corners = gather_corner(*sides)
        share_b = hidden_layer(
            device, second_normed, grad_low, near_pieces, hidden_width, 1, 1, share_a[2:]
        )
        share_b, corners, moved = together(share_b, corners, moved)
        raw_total = raw_total + moved
        moved = lax.ppermute(raw_total, *steps[4])
        far_pieces = gather_end(far, *sides, *corners)
        near_grads = share_b[2:]
        near_received = pairwise(near_grads[1], "dp", 1)
        share_c = hidden_layer(device, second_normed, grad_low, far_pieces, hidden_width, 0, 2)
        share_c, near_received, moved = together(share_c, near_received, moved)
        raw_total = raw_total + moved
        far_grads = share_c[2:]
        far_received = pairwise(far_grads[1], "dp", 1)
        near_corners = reduce_chips_corner(near_grads[0], near_received)
        second_back = share_a[1] + share_b[1] + share_c[1]
        activations = (middle + share_a[0] + share_b[0] + share_c[0]).astype(BF16)
    else:
        share_a = hidden_layer(device, second_normed, grad_low, near_pieces, hidden_width, 0, 2)
        share_c = hidden_layer(device, second_normed, grad_low, far_pieces, hidden_width, 0, 2)
        near_grads, far_grads = share_a[2:], share_c[2:]
        raw_total = sum_small(raw_total)
        second_back = share_a[1] + share_c[1]
        activations = (middle + share_a[0] + share_c[0]).astype(BF16)

    weight_scale = total_patches / raw_total[0, 0]

    second_scaled = second_back * gains[1]
    gain_second = jnp.sum(second_back * second_hat, axis=0)
    middle_grad = grad_out + second_rms * (
        second_scaled - second_hat * jnp.mean(second_scaled * second_hat, axis=1, keepdims=True)
    )
    middle_low = middle_grad.astype(BF16)
    grad_context = dot_back(middle_low, output_w).astype(BF16)

    def weight_grads(context_part, parts):
        grad_queries, grad_keys, grad_values = parts
        return [
            dot_weight(grad_queries, first_normed).astype(BF16),
            dot_weight(grad_keys, window).astype(BF16),
            dot_weight(grad_values, window).astype(BF16),
            dot_weight(context_part, middle_low).astype(BF16),
        ]

    slices_half = mp_size // 2
    if fast:
        grad_context, near_corners, far_received = together(grad_context, near_corners, far_received)
        near_sides = reduce_chips_sides(near_grads[0], near_received, *near_corners)
        far_corners = reduce_chips_corner(far_grads[0], far_received)
    backs_a = attend_back(inputs, context_a, grad_context, sums_a, tile, 0, half_pairs)
    cut_a = cut_attend(device, weight_grads(context_a, backs_a), slices_half)
    if fast:
        received_a = pairwise(cut_a[1], "dp", 1)
        grad_context, cut_a, near_sides, far_corners = together(
            grad_context, cut_a, near_sides, far_corners
        )
        near_own = reduce_chips_own(near_grads[0], near_received, *near_sides)
        near_one = pairwise(near_own[1].astype(BF16), "mp", 1)
        far_sides = reduce_chips_sides(far_grads[0], far_received, *far_corners)
    backs_b = attend_back(inputs, context_b, grad_context, sums_b, tile, half_pairs, half_pairs)
    if fast:
        backs_b, far_sides, received_a = together(backs_b, far_sides, received_a)
        far_own = reduce_chips_own(far_grads[0], far_received, *far_sides)
        far_three = pairwise(far_own[1].astype(BF16), "mp", 1)
        corners_a = reduce_chips_corner(cut_a[0], received_a)
    cut_b = cut_attend(device, weight_grads(context_b, backs_b), slices_half)
    if fast:
        received_b = pairwise(cut_b[1], "dp", 1)
        backs_b, cut_b, corners_a, far_three, near_one = together(
            backs_b, cut_b, corners_a, far_three, near_one
        )
        far_two = pairwise((far_own[0] + far_three.astype(F32)).astype(BF16), "mp", 2)
        sides_a = reduce_chips_sides(cut_a[0], received_a, *corners_a)
    window_back, gain_first = project_back(backs_a, backs_b, attend_w, window)
    gain_sums = jnp.stack([gain_first[0] / gains[0], gain_second])

    def halo_back(share):
        return lax.ppermute(share.astype(BF16), "mp", down_one)

    shares = [window_back[k * count : (k + 1) * count] for k in range(earlier)]
    if fast:
        window_back, received_b, sides_a = together(window_back, received_b, sides_a)
        shares = [window_back[k * count : (k + 1) * count] for k in range(earlier)]
        carried = halo_back(shares[0])
        corners_b = reduce_chips_corner(cut_b[0], received_b)
        own_a = reduce_chips_own(cut_a[0], received_a, *sides_a)
        one_a = pairwise(own_a[1].astype(BF16), "mp", 1)
        moved = lax.ppermute(gain_sums, *steps[0])
    else:
        carried = halo_back(shares[0])
        for share in shares[1:]:
            carried = halo_back(share + carried.astype(F32))
        gain_sums = sum_small(gain_sums)
    grad_scale = weight_scale * total_patches ** (-0.5)
    reduce_step, expand_step = STEP_RATE * FF ** (-0.5), STEP_RATE * D ** (-0.5)
    if fast:
        hidden_sum = near_own[0] + near_one.astype(F32) + far_two.astype(F32)
        hidden_sum = hidden_sum * grad_scale
        expand_grad = from_piece(
            columns_of_rows(hidden_sum[: 2 * hidden_width], 2), *grids["expand"][:2]
        )
        reduce_grad = from_piece(
            rows_to_rows(hidden_sum[2 * hidden_width : 3 * hidden_width], D // (2 * LANES)),
            *grids["reduce"][:2]
        )
        reduce_grad, expand_grad, corners_b, moved = together(
            reduce_grad, expand_grad, corners_b, moved
        )
        gain_sums = gain_sums + moved
        moved = lax.ppermute(gain_sums, *steps[1])
        sides_b = reduce_chips_sides(cut_b[0], received_b, *corners_b)
        reduce_out = step_columns(reduce_grad, reduce_master, reduce_left, reduce_right, reduce_step, 4)
        reduce_out, expand_grad, sides_b, carried, one_a, moved = together(
            reduce_out, expand_grad, sides_b, carried, one_a, moved
        )
        gain_sums = gain_sums + moved
        moved = lax.ppermute(gain_sums, *steps[2])
        own_b = reduce_chips_own(cut_b[0], received_b, *sides_b)
        three_b = pairwise(own_b[1].astype(BF16), "mp", 1)
        for share in shares[1:]:
            carried = halo_back(share + carried.astype(F32))
        expand_out = step_rows(expand_grad, expand_master, expand_left, expand_right, expand_step, 8)
        expand_out, three_b, moved = together(expand_out, three_b, moved)
        gain_sums = gain_sums + moved
        moved = lax.ppermute(gain_sums, *steps[3])
        two_b = pairwise((own_b[0] + three_b.astype(F32)).astype(BF16), "mp", 2)
        attend_sum = (own_a[0] + one_a.astype(F32) + two_b.astype(F32)) * grad_scale
        attend_sum, carried, moved = together(attend_sum, carried, moved)
        gain_sums = gain_sums + moved
        gain_sums = gain_sums + lax.ppermute(gain_sums, *steps[4])
        output_grad = from_piece(
            rows_to_rows(attend_sum[3 * head_width :], D // (2 * LANES)), *grids["output"][:2]
        )
        attend_grad = from_piece(columns_of_rows(attend_sum[: 3 * head_width], 3), *grids["attend"][:2])
    else:
        hidden_cut = jnp.stack(
            [jnp.concatenate([near_grads[core], far_grads[core]], axis=1) for core in range(2)], axis=1
        )
        attend_cut = jnp.stack(
            [jnp.concatenate([cut_a[core], cut_b[core]], axis=1) for core in range(2)], axis=1
        )
        expand_grad = grad_scale * grad_by_columns(
            join_columns(hidden_cut[:, :, :, : 2 * hidden_width], 2), expand_master, dp_size, mp_size
        )
        reduce_grad = grad_scale * grad_by_rows(
            join_rows(hidden_cut[:, :, :, 2 * hidden_width :]),
            reduce_master,
            hidden_width,
            dp_size,
            mp_size,
        )
        output_grad = grad_scale * grad_by_rows(
            join_rows(attend_cut[:, :, :, 3 * head_width :]), output_master, head_width, dp_size, mp_size
        )
        attend_grad = grad_scale * grad_by_columns(
            join_columns(attend_cut[:, :, :, : 3 * head_width], 3), attend_master, dp_size, mp_size
        )
        reduce_out = step_columns(reduce_grad, reduce_master, reduce_left, reduce_right, reduce_step, 4)
        expand_out = step_rows(expand_grad, expand_master, expand_left, expand_right, expand_step, 8)
    first_back = window_back[history:] + carried.astype(F32)
    first_scaled = first_back * gains[0]
    input_grad = weight_scale * (
        middle_grad
        + first_rms
        * (first_scaled - first_hat * jnp.mean(first_scaled * first_hat, axis=1, keepdims=True))
    )

    reduce_weight, left_reduce, right_reduce = reduce_out
    expand_weight, left_expand, right_expand = expand_out
    gains_grad = gain_sums * grad_scale
    output_weight, left_output, right_output = step_rows(
        output_grad, output_master, output_left, output_right, STEP_RATE * OUT_FAN ** (-0.5), 8
    )
    attend_weight, left_attend, right_attend = step_rows(
        attend_grad, attend_master, attend_left, attend_right, STEP_RATE * D ** (-0.5), 8
    )
    gains_weight, left_gains, right_gains = gain_update(gains_grad, gains, gains_left, gains_right)
    return (
        activations,
        input_grad,
        attend_grad,
        attend_weight,
        left_attend,
        right_attend,
        output_grad,
        output_weight,
        left_output,
        right_output,
        expand_grad,
        expand_weight,
        left_expand,
        right_expand,
        reduce_grad,
        reduce_weight,
        left_reduce,
        right_reduce,
        gains_grad,
        gains_weight,
        left_gains,
        right_gains,
    )


def solution(mesh):
    rows = P(("dp", "mp"), None)
    single = P(("dp", "mp"), None, None)
    stacked = P(None, ("dp", "mp"), None, None)
    return jax.shard_map(
        body,
        mesh=mesh,
        in_specs=(
            rows,
            rows,
            P(("dp", "mp")),
            P(("dp", "mp")),
            P("dp", None),
            stacked,
            single,
            stacked,
            single,
            P(),
            stacked,
            stacked,
            single,
            single,
            stacked,
            stacked,
            single,
            single,
            P(),
            P(),
        ),
        out_specs=(
            rows,
            rows,
            stacked,
            stacked,
            stacked,
            stacked,
            single,
            single,
            single,
            single,
            stacked,
            stacked,
            stacked,
            stacked,
            single,
            single,
            single,
            single,
            P(),
            P(),
            P(),
            P(),
        ),
        check_vma=False,
    )
```

```python
import functools
import math

import jax
import jax.numpy as jnp
from jax import lax
from jax.experimental import pallas as pl
from jax.experimental.pallas import tpu as pltpu
from jax.sharding import PartitionSpec as P

D = 1024
HEADS = 16
HD = 64
FF = 2816
BLK = 64
FBLK = 176
ROOTS = 6
OUT_FAN = 8
SPAN = 1024

EPSILON = 1e-05
STEP_RATE = 16.0
GAIN_RATE = 2.0
MASKED = -1e30
F32 = jnp.float32
BF16 = jnp.bfloat16
PAIR = 2 * HD


CHIPS = 4
LANES = 128


def piece_shape(blocked_shape, group_rows, dp_size):
    per_owner, height, width = blocked_shape[-3:]
    column_blocks = dp_size * per_owner // (group_rows // height)
    if per_owner % column_blocks == 0:
        rows, columns = per_owner // column_blocks, column_blocks
    else:
        rows, columns = 1, per_owner
    grid_columns = column_blocks // columns
    return rows, columns, dp_size // grid_columns, grid_columns


def to_piece(blocked, rows, columns):
    leading = blocked.shape[:-3]
    height, width = blocked.shape[-2:]
    grid = blocked.reshape(leading + (rows, columns, height, width))
    return jnp.swapaxes(grid, -3, -2).reshape(leading + (rows * height, columns * width))


def from_piece(piece, rows, columns):
    leading = piece.shape[:-2]
    height, width = piece.shape[-2] // rows, piece.shape[-1] // columns
    grid = piece.reshape(leading + (rows, height, columns, width))
    return jnp.swapaxes(grid, -3, -2).reshape(leading + (rows * columns, height, width))


def rows_of_columns(piece):
    return jnp.swapaxes(piece, -1, -2).reshape(-1, LANES)


def columns_of_rows(rows, members):
    return jnp.swapaxes(rows.reshape(members, -1, LANES), -1, -2)


def rows_of_rows(piece):
    height, width = piece.shape
    return jnp.swapaxes(piece.reshape(height, width // LANES, LANES), 0, 1).reshape(-1, LANES)


def rows_to_rows(rows, blocks):
    grid = jnp.swapaxes(rows.reshape(blocks, -1, LANES), 0, 1)
    return grid.reshape(grid.shape[0], blocks * LANES)


def together(*values):
    return lax.optimization_barrier(values)


def pairwise(values, axis, step):
    return lax.ppermute(values, axis, [(i, i ^ step) for i in range(lax.axis_size(axis))])


def gather_sides(slices):
    return pairwise(slices, "dp", 2), pairwise(slices, "dp", 4), pairwise(slices, "dp", 1)


def gather_corner(across_x, across_y, other):
    half = across_x.shape[0] // 2
    return (
        pairwise(across_y[:half], "dp", 2),
        pairwise(across_x[half:], "dp", 4),
        pairwise(jnp.concatenate([across_x, across_y]), "dp", 1),
    )


def gather_end(slices, across_x, across_y, other, corner_x, corner_y, other_sides):
    corner = jnp.concatenate([corner_x, corner_y])
    return (
        slices, across_x, across_y, corner, other, other_sides, other_sides, pairwise(corner, "dp", 1)
    )


def first_slices(pieces):
    return [0] * 6 + [pieces[6].shape[0] - pieces[0].shape[0], 0]


def add_up(*refs):
    total = refs[0][...].astype(F32)
    for ref in refs[1:]:
        total = total + ref[...].astype(F32)
    return total


def add_call(kernel, slices, in_specs, out_specs, out_shape, name, *operands):
    return pl.pallas_call(
        kernel,
        grid=(slices,),
        in_specs=in_specs,
        out_specs=out_specs,
        out_shape=out_shape,
        cost_estimate=moved(sum(v.size // CHIPS for v in operands)),
        name=name,
    )(*operands)


def chip_slice(chip, rows):
    return pl.BlockSpec((1, 1, rows, LANES), lambda k: (chip, k, 0, 0))


def one_slice(rows, first=0, last=None):
    if last is None:
        return pl.BlockSpec((1, rows, LANES), lambda k: (k, 0, 0))
    return pl.BlockSpec((1, rows, LANES), lambda k: (jnp.clip(k, first, last) - first, 0, 0))


def corner_kernel(half, own, received, to_x, to_y):
    total = add_up(own, received)[0].astype(BF16)

    @pl.when(pl.program_id(0) < half)
    def _():
        to_x[...] = total

    @pl.when(pl.program_id(0) >= half)
    def _():
        to_y[...] = total


def corner_sums(own_core, received):
    slices, rows = own_core.shape[1:3]
    half = slices // 2
    shape = jax.ShapeDtypeStruct((half, rows, LANES), BF16)
    to_x, to_y = add_call(
        functools.partial(corner_kernel, half),
        slices,
        [chip_slice(3, rows)] * 2,
        [one_slice(rows, 0, half - 1), one_slice(rows, half, slices - 1)],
        [shape, shape],
        "add_corner",
        own_core,
        received,
    )
    return to_x, to_y


def send_planar(to_x, to_y):
    return pairwise(to_x, "dp", 2), pairwise(to_y, "dp", 4)


def sides_kernel(half, own_x, received_x, own_y, received_y, corner_x, corner_y, to_x, to_y):
    @pl.when(pl.program_id(0) < half)
    def _():
        to_x[...] = add_up(own_x, received_x)[0].astype(BF16)
        to_y[...] = (add_up(own_y, received_y)[0] + corner_x[...].astype(F32)).astype(BF16)

    @pl.when(pl.program_id(0) >= half)
    def _():
        to_x[...] = (add_up(own_x, received_x)[0] + corner_y[...].astype(F32)).astype(BF16)
        to_y[...] = add_up(own_y, received_y)[0].astype(BF16)


def side_sums(own_core, received, corner_x, corner_y):
    slices, rows = own_core.shape[1:3]
    half = slices // 2
    shape = jax.ShapeDtypeStruct((slices, rows, LANES), BF16)
    to_x, to_y = add_call(
        functools.partial(sides_kernel, half),
        slices,
        [chip_slice(1, rows)] * 2
        + [chip_slice(2, rows)] * 2
        + [one_slice(rows, 0, half - 1), one_slice(rows, half, slices - 1)],
        [one_slice(rows)] * 2,
        [shape, shape],
        "add_sides",
        own_core,
        received,
        own_core,
        received,
        corner_x,
        corner_y,
    )
    return to_x, to_y


def own_kernel(own, received, from_x, from_y, kept, sent):
    total = add_up(own, received)[0] + add_up(from_x, from_y)

    @pl.when(pl.program_id(0) == 0)
    def _():
        kept[...] = total

    @pl.when(pl.program_id(0) == 1)
    def _():
        sent[...] = total.astype(BF16)


def own_sums(own_core, received, from_x, from_y):
    rows = own_core.shape[2]
    kept, sent = add_call(
        own_kernel,
        2,
        [chip_slice(0, rows)] * 2 + [one_slice(rows)] * 2,
        [one_slice(rows, 0, 0)] * 2,
        [jax.ShapeDtypeStruct((1, rows, LANES), F32), jax.ShapeDtypeStruct((1, rows, LANES), BF16)],
        "add_own",
        own_core,
        received,
        from_x,
        from_y,
    )
    return kept[0], sent[0]


def coordinate(fast):
    return lax.axis_index("dp").astype(jnp.int32).reshape(1) if fast else jnp.zeros((1,), jnp.int32)


def gather_all(piece):
    return lax.all_gather(lax.all_gather(piece, "mp"), "dp")


def scatter_all(parts):
    reduced = lax.psum_scatter(parts, "dp", scatter_dimension=0, tiled=False)
    return lax.psum_scatter(reduced, "mp", scatter_dimension=0, tiled=False)


def weight_by_columns(master, dp_size):
    rows, columns, grid_rows, grid_columns = piece_shape(master.shape, D, dp_size)
    gathered = gather_all(to_piece(master.astype(BF16), rows, columns))
    mp, members, height, width = gathered.shape[1:]
    grid = gathered.reshape(grid_rows, grid_columns, mp, members, height, width)
    grid = jnp.transpose(grid, (3, 0, 4, 2, 1, 5))
    return grid.reshape(members, grid_rows * height, mp * grid_columns * width)


def weight_by_rows(master, group_rows, dp_size):
    rows, columns, grid_rows, grid_columns = piece_shape(master.shape, group_rows, dp_size)
    gathered = gather_all(to_piece(master.astype(BF16), rows, columns))
    mp, height, width = gathered.shape[1:]
    grid = gathered.reshape(grid_rows, grid_columns, mp, height, width)
    grid = jnp.transpose(grid, (2, 0, 3, 1, 4))
    return grid.reshape(mp * grid_rows * height, grid_columns * width)


def grad_by_columns(matrix, master, dp_size, mp_size):
    rows, columns, grid_rows, grid_columns = piece_shape(master.shape, D, dp_size)
    members = matrix.shape[0]
    height, width = rows * master.shape[-2], columns * master.shape[-1]
    grid = matrix.reshape(members, grid_rows, height, mp_size, grid_columns, width)
    grid = jnp.transpose(grid, (1, 4, 3, 0, 2, 5))
    parts = grid.reshape(dp_size, mp_size, members, height, width)
    return from_piece(scatter_all(parts).astype(F32), rows, columns)


def grad_by_rows(matrix, master, group_rows, dp_size, mp_size):
    rows, columns, grid_rows, grid_columns = piece_shape(master.shape, group_rows, dp_size)
    height, width = rows * master.shape[-2], columns * master.shape[-1]
    grid = matrix.reshape(mp_size, grid_rows, height, grid_columns, width)
    grid = jnp.transpose(grid, (1, 3, 0, 2, 4))
    parts = grid.reshape(dp_size, mp_size, height, width)
    return from_piece(scatter_all(parts).astype(F32), rows, columns)


def cut_columns(matrices, mp_size):
    members, _, width = matrices.shape
    grid = matrices.reshape(members, CHIPS, 2, LANES, mp_size, width // mp_size)
    return jnp.transpose(grid, (1, 2, 4, 0, 5, 3)).reshape(CHIPS, 2, mp_size, -1, LANES)


def join_columns(pieces, members):
    grid = pieces.reshape(pieces.shape[:3] + (members, -1, LANES))
    return jnp.transpose(grid, (3, 0, 1, 5, 2, 4)).reshape(members, D, -1)


def cut_rows(matrix, mp_size):
    grid = matrix.reshape(mp_size, CHIPS, matrix.shape[0] // (mp_size * CHIPS), 2, D // (2 * LANES), LANES)
    return jnp.transpose(grid, (1, 3, 0, 4, 2, 5)).reshape(CHIPS, 2, mp_size, -1, LANES)


def join_rows(pieces):
    grid = pieces.reshape(pieces.shape[:3] + (D // (2 * LANES), -1, LANES))
    return jnp.transpose(grid, (2, 0, 4, 1, 3, 5)).reshape(-1, D)


def lanes_of(device, relative):
    return pl.ds(pl.multiple_of((device ^ relative) * LANES, LANES), LANES)


def half_lanes(device, core, block):
    start = ((device & 1) ^ core) * (D // 2) + block * LANES
    return pl.ds(pl.multiple_of(start, LANES), LANES)


def rows_at(device, chip, height):
    return pl.ds(pl.multiple_of(((device >> 1) ^ chip) * height, 16), height)


def project_kernel(shard_count, device_ref, *refs):
    shards, refs = refs[:shard_count], refs[shard_count:]
    attend_ref, output_ref, query_ref, key_ref, value_ref, window_ref = refs[2 * CHIPS :]
    device = device_ref[0]
    height = attend_ref.shape[1]
    count = query_ref.shape[0]
    for core in range(2):
        for chip in range(CHIPS):
            piece = refs[core * CHIPS + chip]
            lanes = lanes_of(device, 2 * chip + core)
            for member in range(3):
                attend_ref[member, :, lanes] = piece[0, pl.ds(member * height, height), :]
            rows = rows_at(device, chip, height // CHIPS)
            for block in range(D // (2 * LANES)):
                output_ref[rows, half_lanes(device, core, block)] = piece[
                    0, pl.ds(3 * height + block * (height // CHIPS), height // CHIPS), :
                ]
    columns = pl.ds(pl.multiple_of(pl.program_id(0) * height, LANES), height)
    query_ref[...] = dot_back(shards[-1][...], attend_ref[0]).astype(BF16)
    for i, shard in enumerate(shards):
        rows = pl.ds(i * count, count)
        key_ref[rows, :] = dot_back(shard[...], attend_ref[1]).astype(BF16)
        value_ref[rows, :] = dot_back(shard[...], attend_ref[2]).astype(BF16)
        window_ref[rows, :] = shard[:, columns]


def cut_attend_kernel(device_ref, query, key, value, output, first, second):
    device = device_ref[0]
    height = query.shape[0]
    for core, pieces in enumerate((first, second)):
        for chip in range(CHIPS):
            lanes = lanes_of(device, 2 * chip + core)
            for member, matrix in enumerate((query, key, value)):
                pieces[chip, 0, pl.ds(member * height, height), :] = matrix[:, lanes]
            rows = rows_at(device, chip, height // CHIPS)
            for block in range(D // (2 * LANES)):
                pieces[chip, 0, pl.ds(3 * height + block * (height // CHIPS), height // CHIPS), :] = (
                    output[rows, half_lanes(device, core, block)]
                )


def grid_call(
    kernel, grid, in_specs, out_specs, out_shape, name, scratch=(), cost=None, aliases=None
):
    return pl.pallas_call(
        kernel,
        grid_spec=pltpu.PrefetchScalarGridSpec(
            num_scalar_prefetch=1,
            grid=grid,
            in_specs=in_specs,
            out_specs=out_specs,
            scratch_shapes=scratch,
        ),
        out_shape=out_shape,
        input_output_aliases=aliases or {},
        cost_estimate=cost,
        name=name,
    )


def moved(count):
    return pl.CostEstimate(flops=0, bytes_accessed=2 * count, transcendentals=0)


def project(device, shards, pieces):
    slices = pieces[0].shape[0]
    height = D // slices
    count = shards[0].shape[0]
    rows = count * len(shards)
    piece = lambda first: pl.BlockSpec((1, 4 * height, LANES), lambda k, d: (first + k, 0, 0))
    columns = lambda rows: pl.BlockSpec((rows, height), lambda k, d: (0, k))
    wide = lambda rows: jax.ShapeDtypeStruct((rows, D), BF16)
    return grid_call(
        functools.partial(project_kernel, len(shards)),
        (slices,),
        [pl.BlockSpec((count, D), lambda k, d: (0, 0))] * len(shards)
        + [piece(first) for first in first_slices(pieces)],
        [
            pl.BlockSpec((3, height, D), lambda k, d: (0, k, 0)),
            pl.BlockSpec((height, D), lambda k, d: (k, 0)),
            columns(count),
            columns(rows),
            columns(rows),
            columns(rows),
        ],
        [jax.ShapeDtypeStruct((3, D, D), BF16), wide(D), wide(count), wide(rows), wide(rows), wide(rows)],
        "project",
        cost=pl.CostEstimate(
            flops=2 * D * D * (2 * rows + count), bytes_accessed=16 * D * D, transcendentals=0
        ),
    )(device, *shards, *pieces)


def cut_attend(device, matrices, slices):
    height = matrices[0].shape[0] // slices
    matrix = pl.BlockSpec((height, D), lambda k, d: (k, 0))
    piece = pl.BlockSpec((CHIPS, 1, 4 * height, LANES), lambda k, d: (0, k, 0, 0))
    shape = jax.ShapeDtypeStruct((CHIPS, slices, 4 * height, LANES), BF16)
    return grid_call(
        cut_attend_kernel,
        (slices,),
        [matrix] * 4,
        [piece, piece],
        [shape, shape],
        "cut_attend",
        cost=moved(8 * slices * height * D),
    )(device, *matrices)


def hidden_kernel(
    kept, device_ref, normed_ref, grads_ref, *refs
):
    parts = refs[: 6 * CHIPS]
    result_ref, back_ref, first, second = refs[6 * CHIPS + kept : 6 * CHIPS + kept + 4]
    (
        normed_t, grads_t, w_gate, w_up, w_down, hidden_t, dgate_t, dup_t, moved_ref
    ) = refs[6 * CHIPS + kept + 4 :]
    device = device_ref[0]
    width = w_gate.shape[0]
    height = width // CHIPS
    blocks = D // (2 * LANES)

    @pl.when(pl.program_id(0) == 0)
    def _():
        normed_t[...] = normed_ref[...].T
        grads_t[...] = grads_ref[...].T
        result_ref[...] = jnp.zeros_like(result_ref)
        back_ref[...] = jnp.zeros_like(back_ref)

    for core in range(2):
        for chip in range(CHIPS):
            gate, up, down = parts[3 * (core * CHIPS + chip) : 3 * (core * CHIPS + chip + 1)]
            lanes = lanes_of(device, 2 * chip + core)
            w_gate[:, lanes] = gate[0]
            w_up[:, lanes] = up[0]
            for block in range(blocks):
                w_down[rows_at(device, chip, height), half_lanes(device, core, block)] = down[
                    0, pl.ds(block * height, height), :
                ]

    joint = 2 * height

    for j in range(width // joint):
        start = j * joint
        rows = pl.ds(start, joint)
        gate_pre = jnp.dot(w_gate[rows, :], normed_t[...], preferred_element_type=F32)
        up_pre = jnp.dot(w_up[rows, :], normed_t[...], preferred_element_type=F32)
        grad_hidden = jnp.dot(w_down[rows, :], grads_t[...], preferred_element_type=F32)
        sig = jax.nn.sigmoid(gate_pre)
        silu = gate_pre * sig
        hidden = (silu * up_pre).astype(BF16)
        dup = (grad_hidden * silu).astype(BF16)
        dgate = (grad_hidden * up_pre * sig * (1.0 + gate_pre * (1.0 - sig))).astype(BF16)
        hidden_t[rows, :] = hidden
        dup_t[rows, :] = dup
        dgate_t[rows, :] = dgate

        moved_ref[...] = jnp.dot(hidden, grads_ref[...], preferred_element_type=F32).astype(BF16)
        for part in range(2):
            chip = (device >> 1) ^ (2 * j + part)
            for core, pieces in enumerate((first, second)):
                for block in range(blocks):
                    pieces[chip, 0, pl.ds(2 * width + block * height, height), :] = moved_ref[
                        pl.ds(part * height, height), half_lanes(device, core, block)
                    ]
        for member, values in enumerate((dgate, dup)):
            moved_ref[...] = jnp.dot(values, normed_ref[...], preferred_element_type=F32).astype(BF16)
            target = pl.ds(member * width + start, joint)
            for core, pieces in enumerate((first, second)):
                for chip in range(CHIPS):
                    pieces[chip, 0, target, :] = moved_ref[:, lanes_of(device, 2 * chip + core)]

    result_ref[...] += jnp.dot(hidden_t[...].T, w_down[...], preferred_element_type=F32)
    back_ref[...] += jnp.dot(dgate_t[...].T, w_gate[...], preferred_element_type=F32)
    back_ref[...] += jnp.dot(dup_t[...].T, w_up[...], preferred_element_type=F32)


def hidden_layer(device, normed, grads, pieces, width, start, slices, earlier=()):
    count = normed.shape[0]
    whole = pl.BlockSpec((count, D), lambda k, d: (0, 0))
    piece = lambda first, part: pl.BlockSpec(
        (1, width, LANES), lambda k, d: (first + start + k, part, 0)
    )
    out_piece = pl.BlockSpec((CHIPS, 1, 3 * width, LANES), lambda k, d: (0, start + k, 0, 0))
    shape = jax.ShapeDtypeStruct((CHIPS, pieces[0].shape[0], 3 * width, LANES), BF16)
    total = jax.ShapeDtypeStruct((count, D), F32)
    first_kept = 3 + 6 * CHIPS
    return grid_call(
        functools.partial(hidden_kernel, len(earlier)),
        (slices,),
        [whole, whole]
        + [piece(first, part) for first in first_slices(pieces) for part in range(3)]
        + [pl.BlockSpec(memory_space=pl.ANY)] * len(earlier),
        [whole, whole, out_piece, out_piece],
        [total, total, shape, shape],
        "hidden_layer",
        scratch=[
            pltpu.VMEM((D, count), BF16),
            pltpu.VMEM((D, count), BF16),
            pltpu.VMEM((width, D), BF16),
            pltpu.VMEM((width, D), BF16),
            pltpu.VMEM((width, D), BF16),
            pltpu.VMEM((width, count), BF16),
            pltpu.VMEM((width, count), BF16),
            pltpu.VMEM((width, count), BF16),
            pltpu.VMEM((2 * width // CHIPS, D), BF16),
        ],
        cost=pl.CostEstimate(
            flops=18 * slices * width * D * count,
            bytes_accessed=12 * slices * width * D,
            transcendentals=0,
        ),
        aliases={first_kept + i: 2 + i for i in range(len(earlier))},
    )(device, normed, grads, *[piece for piece in pieces for _ in range(3)], *earlier)


def exchanges():
    axes = ("dp", "mp")
    size = lax.axis_size(axes)
    masks = [1 << bit for bit in range(size.bit_length() - 1)]
    if size == 32:
        masks = [3, 5, 9, 17, 7]
    return [(axes, [(i, i ^ mask) for i in range(size)]) for mask in masks]


def neighbours(values, axis, steps):
    return [pairwise(values, axis, step) for step in steps]


def sum_of_four(values, others):
    return (values + others[0]) + (others[1] + others[2])


def hash_rows(hashes):
    digits = jnp.stack([hashes >> 14, (hashes >> 7) & 127, hashes & 127])
    rows = digits.astype(BF16).reshape(-1, LANES)
    return jnp.pad(rows, ((0, -rows.shape[0] % 32), (0, 0)))


def rows_hash(rows, count):
    used = 3 * count // LANES
    digits = rows[..., :used, :].reshape(-1, 3, count).astype(F32)
    return ((digits[:, 0] * 128.0 + digits[:, 1]) * 128.0 + digits[:, 2]).reshape(-1)


def gather_small(values):
    for axis, pairs in exchanges():
        values = jnp.concatenate([values, lax.ppermute(values, axis, pairs)], axis=0)
    return values


def sum_small(values):
    for axis, pairs in exchanges():
        values = values + lax.ppermute(values, axis, pairs)
    return values


def fill_bias(bias_ref, query_labels, key_labels, tile, tile_count, history):
    for t in range(tile_count):
        span = SPAN + tile
        key_pos = lax.broadcasted_iota(jnp.int32, (span, tile), 0) + (history - SPAN + t * tile)
        query_pos = lax.broadcasted_iota(jnp.int32, (span, tile), 1) + (history + t * tile)
        same = key_labels[pl.ds(history - SPAN + t * tile, span), :] == query_labels[:, pl.ds(t * tile, tile)]
        bias_ref[t] = jnp.where(same & (key_pos <= query_pos), 0.0, MASKED)


def head_rows(values, head):
    row = lax.broadcasted_iota(jnp.int32, values.shape, 0)
    return jnp.where((row >= head * HD) & (row < (head + 1) * HD), values, jnp.zeros_like(values))


def head_lanes(values, head):
    lane = lax.broadcasted_iota(jnp.int32, values.shape, 1)
    return jnp.where((lane >= head * HD) & (lane < (head + 1) * HD), values, jnp.zeros_like(values))


def attend_kernel(
    tile, history, query_labels, key_labels, q_ref, k_ref, v_ref, o_ref, lse_ref, bias_ref, vt_ref
):
    tile_count = q_ref.shape[0] // tile
    span = SPAN + tile

    @pl.when(pl.program_id(0) == 0)
    def _():
        fill_bias(bias_ref, query_labels, key_labels, tile, tile_count, history)

    vt_ref[...] = v_ref[...].T
    chunk = math.gcd(span, 256)
    for t in range(tile_count):
        base = history - SPAN + t * tile
        queries = (q_ref[pl.ds(t * tile, tile), :] * HD ** (-0.5)).astype(BF16).T
        outputs = []
        for head in range(2):
            rows = head_rows(queries, head)
            scores, maximum = [], None
            for start in range(0, span, chunk):
                part = (
                    jnp.dot(k_ref[pl.ds(base + start, chunk), :], rows, preferred_element_type=F32)
                    + bias_ref[t, pl.ds(start, chunk), :]
                )
                top = jnp.max(part, axis=0, keepdims=True)
                maximum = top if maximum is None else jnp.maximum(maximum, top)
                scores.append(part)
            total, weighted = 0.0, 0.0
            for i, part in enumerate(scores):
                powers = jnp.exp(part - maximum)
                total = total + jnp.sum(powers, axis=0, keepdims=True)
                weighted = weighted + jnp.dot(
                    vt_ref[pl.ds(head * HD, HD), pl.ds(base + i * chunk, chunk)],
                    powers.astype(BF16),
                    preferred_element_type=F32,
                )
            outputs.append(weighted * (1.0 / total))
            lse_ref[0, pl.ds(head, 1), pl.ds(t * tile, tile)] = maximum + jnp.log(total)
        o_ref[pl.ds(t * tile, tile), :] = jnp.concatenate(outputs, axis=0).T.astype(BF16)


def attend_back_kernel(
    tile, history, query_labels, key_labels, q_ref, k_ref, v_ref, o_ref, do_ref, lse_ref,
    dq_ref, dk_ref, dv_ref, bias_ref, kt_ref, dk_acc, dv_acc,
):
    tile_count = q_ref.shape[0] // tile
    span = SPAN + tile

    @pl.when(pl.program_id(0) == 0)
    def _():
        fill_bias(bias_ref, query_labels, key_labels, tile, tile_count, history)

    kt_ref[...] = k_ref[...].T
    dk_acc[...] = jnp.zeros_like(dk_acc)
    dv_acc[...] = jnp.zeros_like(dv_acc)
    for t in range(tile_count):
        base = history - SPAN + t * tile
        scaled = (q_ref[pl.ds(t * tile, tile), :] * HD ** (-0.5)).astype(BF16)
        grads = do_ref[pl.ds(t * tile, tile), :]
        scaled_t, grads_t = scaled.T, grads.T
        product_t = grads_t.astype(F32) * o_ref[pl.ds(t * tile, tile), :].T.astype(F32)
        keys = k_ref[pl.ds(base, span), :]
        values = v_ref[pl.ds(base, span), :]
        grad_queries = []
        for head in range(2):
            scores = (
                jnp.dot(keys, head_rows(scaled_t, head), preferred_element_type=F32) + bias_ref[t]
            )
            attention = jnp.exp(scores - lse_ref[0, pl.ds(head, 1), pl.ds(t * tile, tile)])
            row_terms = jnp.sum(product_t[head * HD : (head + 1) * HD], axis=0, keepdims=True)
            grad_attention = jnp.dot(values, head_rows(grads_t, head), preferred_element_type=F32)
            grad_scores = (attention * (grad_attention - row_terms)).astype(BF16)
            dv_acc[pl.ds(base, span), :] += jnp.dot(
                attention.astype(BF16), head_lanes(grads, head), preferred_element_type=F32
            )
            dk_acc[pl.ds(base, span), :] += jnp.dot(
                grad_scores, head_lanes(scaled, head), preferred_element_type=F32
            )
            grad_queries.append(
                jnp.dot(
                    kt_ref[pl.ds(head * HD, HD), pl.ds(base, span)],
                    grad_scores,
                    preferred_element_type=F32,
                )
            )
        dq_ref[pl.ds(t * tile, tile), :] = (
            jnp.concatenate(grad_queries, axis=0).T * HD ** (-0.5)
        ).astype(BF16)
    dk_ref[...] = dk_acc[...].astype(BF16)
    dv_ref[...] = dv_acc[...].astype(BF16)


def attention_specs(count, window, start):
    whole = lambda shape: pl.BlockSpec(shape, lambda h: (0,) * len(shape))
    specs = []
    for first in (start, 0):
        own = pl.BlockSpec((count, PAIR), lambda h, first=first: (0, first + h))
        seen = pl.BlockSpec((window, PAIR), lambda h, first=first: (0, first + h))
        specs.append((own, seen))
    sums = pl.BlockSpec((1, 2, count), lambda h: (h, 0, 0))
    labels = [whole((1, count)), whole((window, 1))]
    return labels, specs[0], specs[1], sums


def attend(inputs, tile, start, pairs):
    _, _, queries, keys, _ = inputs
    count, window = queries.shape[0], keys.shape[0]
    labels, (own, seen), (own_out, _), sums = attention_specs(count, window, start)
    work = 2 * count * (SPAN + tile) * PAIR * pairs
    return pl.pallas_call(
        functools.partial(attend_kernel, tile, window - count),
        grid=(pairs,),
        in_specs=labels + [own, seen, seen],
        out_specs=[own_out, sums],
        out_shape=[
            jax.ShapeDtypeStruct((count, pairs * PAIR), BF16),
            jax.ShapeDtypeStruct((pairs, 2, count), F32),
        ],
        scratch_shapes=[
            pltpu.VMEM((count // tile, SPAN + tile, tile), F32),
            pltpu.VMEM((PAIR, window), BF16),
        ],
        cost_estimate=pl.CostEstimate(
            flops=4 * work, bytes_accessed=4 * (window + count) * PAIR * pairs, transcendentals=0
        ),
        name="attend",
    )(*inputs)


def attend_back(inputs, context, grads, log_sums, tile, start, pairs):
    _, _, queries, keys, _ = inputs
    count, window = queries.shape[0], keys.shape[0]
    labels, (own, seen), (own_out, seen_out), sums = attention_specs(count, window, start)
    work = 2 * count * (SPAN + tile) * PAIR * pairs
    return pl.pallas_call(
        functools.partial(attend_back_kernel, tile, window - count),
        grid=(pairs,),
        in_specs=labels + [own, seen, seen, own_out, own, sums],
        out_specs=[own_out, seen_out, seen_out],
        out_shape=[
            jax.ShapeDtypeStruct((count, pairs * PAIR), BF16),
            jax.ShapeDtypeStruct((window, pairs * PAIR), BF16),
            jax.ShapeDtypeStruct((window, pairs * PAIR), BF16),
        ],
        scratch_shapes=[
            pltpu.VMEM((count // tile, SPAN + tile, tile), F32),
            pltpu.VMEM((PAIR, window), BF16),
            pltpu.VMEM((window, PAIR), F32),
            pltpu.VMEM((window, PAIR), F32),
        ],
        cost_estimate=pl.CostEstimate(
            flops=10 * work, bytes_accessed=8 * (window + count) * PAIR * pairs, transcendentals=0
        ),
        name="attend_back",
    )(*inputs, context, grads, log_sums)


def project_back_kernel(per_shard, *refs):
    queries, keys, values = refs[0:2], refs[2:4], refs[4:6]
    weights, normed = refs[6:8]
    back_refs, gain_ref, total = refs[8:-2], refs[-2], refs[-1]
    half = queries[0].shape[1]
    shard = lax.div(pl.program_id(0), per_shard)
    back = None
    for member, parts in ((1, keys), (2, values)):
        for i, part in enumerate(parts):
            term = mxu(part[...], weights[member, pl.ds(i * half, half), :])
            back = term if back is None else back + term
    total[...] = back

    @pl.when(shard == len(back_refs) - 1)
    def _():
        total[...] += mxu(queries[0][...], weights[0, pl.ds(0, half), :]) + mxu(
            queries[1][...], weights[0, pl.ds(half, half), :]
        )

    for i, ref in enumerate(back_refs):

        @pl.when(shard == i)
        def _(ref=ref):
            ref[...] = total[...].astype(ref.dtype)

    @pl.when(pl.program_id(0) == 0)
    def _():
        gain_ref[...] = jnp.zeros_like(gain_ref)

    gain_ref[...] += jnp.sum(total[...] * normed[...].astype(F32), axis=0, keepdims=True)


def project_back(first, second, weights, window):
    count, half = first[0].shape
    rows = window.shape[0]
    shards = rows // count
    tile = min(256, count)
    per_shard = count // tile
    shard_spec = lambda width, shard: pl.BlockSpec(
        (tile, width), lambda i: (jnp.clip(i - shard * per_shard, 0, per_shard - 1), 0)
    )
    own = shard_spec(half, shards - 1)
    seen = pl.BlockSpec((tile, half), lambda i: (i, 0))
    wide = pl.BlockSpec((tile, D), lambda i: (i, 0))
    shapes = [
        jax.ShapeDtypeStruct((count, D), BF16 if shard == 0 and shards > 1 else F32)
        for shard in range(shards)
    ]
    outs = pl.pallas_call(
        functools.partial(project_back_kernel, per_shard),
        grid=(rows // tile,),
        in_specs=[own, own, seen, seen, seen, seen, pl.BlockSpec((3, D, D), lambda i: (0, 0, 0)), wide],
        out_specs=[shard_spec(D, shard) for shard in range(shards)]
        + [pl.BlockSpec((1, D), lambda i: (0, 0))],
        out_shape=shapes + [jax.ShapeDtypeStruct((1, D), F32)],
        scratch_shapes=[pltpu.VMEM((tile, D), F32)],
        cost_estimate=pl.CostEstimate(
            flops=2 * D * D * (2 * rows + count), bytes_accessed=12 * rows * D, transcendentals=0
        ),
        name="project_back",
    )(first[0], second[0], first[1], second[1], first[2], second[2], weights, window)
    return outs[:-1], outs[-1]


def split(values):
    high = values.astype(BF16)
    return high, (values - high.astype(F32)).astype(BF16)


def dot_split(first, second, contract):
    dims = ((contract, contract), ((), ()))
    (a, b), (c, d) = split(first), split(second)
    multiply = lambda x, y: lax.dot_general(x, y, dims, preferred_element_type=F32)
    return multiply(a, c) + multiply(b, c) + multiply(a, d)


def total_of(values):
    return jnp.sum(jnp.sum(values, axis=0, keepdims=True), axis=1, keepdims=True)


def mxu(first, second):
    return jnp.dot(first, second, preferred_element_type=F32)


class Chain:
    def __init__(self, matrix, rows, spread):
        self.matrix, self.rows, self.spread = matrix, rows, spread

    def square(self):
        self.low = self.matrix.astype(BF16)
        height = self.rows.shape[0]
        stacked = jnp.concatenate([self.rows.astype(BF16), self.low], axis=0)
        both = mxu(stacked, self.spread(self.low))
        self.rows = 1.25 * self.rows - 0.25 * both[:height]
        self.rest = (0.0625 * both[height:] - 0.625 * self.low.astype(F32)).astype(BF16)

    def half(self):
        self.right = self.spread(self.rest)
        self.matrix = 1.5625 * self.matrix + mxu(self.low, self.right)

    def whole(self):
        self.matrix = 1.5625 * self.matrix + mxu(self.matrix.astype(BF16), self.right)

    def last(self):
        self.rows = 1.25 * self.rows - 0.25 * mxu(
            self.rows.astype(BF16), self.spread(self.matrix.astype(BF16))
        )


def run_chains(chains):
    for _ in range(ROOTS - 1):
        for chain in chains:
            chain.square()
        for chain in chains:
            chain.half()
        for chain in chains:
            chain.whole()
    for chain in chains:
        chain.last()


def quarter(norm):
    return lax.rsqrt(jnp.sqrt(norm))


def shampoo_blocks(step_size, pack, grads, shorts_old, longs_old, short_out, long_out):
    blocks = len(grads)
    short, width = grads[0].shape
    side = pack * short
    row = lax.broadcasted_iota(jnp.int32, (side, side), 0)
    lane = lax.broadcasted_iota(jnp.int32, (side, side), 1)
    mask = jnp.where(lax.div(row, short) == lax.div(lane, short), 1.0, 0.0).astype(BF16)
    eye = jnp.where(
        lax.broadcasted_iota(jnp.int32, (short, side), 0)
        == lax.rem(lax.broadcasted_iota(jnp.int32, (short, side), 1), short),
        1.0,
        0.0,
    )
    spread = lambda values: jnp.concatenate([values] * pack, axis=0) * mask
    beside = lambda values: jnp.concatenate(values, axis=1)
    alone = lambda values: values
    packed_long = width == short

    shorts, longs, scales = [], [], []
    for b, grad in enumerate(grads):
        short_new = 0.5 * shorts_old(b) + 0.5 * dot_split(grad, grad, (1,))
        grad_t = grad.T
        long_new = 0.5 * longs_old(b) + 0.5 * dot_split(grad_t, grad_t, (1,))
        short_out(b, short_new)
        long_out(b, long_new)
        short_norm = jnp.sqrt(total_of(short_new * short_new) + 1e-06)
        long_norm = jnp.sqrt(total_of(long_new * long_new) + 1e-06)
        shorts.append(short_new / short_norm)
        longs.append(long_new / long_norm)
        scales.append(step_size * quarter(short_norm) * quarter(long_norm))
    groups = [range(i, i + pack) for i in range(0, blocks, pack)]
    left = [Chain(beside([shorts[b] for b in g]), eye, spread) for g in groups]
    if packed_long:
        right = [
            Chain(beside([longs[b] for b in g]), beside([grads[b] for b in g]), spread) for g in groups
        ]
    else:
        right = [Chain(longs[b], grads[b], alone) for b in range(blocks)]
    run_chains(left + right)
    steps = []
    for i, g in enumerate(groups):
        high, low = split(left[i].rows)
        if packed_long:
            second, second_low = split(right[i].rows)
            second, second_low = spread(second), spread(second_low)
            total = mxu(high, second) + mxu(low, second) + mxu(high, second_low)
            parts = [total[:, j * short : (j + 1) * short] for j in range(pack)]
        else:
            second, second_low = split(jnp.concatenate([right[b].rows for b in g], axis=0))
            high, low = spread(high), spread(low)
            total = mxu(high, second) + mxu(low, second) + mxu(high, second_low)
            parts = [total[j * short : (j + 1) * short] for j in range(pack)]
        steps += [scales[b] * part for b, part in zip(g, parts)]
    return steps


def put(ref, lead=()):
    def store(b, values):
        ref[lead + (b,)] = values

    return store


def shampoo_kernel(
    step_size, pack, grad_ref, master_ref, short_ref, long_ref, weight_ref, short_out, long_out
):
    blocks = grad_ref.shape[0]
    steps = shampoo_blocks(
        step_size,
        pack,
        [grad_ref[b] for b in range(blocks)],
        lambda b: short_ref[b],
        lambda b: long_ref[b],
        put(short_out),
        put(long_out),
    )
    for b, step in enumerate(steps):
        weight_ref[b] = master_ref[b] - step


def shampoo_rows_kernel(
    step_size, turned, across, kept, scale_ref, own, one, two, master_ref, short_ref, long_ref, *refs
):
    grad_ref, weight_ref, short_out, long_out = refs[kept:]
    rows = own[0] + one[...].astype(F32) + two[...].astype(F32)
    rows = rows * scale_ref[0]
    groups = 4
    height = rows.shape[0] // groups
    grads = [None] * (2 * groups)
    for group in range(groups):
        slab = rows[group * height : (group + 1) * height]
        tall = slab.T if turned else None
        for half in range(2):
            b = half * groups + group if across else 2 * group + half
            lanes = slice(half * BLK, (half + 1) * BLK)
            grads[b] = tall[lanes] if turned else slab[:, lanes]
            grad_ref[0, b] = grads[b]
    steps = shampoo_blocks(
        step_size,
        4,
        grads,
        lambda b: short_ref[0, b],
        lambda b: long_ref[0, b],
        put(short_out, (0,)),
        put(long_out, (0,)),
    )
    for b, step in enumerate(steps):
        weight_ref[0, b] = master_ref[0, b] - step


def shampoo_rows(
    terms, scale, master, short_old, long_old, step_size, first, turned, across, start=0, stop=None, earlier=()
):
    members, blocks, height, width = master.shape
    stop = members if stop is None else stop
    short, long = short_old.shape[-1], long_old.shape[-1]
    rows = blocks // 2 * long
    spec = lambda *shape: pl.BlockSpec((1, blocks) + shape, lambda i: (start + i, 0, 0, 0))
    shape = lambda *dims: jax.ShapeDtypeStruct((members, blocks) + dims, F32)
    term = pl.BlockSpec((rows, LANES), lambda i: (first + start + i, 0))
    own = pl.BlockSpec((1, rows, LANES), lambda i: (0, first + start + i, 0))
    return pl.pallas_call(
        functools.partial(shampoo_rows_kernel, step_size, turned, across, len(earlier)),
        grid=(stop - start,),
        in_specs=[
            pl.BlockSpec(memory_space=pltpu.SMEM),
            own,
            term,
            term,
            spec(height, width),
            spec(short, short),
            spec(long, long),
        ]
        + [pl.BlockSpec(memory_space=pl.ANY)] * len(earlier),
        out_specs=[spec(height, width), spec(height, width), spec(short, short), spec(long, long)],
        out_shape=[shape(height, width), shape(height, width), shape(short, short), shape(long, long)],
        input_output_aliases={7 + i: i for i in range(len(earlier))},
        cost_estimate=pl.CostEstimate(
            flops=160 * (stop - start) * blocks * long * long * long,
            bytes_accessed=8 * (stop - start) * blocks * (long * long + short * short + 2 * short * long),
            transcendentals=0,
        ),
        name="shampoo_rows",
    )(scale.reshape(1), terms[0][None], terms[1], terms[2], master, short_old, long_old, *earlier)


def shampoo(gradient, master, short_old, long_old, step_size, blocks):
    count, short, width = gradient.shape
    blocks = min(blocks, count)
    pack = min(4, blocks)
    spec = lambda *shape: pl.BlockSpec((blocks,) + shape, lambda i: (i, 0, 0))
    specs = [spec(short, width), spec(short, short), spec(width, width)]
    shape = lambda *dims: jax.ShapeDtypeStruct((count,) + dims, F32)
    return pl.pallas_call(
        functools.partial(shampoo_kernel, step_size, pack),
        grid=(count // blocks,),
        in_specs=specs[:1] + specs,
        out_specs=specs,
        out_shape=[shape(short, width), shape(short, short), shape(width, width)],
        cost_estimate=pl.CostEstimate(
            flops=40 * count * width * width * width,
            bytes_accessed=8 * count * (width * width + short * short + 2 * short * width),
            transcendentals=0,
        ),
        name="shampoo",
    )(gradient, master, short_old, long_old)
def step_rows(gradient, master, left, right, step_size, blocks):
    flat = lambda values: values.reshape((-1,) + values.shape[-2:])
    outs = shampoo(flat(gradient), flat(master), flat(left), flat(right), step_size, blocks)
    return tuple(v.reshape(gradient.shape[:-2] + v.shape[-2:]) for v in outs)


def turn(values):
    return jnp.swapaxes(values, -1, -2)


def step_columns(gradient, master, left, right, step_size, blocks):
    weight, right, left = shampoo(turn(gradient), turn(master), right, left, step_size, blocks)
    return turn(weight), left, right


def two_by_two(first, second):
    (a, b), (c, d) = first
    (e, f), (g, h) = second
    return ((a * e + b * g, a * f + b * h), (c * e + d * g, c * f + d * h))


def quarter_root_pair(statistic):
    frobenius = jnp.sqrt(sum(v * v for row in statistic for v in row) + 1e-06)
    matrix = tuple(tuple(v / frobenius for v in row) for row in statistic)
    estimate = ((1.0, 0.0), (0.0, 1.0))
    for iteration in range(ROOTS):
        (a, b), (c, d) = matrix
        update = (((5.0 - a) * 0.25, -b * 0.25), (-c * 0.25, (5.0 - d) * 0.25))
        estimate = two_by_two(estimate, update)
        squared = two_by_two(update, update)
        matrix = two_by_two(two_by_two(squared, squared), matrix)
    scale = lax.rsqrt(jnp.sqrt(frobenius))
    return tuple(tuple(v * scale for v in row) for row in estimate)


def gain_kernel(grad_ref, gain_ref, left_ref, right_ref, weight_ref, left_out, right_out):
    grads = [grad_ref[pl.ds(i, 1), :] for i in range(2)]
    inner = lambda i, j: jnp.sum(grads[i] * grads[j], axis=1, keepdims=True)
    products = ((inner(0, 0), inner(0, 1)), (inner(1, 0), inner(1, 1)))
    left = tuple(
        tuple(
            0.5 * left_ref[pl.ds(i, 1), pl.ds(j, 1)] + 0.5 * products[i][j] for j in range(2)
        )
        for i in range(2)
    )
    left_out[...] = jnp.concatenate([jnp.concatenate(row, axis=1) for row in left], axis=0)
    right = 0.5 * right_ref[...] + 0.5 * (grads[0] * grads[0] + grads[1] * grads[1])
    right_out[...] = right
    root = quarter_root_pair(left)
    scale = GAIN_RATE * lax.rsqrt(jnp.sqrt(right))
    for i in range(2):
        mixed = root[i][0] * grads[0] + root[i][1] * grads[1]
        weight_ref[pl.ds(i, 1), :] = gain_ref[pl.ds(i, 1), :] - scale * mixed


def gain_update(gradient, gain_rows, left_old, right_old):
    shapes = [gain_rows.shape, left_old.shape, (1, right_old.size)]
    weight, left_new, right_new = pl.pallas_call(
        gain_kernel,
        out_shape=[jax.ShapeDtypeStruct(shape, F32) for shape in shapes],
        name="gain_update",
    )(gradient, gain_rows, left_old, right_old.reshape(1, -1))
    return weight, left_new, right_new.reshape(-1)


def dot(first, second):
    return jnp.dot(first, second, preferred_element_type=F32)


def dot_back(first, second):
    return lax.dot_general(first, second, (((1,), (1,)), ((), ())), preferred_element_type=F32)


def dot_weight(first, second):
    return lax.dot_general(first, second, (((0,), (0,)), ((), ())), preferred_element_type=F32)


def body(
    patches,
    cotangent,
    lengths,
    hashes,
    segments,
    attend_master,
    output_master,
    expand_master,
    reduce_master,
    gains,
    attend_left,
    attend_right,
    output_left,
    output_right,
    expand_left,
    expand_right,
    reduce_left,
    reduce_right,
    gains_left,
    gains_right,
):
    dp_size, mp_size = lax.axis_size("dp"), lax.axis_size("mp")
    mp_index = lax.axis_index("mp")
    count = patches.shape[0]
    head_width, hidden_width = D // mp_size, FF // mp_size
    head_rows_width = head_width // CHIPS
    total_patches = count * dp_size * mp_size
    earlier = -(-(SPAN - 1) // count)
    history = earlier * count
    tile = min(256, count)
    fast = dp_size == 2 * CHIPS and mp_size == 4
    device = coordinate(fast)
    grids = {
        name: piece_shape(master.shape, rows, dp_size)
        for name, master, rows in (
            ("attend", attend_master, D),
            ("output", output_master, head_width),
            ("expand", expand_master, D),
            ("reduce", reduce_master, hidden_width),
        )
    }

    stream = patches.astype(F32)
    first_rms = lax.rsqrt(jnp.mean(stream * stream, axis=1, keepdims=True) + EPSILON)
    first_hat = stream * first_rms
    first_normed = (first_hat * gains[0]).astype(BF16)

    row_labels = segments.reshape(-1)
    padded = jnp.concatenate([jnp.full((history,), -1, jnp.int32), row_labels])
    key_labels = lax.dynamic_slice_in_dim(padded, mp_index * count, history + count, 0)
    query_labels = key_labels[history:].reshape(1, count)
    key_labels = key_labels.reshape(-1, 1)
    up_one = [(i, i + 1) for i in range(mp_size - 1)]
    down_one = [(i + 1, i) for i in range(mp_size - 1)]
    half_pairs = HEADS * HD // PAIR // 2

    def count_own(all_hashes):
        own = hashes.astype(F32)
        return jnp.sum((own[:, None] == all_hashes[None, :]).astype(F32), axis=1)

    def halo(values):
        return lax.ppermute(values, "mp", up_one)

    if fast:
        attend_rows = jnp.concatenate(
            [
                rows_of_columns(to_piece(attend_master.astype(BF16), *grids["attend"][:2])),
                rows_of_rows(to_piece(output_master.astype(BF16), *grids["output"][:2])),
                hash_rows(hashes),
            ]
        )
        slice_two = pairwise(attend_rows, "mp", 2)
        slice_one = pairwise(attend_rows, "mp", 1)
        halo_source, slice_two = together(first_normed, slice_two)
        slice_three = pairwise(slice_two, "mp", 1)
        near_halo = halo(halo_source)
        attend_slices = jnp.stack([attend_rows, slice_one, slice_two, slice_three])
        sides = gather_sides(attend_slices)
        near_halo, sides = together(near_halo, sides)
        corners = gather_corner(*sides)
        shards = [near_halo, first_normed]
        for _ in range(earlier - 1):
            shards.insert(0, halo(shards[0]))
        shards[0], corners = together(shards[0], corners)
        attend_pieces = gather_end(attend_slices, *sides, *corners)
        all_hashes = jnp.concatenate(
            [rows_hash(piece[:, 4 * head_width :], count) for i, piece in enumerate(attend_pieces) if i != 6]
        )
    else:
        attend_cut = jnp.concatenate(
            [
                cut_columns(weight_by_columns(attend_master, dp_size), mp_size),
                cut_rows(weight_by_rows(output_master, head_width, dp_size), mp_size),
            ],
            axis=3,
        )
        attend_pieces = [attend_cut[chip, core] for core in range(2) for chip in range(CHIPS)]
        hidden_cut = jnp.concatenate(
            [
                cut_columns(weight_by_columns(expand_master, dp_size), mp_size),
                cut_rows(weight_by_rows(reduce_master, hidden_width, dp_size), mp_size),
            ],
            axis=3,
        )
        near_pieces, far_pieces = (
            [hidden_cut[chip, core, k : k + 2] for core in range(2) for chip in range(CHIPS)]
            for k in (0, 2)
        )
        shards = [first_normed]
        for _ in range(earlier):
            shards.insert(0, halo(shards[0]))
        all_hashes = gather_small(hashes).astype(F32)

    raw_weight = lengths.astype(F32) * lax.rsqrt(count_own(all_hashes))
    raw_total = jnp.sum(raw_weight).reshape(1, 1)
    steps = exchanges()
    grad_out = cotangent.astype(F32) * raw_weight[:, None]
    grad_low = grad_out.astype(BF16)

    if fast:
        hidden_rows = jnp.concatenate(
            [
                rows_of_columns(to_piece(expand_master.astype(BF16), *grids["expand"][:2])),
                rows_of_rows(to_piece(reduce_master.astype(BF16), *grids["reduce"][:2])),
            ]
        )
        shards[0], hidden_rows = together(shards[0], hidden_rows)
        slice_one = pairwise(hidden_rows, "mp", 1)
        slice_two = pairwise(hidden_rows, "mp", 2)
    attend_w, output_w, queries, keys, values, window = project(device, shards, attend_pieces)
    labels = (query_labels, key_labels)
    if fast:
        queries, slice_one = together(queries, slice_one)
        near = jnp.stack([hidden_rows, slice_one])
        sides = gather_sides(near)
    inputs = labels + (queries, keys, values)
    context_a, sums_a = attend(inputs, tile, 0, half_pairs)
    if fast:
        queries, context_a, sides, slice_two = together(queries, context_a, sides, slice_two)
        inputs = labels + (queries, keys, values)
        corners = gather_corner(*sides)
        slice_three = pairwise(slice_two, "mp", 1)
        moved = lax.ppermute(raw_total, *steps[0])
    context_b, sums_b = attend(inputs, tile, half_pairs, half_pairs)
    if fast:
        context_b, corners, slice_three, moved = together(context_b, corners, slice_three, moved)
        raw_total = raw_total + moved
        moved = lax.ppermute(raw_total, *steps[1])
        near_pieces = gather_end(near, *sides, *corners)
        far = jnp.stack([slice_two, slice_three])
        sides = gather_sides(far)
    half = context_a.shape[1]
    middle = stream + dot(context_a, output_w[:half]) + dot(context_b, output_w[half:])

    second_rms = lax.rsqrt(jnp.mean(middle * middle, axis=1, keepdims=True) + EPSILON)
    second_hat = middle * second_rms
    second_normed = (second_hat * gains[1]).astype(BF16)
    if fast:
        second_normed, near_pieces, moved = together(second_normed, near_pieces, moved)
        raw_total = raw_total + moved
        moved = lax.ppermute(raw_total, *steps[2])
        share_a = hidden_layer(device, second_normed, grad_low, near_pieces, hidden_width, 0, 1)
        share_a, sides, moved = together(share_a, sides, moved)
        raw_total = raw_total + moved
        moved = lax.ppermute(raw_total, *steps[3])
        corners = gather_corner(*sides)
        share_b = hidden_layer(
            device, second_normed, grad_low, near_pieces, hidden_width, 1, 1, share_a[2:]
        )
        share_b, corners, moved = together(share_b, corners, moved)
        raw_total = raw_total + moved
        moved = lax.ppermute(raw_total, *steps[4])
        far_pieces = gather_end(far, *sides, *corners)
        near_grads = share_b[2:]
        near_received = pairwise(near_grads[1], "dp", 1)
        share_c = hidden_layer(device, second_normed, grad_low, far_pieces, hidden_width, 0, 2)
        share_c, near_received, moved = together(share_c, near_received, moved)
        raw_total = raw_total + moved
        far_grads = share_c[2:]
        far_received = pairwise(far_grads[1], "dp", 1)
        near_corners = send_planar(*corner_sums(near_grads[0], near_received))
        second_back = share_a[1] + share_b[1] + share_c[1]
        activations = (middle + share_a[0] + share_b[0] + share_c[0]).astype(BF16)
    else:
        share_a = hidden_layer(device, second_normed, grad_low, near_pieces, hidden_width, 0, 2)
        share_c = hidden_layer(device, second_normed, grad_low, far_pieces, hidden_width, 0, 2)
        near_grads, far_grads = share_a[2:], share_c[2:]
        raw_total = sum_small(raw_total)
        second_back = share_a[1] + share_c[1]
        activations = (middle + share_a[0] + share_c[0]).astype(BF16)

    weight_scale = total_patches / raw_total[0, 0]

    second_scaled = second_back * gains[1]
    gain_second = jnp.sum(second_back * second_hat, axis=0)
    middle_grad = grad_out + second_rms * (
        second_scaled - second_hat * jnp.mean(second_scaled * second_hat, axis=1, keepdims=True)
    )
    middle_low = middle_grad.astype(BF16)
    grad_context = dot_back(middle_low, output_w).astype(BF16)

    def key_grads(parts):
        return dot_weight(parts[1], window).astype(BF16)

    def weight_grads(context_part, parts, keys_part):
        return [
            dot_weight(parts[0], first_normed).astype(BF16),
            keys_part,
            dot_weight(parts[2], window).astype(BF16),
            dot_weight(context_part, middle_low).astype(BF16),
        ]

    slices_half = mp_size // 2
    if fast:
        grad_context, near_corners = together(grad_context, near_corners)
        near_sides = side_sums(near_grads[0], near_received, *near_corners)
        grad_context, near_sides = together(grad_context, near_sides)
        near_sides = send_planar(*near_sides)
    backs_a = attend_back(inputs, context_a, grad_context, sums_a, tile, 0, half_pairs)
    keys_a = key_grads(backs_a)
    if fast:
        backs_a, keys_a, near_sides, far_received = together(backs_a, keys_a, near_sides, far_received)
        far_corners = corner_sums(far_grads[0], far_received)
        near_own, near_one = own_sums(near_grads[0], near_received, *near_sides)
        backs_a, far_corners, near_one = together(backs_a, far_corners, near_one)
        far_corners = send_planar(*far_corners)
        near_one = pairwise(near_one, "mp", 1)
    cut_a = cut_attend(device, weight_grads(context_a, backs_a, keys_a), slices_half)
    if fast:
        cut_a, grad_context, far_corners = together(cut_a, grad_context, far_corners)
        far_sides = side_sums(far_grads[0], far_received, *far_corners)
        cut_a, grad_context, far_sides = together(cut_a, grad_context, far_sides)
        far_sides = send_planar(*far_sides)
        received_a = pairwise(cut_a[1], "dp", 1)
    backs_b = attend_back(inputs, context_b, grad_context, sums_b, tile, half_pairs, half_pairs)
    keys_b = key_grads(backs_b)
    if fast:
        backs_b, keys_b, far_sides, received_a, near_one = together(
            backs_b, keys_b, far_sides, received_a, near_one
        )
        far_own, far_three = own_sums(far_grads[0], far_received, *far_sides)
        corners_a = corner_sums(cut_a[0], received_a)
        backs_b, far_three, corners_a = together(backs_b, far_three, corners_a)
        far_three = pairwise(far_three, "mp", 1)
        corners_a = send_planar(*corners_a)
    cut_b = cut_attend(device, weight_grads(context_b, backs_b, keys_b), slices_half)
    if fast:
        backs_b, cut_b, corners_a, far_three = together(backs_b, cut_b, corners_a, far_three)
        sides_a = side_sums(cut_a[0], received_a, *corners_a)
        far_two = (far_own + far_three.astype(F32)).astype(BF16)
        backs_b, cut_b, sides_a, far_two = together(backs_b, cut_b, sides_a, far_two)
        sides_a = send_planar(*sides_a)
        far_two = pairwise(far_two, "mp", 2)
        received_b = pairwise(cut_b[1], "dp", 1)
    shares, gain_first = project_back(backs_a, backs_b, attend_w, window)
    gain_sums = jnp.stack([gain_first[0] / gains[0], gain_second])

    def halo_back(share):
        return lax.ppermute(share.astype(BF16), "mp", down_one)

    def first_grad(carried):
        first_back = shares[-1] + carried.astype(F32)
        first_scaled = first_back * gains[0]
        return weight_scale * (
            middle_grad
            + first_rms
            * (first_scaled - first_hat * jnp.mean(first_scaled * first_hat, axis=1, keepdims=True))
        )

    if fast:
        shares, received_b, sides_a, far_two = together(shares, received_b, sides_a, far_two)
        corners_b = corner_sums(cut_b[0], received_b)
        own_a, one_a = own_sums(cut_a[0], received_a, *sides_a)
        shares, corners_b, one_a, far_two = together(shares, corners_b, one_a, far_two)
        corners_b = send_planar(*corners_b)
        carried = halo_back(shares[0])
        one_a = pairwise(one_a, "mp", 1)
    else:
        carried = halo_back(shares[0])
        for share in shares[1:-1]:
            carried = halo_back(share + carried.astype(F32))
        gain_sums = sum_small(gain_sums)
        input_grad = first_grad(carried)
    grad_scale = weight_scale * total_patches ** (-0.5)
    reduce_step, output_step = STEP_RATE * FF ** (-0.5), STEP_RATE * OUT_FAN ** (-0.5)
    expand_step = attend_step = STEP_RATE * D ** (-0.5)
    if fast:
        far_two, corners_b = together(far_two, corners_b)
        sides_b = side_sums(cut_b[0], received_b, *corners_b)
        far_two, sides_b = together(far_two, sides_b)
        sides_b = send_planar(*sides_b)
        terms = (near_own, near_one, far_two)
        reduce_out = shampoo_rows(
            terms, grad_scale, turn(reduce_master)[None], reduce_right[None], reduce_left[None],
            reduce_step, 2, True, False,
        )
        reduce_out, terms, sides_b, carried, one_a, gain_sums = together(
            reduce_out, terms, sides_b, carried, one_a, gain_sums
        )
        own_b, three_b = own_sums(cut_b[0], received_b, *sides_b)
        carried = [(share + carried.astype(F32)).astype(BF16) for share in shares[1:-1]]
        terms, three_b, carried, gain_sums = together(terms, three_b, carried, gain_sums)
        three_b = pairwise(three_b, "mp", 1)
        carried = halo_back(carried[0])
        planar = neighbours(gain_sums, "dp", (2, 4, 6))
        expand_inputs = (grad_scale, expand_master, expand_left, expand_right, expand_step, 0, True, True)
        expand_out = shampoo_rows(terms, *expand_inputs, 0, 1)
        expand_out, terms, three_b, planar = together(expand_out, terms, three_b, planar)
        gain_sums = sum_of_four(gain_sums, planar)
        two_b = (own_b + three_b.astype(F32)).astype(BF16)
        terms, two_b, gain_sums = together(terms, two_b, gain_sums)
        two_b = pairwise(two_b, "mp", 2)
        moved = pairwise(gain_sums, "dp", 1)
        expand_out = shampoo_rows(terms, *expand_inputs, 1, 2, expand_out)
        input_grad = first_grad(carried)
        expand_out, two_b, input_grad, moved = together(expand_out, two_b, input_grad, moved)
        gain_sums = gain_sums + moved
        along = neighbours(gain_sums, "mp", (1, 2, 3))
        terms = (own_a, one_a, two_b)
        attend_out = shampoo_rows(
            terms, grad_scale, attend_master, attend_left, attend_right, attend_step, 0, True, True
        )
        attend_out, terms, along = together(attend_out, terms, along)
        gain_sums = sum_of_four(gain_sums, along)
        output_out = shampoo_rows(
            terms, grad_scale, output_master[None], output_left[None], output_right[None], output_step,
            3, False, False,
        )
        alone = lambda outs: [v[0] for v in outs]
        reduce_grad, reduce_weight, right_reduce, left_reduce = alone(reduce_out)
        reduce_grad, reduce_weight = turn(reduce_grad), turn(reduce_weight)
        expand_grad, expand_weight, left_expand, right_expand = expand_out
        attend_grad, attend_weight, left_attend, right_attend = attend_out
        output_grad, output_weight, left_output, right_output = alone(output_out)
    else:
        hidden_cut = jnp.stack(
            [jnp.concatenate([near_grads[core], far_grads[core]], axis=1) for core in range(2)], axis=1
        )
        attend_cut = jnp.stack(
            [jnp.concatenate([cut_a[core], cut_b[core]], axis=1) for core in range(2)], axis=1
        )
        expand_grad = grad_scale * grad_by_columns(
            join_columns(hidden_cut[:, :, :, : 2 * hidden_width], 2), expand_master, dp_size, mp_size
        )
        reduce_grad = grad_scale * grad_by_rows(
            join_rows(hidden_cut[:, :, :, 2 * hidden_width :]),
            reduce_master,
            hidden_width,
            dp_size,
            mp_size,
        )
        output_grad = grad_scale * grad_by_rows(
            join_rows(attend_cut[:, :, :, 3 * head_width :]), output_master, head_width, dp_size, mp_size
        )
        attend_grad = grad_scale * grad_by_columns(
            join_columns(attend_cut[:, :, :, : 3 * head_width], 3), attend_master, dp_size, mp_size
        )
        reduce_weight, left_reduce, right_reduce = step_columns(
            reduce_grad, reduce_master, reduce_left, reduce_right, reduce_step, 4
        )
        expand_weight, left_expand, right_expand = step_rows(
            expand_grad, expand_master, expand_left, expand_right, expand_step, 8
        )
        output_weight, left_output, right_output = step_rows(
            output_grad, output_master, output_left, output_right, output_step, 8
        )
        attend_weight, left_attend, right_attend = step_rows(
            attend_grad, attend_master, attend_left, attend_right, attend_step, 8
        )

    gains_grad = gain_sums * grad_scale
    gains_weight, left_gains, right_gains = gain_update(gains_grad, gains, gains_left, gains_right)
    return (
        activations,
        input_grad,
        attend_grad,
        attend_weight,
        left_attend,
        right_attend,
        output_grad,
        output_weight,
        left_output,
        right_output,
        expand_grad,
        expand_weight,
        left_expand,
        right_expand,
        reduce_grad,
        reduce_weight,
        left_reduce,
        right_reduce,
        gains_grad,
        gains_weight,
        left_gains,
        right_gains,
    )


def solution(mesh):
    rows = P(("dp", "mp"), None)
    single = P(("dp", "mp"), None, None)
    stacked = P(None, ("dp", "mp"), None, None)
    return jax.shard_map(
        body,
        mesh=mesh,
        in_specs=(
            rows,
            rows,
            P(("dp", "mp")),
            P(("dp", "mp")),
            P("dp", None),
            stacked,
            single,
            stacked,
            single,
            P(),
            stacked,
            stacked,
            single,
            single,
            stacked,
            stacked,
            single,
            single,
            P(),
            P(),
        ),
        out_specs=(
            rows,
            rows,
            stacked,
            stacked,
            stacked,
            stacked,
            single,
            single,
            single,
            single,
            stacked,
            stacked,
            stacked,
            stacked,
            single,
            single,
            single,
            single,
            P(),
            P(),
            P(),
            P(),
        ),
        check_vma=False,
    )
```

```python
import functools
import math

import jax
import jax.numpy as jnp
from jax import lax
from jax.experimental import pallas as pl
from jax.experimental.pallas import tpu as pltpu
from jax.sharding import PartitionSpec as P

D = 1024
HEADS = 16
HD = 64
FF = 2816
BLK = 64
FBLK = 176
ROOTS = 6
OUT_FAN = 8
SPAN = 1024

EPSILON = 1e-05
STEP_RATE = 16.0
GAIN_RATE = 2.0
MASKED = -1e30
F32 = jnp.float32
BF16 = jnp.bfloat16
PAIR = 2 * HD


CHIPS = 4
LANES = 128


def piece_shape(blocked_shape, group_rows, dp_size):
    per_owner, height, width = blocked_shape[-3:]
    column_blocks = dp_size * per_owner // (group_rows // height)
    if per_owner % column_blocks == 0:
        rows, columns = per_owner // column_blocks, column_blocks
    else:
        rows, columns = 1, per_owner
    grid_columns = column_blocks // columns
    return rows, columns, dp_size // grid_columns, grid_columns


def to_piece(blocked, rows, columns):
    leading = blocked.shape[:-3]
    height, width = blocked.shape[-2:]
    grid = blocked.reshape(leading + (rows, columns, height, width))
    return jnp.swapaxes(grid, -3, -2).reshape(leading + (rows * height, columns * width))


def from_piece(piece, rows, columns):
    leading = piece.shape[:-2]
    height, width = piece.shape[-2] // rows, piece.shape[-1] // columns
    grid = piece.reshape(leading + (rows, height, columns, width))
    return jnp.swapaxes(grid, -3, -2).reshape(leading + (rows * columns, height, width))


def rows_of_columns(piece):
    return jnp.swapaxes(piece, -1, -2).reshape(-1, LANES)


def columns_of_rows(rows, members):
    return jnp.swapaxes(rows.reshape(members, -1, LANES), -1, -2)


def rows_of_rows(piece):
    height, width = piece.shape
    return jnp.swapaxes(piece.reshape(height, width // LANES, LANES), 0, 1).reshape(-1, LANES)


def rows_to_rows(rows, blocks):
    grid = jnp.swapaxes(rows.reshape(blocks, -1, LANES), 0, 1)
    return grid.reshape(grid.shape[0], blocks * LANES)


def together(*values):
    return lax.optimization_barrier(values)


def pairwise(values, axis, step):
    return lax.ppermute(values, axis, [(i, i ^ step) for i in range(lax.axis_size(axis))])


def gather_sides(slices):
    return pairwise(slices, "dp", 2), pairwise(slices, "dp", 4), pairwise(slices, "dp", 1)


def gather_corner(across_x, across_y, other):
    half = across_x.shape[0] // 2
    return (
        pairwise(across_y[:half], "dp", 2),
        pairwise(across_x[half:], "dp", 4),
        pairwise(jnp.concatenate([across_x, across_y]), "dp", 1),
    )


def gather_end(slices, across_x, across_y, other, corner_x, corner_y, other_sides):
    corner = jnp.concatenate([corner_x, corner_y])
    return (
        slices, across_x, across_y, corner, other, other_sides, other_sides, pairwise(corner, "dp", 1)
    )


def first_slices(pieces):
    return [0] * 6 + [pieces[6].shape[0] - pieces[0].shape[0], 0]


def add_up(*refs):
    total = refs[0][...].astype(F32)
    for ref in refs[1:]:
        total = total + ref[...].astype(F32)
    return total


def add_call(kernel, slices, in_specs, out_specs, out_shape, name, *operands):
    return pl.pallas_call(
        kernel,
        grid=(slices,),
        in_specs=in_specs,
        out_specs=out_specs,
        out_shape=out_shape,
        cost_estimate=moved(sum(v.size // CHIPS for v in operands)),
        name=name,
    )(*operands)


def chip_slice(chip, rows):
    return pl.BlockSpec((1, 1, rows, LANES), lambda k: (chip, k, 0, 0))


def one_slice(rows, first=0, last=None):
    if last is None:
        return pl.BlockSpec((1, rows, LANES), lambda k: (k, 0, 0))
    return pl.BlockSpec((1, rows, LANES), lambda k: (jnp.clip(k, first, last) - first, 0, 0))


def corner_kernel(half, own, received, to_x, to_y):
    total = add_up(own, received)[0].astype(BF16)

    @pl.when(pl.program_id(0) < half)
    def _():
        to_x[...] = total

    @pl.when(pl.program_id(0) >= half)
    def _():
        to_y[...] = total


def corner_sums(own_core, received):
    slices, rows = own_core.shape[1:3]
    half = slices // 2
    shape = jax.ShapeDtypeStruct((half, rows, LANES), BF16)
    to_x, to_y = add_call(
        functools.partial(corner_kernel, half),
        slices,
        [chip_slice(3, rows)] * 2,
        [one_slice(rows, 0, half - 1), one_slice(rows, half, slices - 1)],
        [shape, shape],
        "add_corner",
        own_core,
        received,
    )
    return to_x, to_y


def send_planar(to_x, to_y):
    return pairwise(to_x, "dp", 2), pairwise(to_y, "dp", 4)


def sides_kernel(half, own_x, received_x, own_y, received_y, corner_x, corner_y, to_x, to_y):
    @pl.when(pl.program_id(0) < half)
    def _():
        to_x[...] = add_up(own_x, received_x)[0].astype(BF16)
        to_y[...] = (add_up(own_y, received_y)[0] + corner_x[...].astype(F32)).astype(BF16)

    @pl.when(pl.program_id(0) >= half)
    def _():
        to_x[...] = (add_up(own_x, received_x)[0] + corner_y[...].astype(F32)).astype(BF16)
        to_y[...] = add_up(own_y, received_y)[0].astype(BF16)


def side_sums(own_core, received, corner_x, corner_y):
    slices, rows = own_core.shape[1:3]
    half = slices // 2
    shape = jax.ShapeDtypeStruct((slices, rows, LANES), BF16)
    to_x, to_y = add_call(
        functools.partial(sides_kernel, half),
        slices,
        [chip_slice(1, rows)] * 2
        + [chip_slice(2, rows)] * 2
        + [one_slice(rows, 0, half - 1), one_slice(rows, half, slices - 1)],
        [one_slice(rows)] * 2,
        [shape, shape],
        "add_sides",
        own_core,
        received,
        own_core,
        received,
        corner_x,
        corner_y,
    )
    return to_x, to_y


def own_kernel(own, received, from_x, from_y, kept, sent):
    total = add_up(own, received)[0] + add_up(from_x, from_y)

    @pl.when(pl.program_id(0) == 0)
    def _():
        kept[...] = total

    @pl.when(pl.program_id(0) == 1)
    def _():
        sent[...] = total.astype(BF16)


def own_sums(own_core, received, from_x, from_y):
    rows = own_core.shape[2]
    kept, sent = add_call(
        own_kernel,
        2,
        [chip_slice(0, rows)] * 2 + [one_slice(rows)] * 2,
        [one_slice(rows, 0, 0)] * 2,
        [jax.ShapeDtypeStruct((1, rows, LANES), F32), jax.ShapeDtypeStruct((1, rows, LANES), BF16)],
        "add_own",
        own_core,
        received,
        from_x,
        from_y,
    )
    return kept[0], sent[0]


def coordinate(fast):
    return lax.axis_index("dp").astype(jnp.int32).reshape(1) if fast else jnp.zeros((1,), jnp.int32)


def gather_all(piece):
    return lax.all_gather(lax.all_gather(piece, "mp"), "dp")


def scatter_all(parts):
    reduced = lax.psum_scatter(parts, "dp", scatter_dimension=0, tiled=False)
    return lax.psum_scatter(reduced, "mp", scatter_dimension=0, tiled=False)


def weight_by_columns(master, dp_size):
    rows, columns, grid_rows, grid_columns = piece_shape(master.shape, D, dp_size)
    gathered = gather_all(to_piece(master.astype(BF16), rows, columns))
    mp, members, height, width = gathered.shape[1:]
    grid = gathered.reshape(grid_rows, grid_columns, mp, members, height, width)
    grid = jnp.transpose(grid, (3, 0, 4, 2, 1, 5))
    return grid.reshape(members, grid_rows * height, mp * grid_columns * width)


def weight_by_rows(master, group_rows, dp_size):
    rows, columns, grid_rows, grid_columns = piece_shape(master.shape, group_rows, dp_size)
    gathered = gather_all(to_piece(master.astype(BF16), rows, columns))
    mp, height, width = gathered.shape[1:]
    grid = gathered.reshape(grid_rows, grid_columns, mp, height, width)
    grid = jnp.transpose(grid, (2, 0, 3, 1, 4))
    return grid.reshape(mp * grid_rows * height, grid_columns * width)


def grad_by_columns(matrix, master, dp_size, mp_size):
    rows, columns, grid_rows, grid_columns = piece_shape(master.shape, D, dp_size)
    members = matrix.shape[0]
    height, width = rows * master.shape[-2], columns * master.shape[-1]
    grid = matrix.reshape(members, grid_rows, height, mp_size, grid_columns, width)
    grid = jnp.transpose(grid, (1, 4, 3, 0, 2, 5))
    parts = grid.reshape(dp_size, mp_size, members, height, width)
    return from_piece(scatter_all(parts).astype(F32), rows, columns)


def grad_by_rows(matrix, master, group_rows, dp_size, mp_size):
    rows, columns, grid_rows, grid_columns = piece_shape(master.shape, group_rows, dp_size)
    height, width = rows * master.shape[-2], columns * master.shape[-1]
    grid = matrix.reshape(mp_size, grid_rows, height, grid_columns, width)
    grid = jnp.transpose(grid, (1, 3, 0, 2, 4))
    parts = grid.reshape(dp_size, mp_size, height, width)
    return from_piece(scatter_all(parts).astype(F32), rows, columns)


def cut_columns(matrices, mp_size):
    members, _, width = matrices.shape
    grid = matrices.reshape(members, CHIPS, 2, LANES, mp_size, width // mp_size)
    return jnp.transpose(grid, (1, 2, 4, 0, 5, 3)).reshape(CHIPS, 2, mp_size, -1, LANES)


def join_columns(pieces, members):
    grid = pieces.reshape(pieces.shape[:3] + (members, -1, LANES))
    return jnp.transpose(grid, (3, 0, 1, 5, 2, 4)).reshape(members, D, -1)


def cut_rows(matrix, mp_size):
    grid = matrix.reshape(mp_size, CHIPS, matrix.shape[0] // (mp_size * CHIPS), 2, D // (2 * LANES), LANES)
    return jnp.transpose(grid, (1, 3, 0, 4, 2, 5)).reshape(CHIPS, 2, mp_size, -1, LANES)


def join_rows(pieces):
    grid = pieces.reshape(pieces.shape[:3] + (D // (2 * LANES), -1, LANES))
    return jnp.transpose(grid, (2, 0, 4, 1, 3, 5)).reshape(-1, D)


def lanes_of(device, relative):
    return pl.ds(pl.multiple_of((device ^ relative) * LANES, LANES), LANES)


def half_lanes(device, core, block):
    start = ((device & 1) ^ core) * (D // 2) + block * LANES
    return pl.ds(pl.multiple_of(start, LANES), LANES)


def rows_at(device, chip, height):
    return pl.ds(pl.multiple_of(((device >> 1) ^ chip) * height, 16), height)


def project_kernel(shard_count, device_ref, *refs):
    shards, refs = refs[:shard_count], refs[shard_count:]
    attend_ref, output_ref, query_ref, key_ref, value_ref, window_ref = refs[2 * CHIPS :]
    device = device_ref[0]
    height = attend_ref.shape[1]
    count = query_ref.shape[0]
    for core in range(2):
        for chip in range(CHIPS):
            piece = refs[core * CHIPS + chip]
            lanes = lanes_of(device, 2 * chip + core)
            for member in range(3):
                attend_ref[member, :, lanes] = piece[0, pl.ds(member * height, height), :]
            rows = rows_at(device, chip, height // CHIPS)
            for block in range(D // (2 * LANES)):
                output_ref[rows, half_lanes(device, core, block)] = piece[
                    0, pl.ds(3 * height + block * (height // CHIPS), height // CHIPS), :
                ]
    columns = pl.ds(pl.multiple_of(pl.program_id(0) * height, LANES), height)
    query_ref[...] = dot_back(shards[-1][...], attend_ref[0]).astype(BF16)
    for i, shard in enumerate(shards):
        rows = pl.ds(i * count, count)
        key_ref[rows, :] = dot_back(shard[...], attend_ref[1]).astype(BF16)
        value_ref[rows, :] = dot_back(shard[...], attend_ref[2]).astype(BF16)
        window_ref[rows, :] = shard[:, columns]


def cut_attend_kernel(device_ref, query, key, value, output, first, second):
    device = device_ref[0]
    height = query.shape[0]
    for core, pieces in enumerate((first, second)):
        for chip in range(CHIPS):
            lanes = lanes_of(device, 2 * chip + core)
            for member, matrix in enumerate((query, key, value)):
                pieces[chip, 0, pl.ds(member * height, height), :] = matrix[:, lanes]
            rows = rows_at(device, chip, height // CHIPS)
            for block in range(D // (2 * LANES)):
                pieces[chip, 0, pl.ds(3 * height + block * (height // CHIPS), height // CHIPS), :] = (
                    output[rows, half_lanes(device, core, block)]
                )


def grid_call(
    kernel, grid, in_specs, out_specs, out_shape, name, scratch=(), cost=None, aliases=None
):
    return pl.pallas_call(
        kernel,
        grid_spec=pltpu.PrefetchScalarGridSpec(
            num_scalar_prefetch=1,
            grid=grid,
            in_specs=in_specs,
            out_specs=out_specs,
            scratch_shapes=scratch,
        ),
        out_shape=out_shape,
        input_output_aliases=aliases or {},
        cost_estimate=cost,
        name=name,
    )


def moved(count):
    return pl.CostEstimate(flops=0, bytes_accessed=2 * count, transcendentals=0)


def project(device, shards, pieces):
    slices = pieces[0].shape[0]
    height = D // slices
    count = shards[0].shape[0]
    rows = count * len(shards)
    piece = lambda first: pl.BlockSpec((1, 4 * height, LANES), lambda k, d: (first + k, 0, 0))
    columns = lambda rows: pl.BlockSpec((rows, height), lambda k, d: (0, k))
    wide = lambda rows: jax.ShapeDtypeStruct((rows, D), BF16)
    return grid_call(
        functools.partial(project_kernel, len(shards)),
        (slices,),
        [pl.BlockSpec((count, D), lambda k, d: (0, 0))] * len(shards)
        + [piece(first) for first in first_slices(pieces)],
        [
            pl.BlockSpec((3, height, D), lambda k, d: (0, k, 0)),
            pl.BlockSpec((height, D), lambda k, d: (k, 0)),
            columns(count),
            columns(rows),
            columns(rows),
            columns(rows),
        ],
        [jax.ShapeDtypeStruct((3, D, D), BF16), wide(D), wide(count), wide(rows), wide(rows), wide(rows)],
        "project",
        cost=pl.CostEstimate(
            flops=2 * D * D * (2 * rows + count), bytes_accessed=16 * D * D, transcendentals=0
        ),
    )(device, *shards, *pieces)


def cut_attend(device, matrices, slices):
    height = matrices[0].shape[0] // slices
    matrix = pl.BlockSpec((height, D), lambda k, d: (k, 0))
    piece = pl.BlockSpec((CHIPS, 1, 4 * height, LANES), lambda k, d: (0, k, 0, 0))
    shape = jax.ShapeDtypeStruct((CHIPS, slices, 4 * height, LANES), BF16)
    return grid_call(
        cut_attend_kernel,
        (slices,),
        [matrix] * 4,
        [piece, piece],
        [shape, shape],
        "cut_attend",
        cost=moved(8 * slices * height * D),
    )(device, *matrices)


def hidden_kernel(
    kept, device_ref, normed_ref, grads_ref, *refs
):
    parts = refs[: 6 * CHIPS]
    result_ref, back_ref, first, second = refs[6 * CHIPS + kept : 6 * CHIPS + kept + 4]
    (
        normed_t, grads_t, w_gate, w_up, w_down, hidden_t, dgate_t, dup_t, moved_ref
    ) = refs[6 * CHIPS + kept + 4 :]
    device = device_ref[0]
    width = w_gate.shape[0]
    height = width // CHIPS
    blocks = D // (2 * LANES)

    @pl.when(pl.program_id(0) == 0)
    def _():
        normed_t[...] = normed_ref[...].T
        grads_t[...] = grads_ref[...].T
        result_ref[...] = jnp.zeros_like(result_ref)
        back_ref[...] = jnp.zeros_like(back_ref)

    for core in range(2):
        for chip in range(CHIPS):
            gate, up, down = parts[3 * (core * CHIPS + chip) : 3 * (core * CHIPS + chip + 1)]
            lanes = lanes_of(device, 2 * chip + core)
            w_gate[:, lanes] = gate[0]
            w_up[:, lanes] = up[0]
            for block in range(blocks):
                w_down[rows_at(device, chip, height), half_lanes(device, core, block)] = down[
                    0, pl.ds(block * height, height), :
                ]

    joint = 2 * height

    for j in range(width // joint):
        start = j * joint
        rows = pl.ds(start, joint)
        gate_pre = jnp.dot(w_gate[rows, :], normed_t[...], preferred_element_type=F32)
        up_pre = jnp.dot(w_up[rows, :], normed_t[...], preferred_element_type=F32)
        grad_hidden = jnp.dot(w_down[rows, :], grads_t[...], preferred_element_type=F32)
        sig = jax.nn.sigmoid(gate_pre)
        silu = gate_pre * sig
        hidden = (silu * up_pre).astype(BF16)
        dup = (grad_hidden * silu).astype(BF16)
        dgate = (grad_hidden * up_pre * sig * (1.0 + gate_pre * (1.0 - sig))).astype(BF16)
        hidden_t[rows, :] = hidden
        dup_t[rows, :] = dup
        dgate_t[rows, :] = dgate

        moved_ref[...] = jnp.dot(hidden, grads_ref[...], preferred_element_type=F32).astype(BF16)
        for part in range(2):
            chip = (device >> 1) ^ (2 * j + part)
            for core, pieces in enumerate((first, second)):
                for block in range(blocks):
                    pieces[chip, 0, pl.ds(2 * width + block * height, height), :] = moved_ref[
                        pl.ds(part * height, height), half_lanes(device, core, block)
                    ]
        for member, values in enumerate((dgate, dup)):
            moved_ref[...] = jnp.dot(values, normed_ref[...], preferred_element_type=F32).astype(BF16)
            target = pl.ds(member * width + start, joint)
            for core, pieces in enumerate((first, second)):
                for chip in range(CHIPS):
                    pieces[chip, 0, target, :] = moved_ref[:, lanes_of(device, 2 * chip + core)]

    result_ref[...] += jnp.dot(hidden_t[...].T, w_down[...], preferred_element_type=F32)
    back_ref[...] += jnp.dot(dgate_t[...].T, w_gate[...], preferred_element_type=F32)
    back_ref[...] += jnp.dot(dup_t[...].T, w_up[...], preferred_element_type=F32)


def hidden_layer(device, normed, grads, pieces, width, start, slices, earlier=()):
    count = normed.shape[0]
    whole = pl.BlockSpec((count, D), lambda k, d: (0, 0))
    piece = lambda first, part: pl.BlockSpec(
        (1, width, LANES), lambda k, d: (first + start + k, part, 0)
    )
    out_piece = pl.BlockSpec((CHIPS, 1, 3 * width, LANES), lambda k, d: (0, start + k, 0, 0))
    shape = jax.ShapeDtypeStruct((CHIPS, pieces[0].shape[0], 3 * width, LANES), BF16)
    total = jax.ShapeDtypeStruct((count, D), F32)
    first_kept = 3 + 6 * CHIPS
    return grid_call(
        functools.partial(hidden_kernel, len(earlier)),
        (slices,),
        [whole, whole]
        + [piece(first, part) for first in first_slices(pieces) for part in range(3)]
        + [pl.BlockSpec(memory_space=pl.ANY)] * len(earlier),
        [whole, whole, out_piece, out_piece],
        [total, total, shape, shape],
        "hidden_layer",
        scratch=[
            pltpu.VMEM((D, count), BF16),
            pltpu.VMEM((D, count), BF16),
            pltpu.VMEM((width, D), BF16),
            pltpu.VMEM((width, D), BF16),
            pltpu.VMEM((width, D), BF16),
            pltpu.VMEM((width, count), BF16),
            pltpu.VMEM((width, count), BF16),
            pltpu.VMEM((width, count), BF16),
            pltpu.VMEM((2 * width // CHIPS, D), BF16),
        ],
        cost=pl.CostEstimate(
            flops=18 * slices * width * D * count,
            bytes_accessed=12 * slices * width * D,
            transcendentals=0,
        ),
        aliases={first_kept + i: 2 + i for i in range(len(earlier))},
    )(device, normed, grads, *[piece for piece in pieces for _ in range(3)], *earlier)


def exchanges():
    axes = ("dp", "mp")
    size = lax.axis_size(axes)
    masks = [1 << bit for bit in range(size.bit_length() - 1)]
    if size == 32:
        masks = [3, 5, 9, 17, 7]
    return [(axes, [(i, i ^ mask) for i in range(size)]) for mask in masks]


def scalar_rows(value):
    row = lax.broadcasted_iota(jnp.int32, (32, LANES), 0)
    rows = jnp.zeros((32, LANES), F32)
    for i in range(3):
        part = lax.reduce_precision(value, 8, 7)
        rows = jnp.where(row == i, part, rows)
        value = value - part
    return rows.astype(BF16)


def neighbours(values, axis, steps):
    return [pairwise(values, axis, step) for step in steps]


def sum_of_four(values, others):
    return (values + others[0]) + (others[1] + others[2])


def hash_rows(hashes):
    digits = jnp.stack([hashes >> 14, (hashes >> 7) & 127, hashes & 127])
    rows = digits.astype(BF16).reshape(-1, LANES)
    return jnp.pad(rows, ((0, -rows.shape[0] % 32), (0, 0)))


def rows_hash(rows, count):
    used = 3 * count // LANES
    digits = rows[..., :used, :].reshape(-1, 3, count).astype(F32)
    return ((digits[:, 0] * 128.0 + digits[:, 1]) * 128.0 + digits[:, 2]).reshape(-1)


def gather_small(values):
    for axis, pairs in exchanges():
        values = jnp.concatenate([values, lax.ppermute(values, axis, pairs)], axis=0)
    return values


def sum_small(values):
    for axis, pairs in exchanges():
        values = values + lax.ppermute(values, axis, pairs)
    return values


def fill_bias(bias_ref, query_labels, key_labels, tile, tile_count, history):
    for t in range(tile_count):
        span = SPAN + tile
        key_pos = lax.broadcasted_iota(jnp.int32, (span, tile), 0) + (history - SPAN + t * tile)
        query_pos = lax.broadcasted_iota(jnp.int32, (span, tile), 1) + (history + t * tile)
        same = key_labels[pl.ds(history - SPAN + t * tile, span), :] == query_labels[:, pl.ds(t * tile, tile)]
        bias_ref[t] = jnp.where(same & (key_pos <= query_pos), 0.0, MASKED)


def head_rows(values, head):
    row = lax.broadcasted_iota(jnp.int32, values.shape, 0)
    return jnp.where((row >= head * HD) & (row < (head + 1) * HD), values, jnp.zeros_like(values))


def head_lanes(values, head):
    lane = lax.broadcasted_iota(jnp.int32, values.shape, 1)
    return jnp.where((lane >= head * HD) & (lane < (head + 1) * HD), values, jnp.zeros_like(values))


def attend_kernel(
    tile, history, query_labels, key_labels, q_ref, k_ref, v_ref, o_ref, lse_ref, bias_ref, vt_ref
):
    tile_count = q_ref.shape[0] // tile
    span = SPAN + tile

    @pl.when(pl.program_id(0) == 0)
    def _():
        fill_bias(bias_ref, query_labels, key_labels, tile, tile_count, history)

    vt_ref[...] = v_ref[...].T
    chunk = math.gcd(span, 256)
    for t in range(tile_count):
        base = history - SPAN + t * tile
        queries = (q_ref[pl.ds(t * tile, tile), :] * HD ** (-0.5)).astype(BF16).T
        outputs = []
        for head in range(2):
            rows = head_rows(queries, head)
            scores, maximum = [], None
            for start in range(0, span, chunk):
                part = (
                    jnp.dot(k_ref[pl.ds(base + start, chunk), :], rows, preferred_element_type=F32)
                    + bias_ref[t, pl.ds(start, chunk), :]
                )
                top = jnp.max(part, axis=0, keepdims=True)
                maximum = top if maximum is None else jnp.maximum(maximum, top)
                scores.append(part)
            total, weighted = 0.0, 0.0
            for i, part in enumerate(scores):
                powers = jnp.exp(part - maximum)
                total = total + jnp.sum(powers, axis=0, keepdims=True)
                weighted = weighted + jnp.dot(
                    vt_ref[pl.ds(head * HD, HD), pl.ds(base + i * chunk, chunk)],
                    powers.astype(BF16),
                    preferred_element_type=F32,
                )
            outputs.append(weighted * (1.0 / total))
            lse_ref[0, pl.ds(head, 1), pl.ds(t * tile, tile)] = maximum + jnp.log(total)
        o_ref[pl.ds(t * tile, tile), :] = jnp.concatenate(outputs, axis=0).T.astype(BF16)


def attend_back_kernel(
    tile, history, query_labels, key_labels, q_ref, k_ref, v_ref, o_ref, do_ref, lse_ref,
    dq_ref, dk_ref, dv_ref, bias_ref, kt_ref, dk_acc, dv_acc,
):
    tile_count = q_ref.shape[0] // tile
    span = SPAN + tile

    @pl.when(pl.program_id(0) == 0)
    def _():
        fill_bias(bias_ref, query_labels, key_labels, tile, tile_count, history)

    kt_ref[...] = k_ref[...].T
    dk_acc[...] = jnp.zeros_like(dk_acc)
    dv_acc[...] = jnp.zeros_like(dv_acc)
    for t in range(tile_count):
        base = history - SPAN + t * tile
        scaled = (q_ref[pl.ds(t * tile, tile), :] * HD ** (-0.5)).astype(BF16)
        grads = do_ref[pl.ds(t * tile, tile), :]
        scaled_t, grads_t = scaled.T, grads.T
        product_t = grads_t.astype(F32) * o_ref[pl.ds(t * tile, tile), :].T.astype(F32)
        keys = k_ref[pl.ds(base, span), :]
        values = v_ref[pl.ds(base, span), :]
        grad_queries = []
        for head in range(2):
            scores = (
                jnp.dot(keys, head_rows(scaled_t, head), preferred_element_type=F32) + bias_ref[t]
            )
            attention = jnp.exp(scores - lse_ref[0, pl.ds(head, 1), pl.ds(t * tile, tile)])
            row_terms = jnp.sum(product_t[head * HD : (head + 1) * HD], axis=0, keepdims=True)
            grad_attention = jnp.dot(values, head_rows(grads_t, head), preferred_element_type=F32)
            grad_scores = (attention * (grad_attention - row_terms)).astype(BF16)
            dv_acc[pl.ds(base, span), :] += jnp.dot(
                attention.astype(BF16), head_lanes(grads, head), preferred_element_type=F32
            )
            dk_acc[pl.ds(base, span), :] += jnp.dot(
                grad_scores, head_lanes(scaled, head), preferred_element_type=F32
            )
            grad_queries.append(
                jnp.dot(
                    kt_ref[pl.ds(head * HD, HD), pl.ds(base, span)],
                    grad_scores,
                    preferred_element_type=F32,
                )
            )
        dq_ref[pl.ds(t * tile, tile), :] = (
            jnp.concatenate(grad_queries, axis=0).T * HD ** (-0.5)
        ).astype(BF16)
    dk_ref[...] = dk_acc[...].astype(BF16)
    dv_ref[...] = dv_acc[...].astype(BF16)


def attention_specs(count, window, start):
    whole = lambda shape: pl.BlockSpec(shape, lambda h: (0,) * len(shape))
    specs = []
    for first in (start, 0):
        own = pl.BlockSpec((count, PAIR), lambda h, first=first: (0, first + h))
        seen = pl.BlockSpec((window, PAIR), lambda h, first=first: (0, first + h))
        specs.append((own, seen))
    sums = pl.BlockSpec((1, 2, count), lambda h: (h, 0, 0))
    labels = [whole((1, count)), whole((window, 1))]
    return labels, specs[0], specs[1], sums


def attend(inputs, tile, start, pairs):
    _, _, queries, keys, _ = inputs
    count, window = queries.shape[0], keys.shape[0]
    labels, (own, seen), (own_out, _), sums = attention_specs(count, window, start)
    work = 2 * count * (SPAN + tile) * PAIR * pairs
    return pl.pallas_call(
        functools.partial(attend_kernel, tile, window - count),
        grid=(pairs,),
        in_specs=labels + [own, seen, seen],
        out_specs=[own_out, sums],
        out_shape=[
            jax.ShapeDtypeStruct((count, pairs * PAIR), BF16),
            jax.ShapeDtypeStruct((pairs, 2, count), F32),
        ],
        scratch_shapes=[
            pltpu.VMEM((count // tile, SPAN + tile, tile), F32),
            pltpu.VMEM((PAIR, window), BF16),
        ],
        cost_estimate=pl.CostEstimate(
            flops=4 * work, bytes_accessed=4 * (window + count) * PAIR * pairs, transcendentals=0
        ),
        name="attend",
    )(*inputs)


def attend_back(inputs, context, grads, log_sums, tile, start, pairs):
    _, _, queries, keys, _ = inputs
    count, window = queries.shape[0], keys.shape[0]
    labels, (own, seen), (own_out, seen_out), sums = attention_specs(count, window, start)
    work = 2 * count * (SPAN + tile) * PAIR * pairs
    return pl.pallas_call(
        functools.partial(attend_back_kernel, tile, window - count),
        grid=(pairs,),
        in_specs=labels + [own, seen, seen, own_out, own, sums],
        out_specs=[own_out, seen_out, seen_out],
        out_shape=[
            jax.ShapeDtypeStruct((count, pairs * PAIR), BF16),
            jax.ShapeDtypeStruct((window, pairs * PAIR), BF16),
            jax.ShapeDtypeStruct((window, pairs * PAIR), BF16),
        ],
        scratch_shapes=[
            pltpu.VMEM((count // tile, SPAN + tile, tile), F32),
            pltpu.VMEM((PAIR, window), BF16),
            pltpu.VMEM((window, PAIR), F32),
            pltpu.VMEM((window, PAIR), F32),
        ],
        cost_estimate=pl.CostEstimate(
            flops=10 * work, bytes_accessed=8 * (window + count) * PAIR * pairs, transcendentals=0
        ),
        name="attend_back",
    )(*inputs, context, grads, log_sums)


def project_back_kernel(per_shard, *refs):
    queries, keys, values = refs[0:2], refs[2:4], refs[4:6]
    weights, normed = refs[6:8]
    back_refs, gain_ref, total = refs[8:-2], refs[-2], refs[-1]
    half = queries[0].shape[1]
    shard = lax.div(pl.program_id(0), per_shard)
    back = None
    for member, parts in ((1, keys), (2, values)):
        for i, part in enumerate(parts):
            term = mxu(part[...], weights[member, pl.ds(i * half, half), :])
            back = term if back is None else back + term
    total[...] = back

    @pl.when(shard == len(back_refs) - 1)
    def _():
        total[...] += mxu(queries[0][...], weights[0, pl.ds(0, half), :]) + mxu(
            queries[1][...], weights[0, pl.ds(half, half), :]
        )

    for i, ref in enumerate(back_refs):

        @pl.when(shard == i)
        def _(ref=ref):
            ref[...] = total[...].astype(ref.dtype)

    @pl.when(pl.program_id(0) == 0)
    def _():
        gain_ref[...] = jnp.zeros_like(gain_ref)

    gain_ref[...] += jnp.sum(total[...] * normed[...].astype(F32), axis=0, keepdims=True)


def project_back(first, second, weights, window):
    count, half = first[0].shape
    rows = window.shape[0]
    shards = rows // count
    tile = min(256, count)
    per_shard = count // tile
    shard_spec = lambda width, shard: pl.BlockSpec(
        (tile, width), lambda i: (jnp.clip(i - shard * per_shard, 0, per_shard - 1), 0)
    )
    own = shard_spec(half, shards - 1)
    seen = pl.BlockSpec((tile, half), lambda i: (i, 0))
    wide = pl.BlockSpec((tile, D), lambda i: (i, 0))
    shapes = [
        jax.ShapeDtypeStruct((count, D), BF16 if shard == 0 and shards > 1 else F32)
        for shard in range(shards)
    ]
    outs = pl.pallas_call(
        functools.partial(project_back_kernel, per_shard),
        grid=(rows // tile,),
        in_specs=[own, own, seen, seen, seen, seen, pl.BlockSpec((3, D, D), lambda i: (0, 0, 0)), wide],
        out_specs=[shard_spec(D, shard) for shard in range(shards)]
        + [pl.BlockSpec((1, D), lambda i: (0, 0))],
        out_shape=shapes + [jax.ShapeDtypeStruct((1, D), F32)],
        scratch_shapes=[pltpu.VMEM((tile, D), F32)],
        cost_estimate=pl.CostEstimate(
            flops=2 * D * D * (2 * rows + count), bytes_accessed=12 * rows * D, transcendentals=0
        ),
        name="project_back",
    )(first[0], second[0], first[1], second[1], first[2], second[2], weights, window)
    return outs[:-1], outs[-1]


def split(values):
    high = values.astype(BF16)
    return high, (values - high.astype(F32)).astype(BF16)


def dot_split(first, second, contract):
    dims = ((contract, contract), ((), ()))
    (a, b), (c, d) = split(first), split(second)
    multiply = lambda x, y: lax.dot_general(x, y, dims, preferred_element_type=F32)
    return multiply(a, c) + multiply(b, c) + multiply(a, d)


def total_of(values):
    return jnp.sum(jnp.sum(values, axis=0, keepdims=True), axis=1, keepdims=True)


def mxu(first, second):
    return jnp.dot(first, second, preferred_element_type=F32)


class Chain:
    def __init__(self, matrix, rows, spread):
        self.matrix, self.rows, self.spread = matrix, rows, spread

    def square(self):
        self.low = self.matrix.astype(BF16)
        height = self.rows.shape[0]
        stacked = jnp.concatenate([self.rows.astype(BF16), self.low], axis=0)
        both = mxu(stacked, self.spread(self.low))
        self.rows = 1.25 * self.rows - 0.25 * both[:height]
        self.rest = (0.0625 * both[height:] - 0.625 * self.low.astype(F32)).astype(BF16)

    def half(self):
        self.right = self.spread(self.rest)
        self.matrix = 1.5625 * self.matrix + mxu(self.low, self.right)

    def whole(self):
        self.matrix = 1.5625 * self.matrix + mxu(self.matrix.astype(BF16), self.right)

    def last(self):
        self.rows = 1.25 * self.rows - 0.25 * mxu(
            self.rows.astype(BF16), self.spread(self.matrix.astype(BF16))
        )


def run_chains(chains):
    for _ in range(ROOTS - 1):
        for chain in chains:
            chain.square()
        for chain in chains:
            chain.half()
        for chain in chains:
            chain.whole()
    for chain in chains:
        chain.last()


def quarter(norm):
    return lax.rsqrt(jnp.sqrt(norm))


def shampoo_blocks(step_size, pack, grads, shorts_old, longs_old, short_out, long_out):
    blocks = len(grads)
    short, width = grads[0].shape
    side = pack * short
    row = lax.broadcasted_iota(jnp.int32, (side, side), 0)
    lane = lax.broadcasted_iota(jnp.int32, (side, side), 1)
    mask = jnp.where(lax.div(row, short) == lax.div(lane, short), 1.0, 0.0).astype(BF16)
    eye = jnp.where(
        lax.broadcasted_iota(jnp.int32, (short, side), 0)
        == lax.rem(lax.broadcasted_iota(jnp.int32, (short, side), 1), short),
        1.0,
        0.0,
    )
    spread = lambda values: jnp.concatenate([values] * pack, axis=0) * mask
    beside = lambda values: jnp.concatenate(values, axis=1)
    alone = lambda values: values
    packed_long = width == short

    shorts, longs, scales = [], [], []
    for b, grad in enumerate(grads):
        short_new = 0.5 * shorts_old(b) + 0.5 * dot_split(grad, grad, (1,))
        grad_t = grad.T
        long_new = 0.5 * longs_old(b) + 0.5 * dot_split(grad_t, grad_t, (1,))
        short_out(b, short_new)
        long_out(b, long_new)
        short_norm = jnp.sqrt(total_of(short_new * short_new) + 1e-06)
        long_norm = jnp.sqrt(total_of(long_new * long_new) + 1e-06)
        shorts.append(short_new / short_norm)
        longs.append(long_new / long_norm)
        scales.append(step_size * quarter(short_norm) * quarter(long_norm))
    groups = [range(i, i + pack) for i in range(0, blocks, pack)]
    left = [Chain(beside([shorts[b] for b in g]), eye, spread) for g in groups]
    if packed_long:
        right = [
            Chain(beside([longs[b] for b in g]), beside([grads[b] for b in g]), spread) for g in groups
        ]
    else:
        right = [Chain(longs[b], grads[b], alone) for b in range(blocks)]
    run_chains(left + right)
    steps = []
    for i, g in enumerate(groups):
        high, low = split(left[i].rows)
        if packed_long:
            second, second_low = split(right[i].rows)
            second, second_low = spread(second), spread(second_low)
            total = mxu(high, second) + mxu(low, second) + mxu(high, second_low)
            parts = [total[:, j * short : (j + 1) * short] for j in range(pack)]
        else:
            second, second_low = split(jnp.concatenate([right[b].rows for b in g], axis=0))
            high, low = spread(high), spread(low)
            total = mxu(high, second) + mxu(low, second) + mxu(high, second_low)
            parts = [total[j * short : (j + 1) * short] for j in range(pack)]
        steps += [scales[b] * part for b, part in zip(g, parts)]
    return steps


def put(ref, lead=()):
    def store(b, values):
        ref[lead + (b,)] = values

    return store


def shampoo_kernel(
    step_size, pack, grad_ref, master_ref, short_ref, long_ref, weight_ref, short_out, long_out
):
    blocks = grad_ref.shape[0]
    steps = shampoo_blocks(
        step_size,
        pack,
        [grad_ref[b] for b in range(blocks)],
        lambda b: short_ref[b],
        lambda b: long_ref[b],
        put(short_out),
        put(long_out),
    )
    for b, step in enumerate(steps):
        weight_ref[b] = master_ref[b] - step


def shampoo_rows_kernel(
    step_size, turned, across, kept, scale_ref, own, one, two, master_ref, short_ref, long_ref, *refs
):
    grad_ref, weight_ref, short_out, long_out = refs[kept:]
    rows = own[0] + one[...].astype(F32) + two[...].astype(F32)
    rows = rows * scale_ref[0]
    groups = 4
    height = rows.shape[0] // groups
    grads = [None] * (2 * groups)
    for group in range(groups):
        slab = rows[group * height : (group + 1) * height]
        tall = slab.T if turned else None
        for half in range(2):
            b = half * groups + group if across else 2 * group + half
            lanes = slice(half * BLK, (half + 1) * BLK)
            grads[b] = tall[lanes] if turned else slab[:, lanes]
            grad_ref[0, b] = grads[b]
    steps = shampoo_blocks(
        step_size,
        4,
        grads,
        lambda b: short_ref[0, b],
        lambda b: long_ref[0, b],
        put(short_out, (0,)),
        put(long_out, (0,)),
    )
    for b, step in enumerate(steps):
        weight_ref[0, b] = master_ref[0, b] - step


def shampoo_rows(
    terms, scale, master, short_old, long_old, step_size, first, turned, across, start=0, stop=None, earlier=()
):
    members, blocks, height, width = master.shape
    stop = members if stop is None else stop
    short, long = short_old.shape[-1], long_old.shape[-1]
    rows = blocks // 2 * long
    spec = lambda *shape: pl.BlockSpec((1, blocks) + shape, lambda i: (start + i, 0, 0, 0))
    shape = lambda *dims: jax.ShapeDtypeStruct((members, blocks) + dims, F32)
    term = pl.BlockSpec((rows, LANES), lambda i: (first + start + i, 0))
    own = pl.BlockSpec((1, rows, LANES), lambda i: (0, first + start + i, 0))
    return pl.pallas_call(
        functools.partial(shampoo_rows_kernel, step_size, turned, across, len(earlier)),
        grid=(stop - start,),
        in_specs=[
            pl.BlockSpec(memory_space=pltpu.SMEM),
            own,
            term,
            term,
            spec(height, width),
            spec(short, short),
            spec(long, long),
        ]
        + [pl.BlockSpec(memory_space=pl.ANY)] * len(earlier),
        out_specs=[spec(height, width), spec(height, width), spec(short, short), spec(long, long)],
        out_shape=[shape(height, width), shape(height, width), shape(short, short), shape(long, long)],
        input_output_aliases={7 + i: i for i in range(len(earlier))},
        cost_estimate=pl.CostEstimate(
            flops=160 * (stop - start) * blocks * long * long * long,
            bytes_accessed=8 * (stop - start) * blocks * (long * long + short * short + 2 * short * long),
            transcendentals=0,
        ),
        name="shampoo_rows",
    )(scale.reshape(1), terms[0][None], terms[1], terms[2], master, short_old, long_old, *earlier)


def shampoo(gradient, master, short_old, long_old, step_size, blocks):
    count, short, width = gradient.shape
    blocks = min(blocks, count)
    pack = min(4, blocks)
    spec = lambda *shape: pl.BlockSpec((blocks,) + shape, lambda i: (i, 0, 0))
    specs = [spec(short, width), spec(short, short), spec(width, width)]
    shape = lambda *dims: jax.ShapeDtypeStruct((count,) + dims, F32)
    return pl.pallas_call(
        functools.partial(shampoo_kernel, step_size, pack),
        grid=(count // blocks,),
        in_specs=specs[:1] + specs,
        out_specs=specs,
        out_shape=[shape(short, width), shape(short, short), shape(width, width)],
        cost_estimate=pl.CostEstimate(
            flops=40 * count * width * width * width,
            bytes_accessed=8 * count * (width * width + short * short + 2 * short * width),
            transcendentals=0,
        ),
        name="shampoo",
    )(gradient, master, short_old, long_old)
def step_rows(gradient, master, left, right, step_size, blocks):
    flat = lambda values: values.reshape((-1,) + values.shape[-2:])
    outs = shampoo(flat(gradient), flat(master), flat(left), flat(right), step_size, blocks)
    return tuple(v.reshape(gradient.shape[:-2] + v.shape[-2:]) for v in outs)


def turn(values):
    return jnp.swapaxes(values, -1, -2)


def step_columns(gradient, master, left, right, step_size, blocks):
    weight, right, left = shampoo(turn(gradient), turn(master), right, left, step_size, blocks)
    return turn(weight), left, right


def two_by_two(first, second):
    (a, b), (c, d) = first
    (e, f), (g, h) = second
    return ((a * e + b * g, a * f + b * h), (c * e + d * g, c * f + d * h))


def quarter_root_pair(statistic):
    frobenius = jnp.sqrt(sum(v * v for row in statistic for v in row) + 1e-06)
    matrix = tuple(tuple(v / frobenius for v in row) for row in statistic)
    estimate = ((1.0, 0.0), (0.0, 1.0))
    for iteration in range(ROOTS):
        (a, b), (c, d) = matrix
        update = (((5.0 - a) * 0.25, -b * 0.25), (-c * 0.25, (5.0 - d) * 0.25))
        estimate = two_by_two(estimate, update)
        squared = two_by_two(update, update)
        matrix = two_by_two(two_by_two(squared, squared), matrix)
    scale = lax.rsqrt(jnp.sqrt(frobenius))
    return tuple(tuple(v * scale for v in row) for row in estimate)


def gain_kernel(grad_ref, gain_ref, left_ref, right_ref, weight_ref, left_out, right_out):
    grads = [grad_ref[pl.ds(i, 1), :] for i in range(2)]
    inner = lambda i, j: jnp.sum(grads[i] * grads[j], axis=1, keepdims=True)
    products = ((inner(0, 0), inner(0, 1)), (inner(1, 0), inner(1, 1)))
    left = tuple(
        tuple(
            0.5 * left_ref[pl.ds(i, 1), pl.ds(j, 1)] + 0.5 * products[i][j] for j in range(2)
        )
        for i in range(2)
    )
    left_out[...] = jnp.concatenate([jnp.concatenate(row, axis=1) for row in left], axis=0)
    right = 0.5 * right_ref[...] + 0.5 * (grads[0] * grads[0] + grads[1] * grads[1])
    right_out[...] = right
    root = quarter_root_pair(left)
    scale = GAIN_RATE * lax.rsqrt(jnp.sqrt(right))
    for i in range(2):
        mixed = root[i][0] * grads[0] + root[i][1] * grads[1]
        weight_ref[pl.ds(i, 1), :] = gain_ref[pl.ds(i, 1), :] - scale * mixed


def gain_update(gradient, gain_rows, left_old, right_old):
    shapes = [gain_rows.shape, left_old.shape, (1, right_old.size)]
    weight, left_new, right_new = pl.pallas_call(
        gain_kernel,
        out_shape=[jax.ShapeDtypeStruct(shape, F32) for shape in shapes],
        name="gain_update",
    )(gradient, gain_rows, left_old, right_old.reshape(1, -1))
    return weight, left_new, right_new.reshape(-1)


def dot(first, second):
    return jnp.dot(first, second, preferred_element_type=F32)


def dot_back(first, second):
    return lax.dot_general(first, second, (((1,), (1,)), ((), ())), preferred_element_type=F32)


def dot_weight(first, second):
    return lax.dot_general(first, second, (((0,), (0,)), ((), ())), preferred_element_type=F32)


def body(
    patches,
    cotangent,
    lengths,
    hashes,
    segments,
    attend_master,
    output_master,
    expand_master,
    reduce_master,
    gains,
    attend_left,
    attend_right,
    output_left,
    output_right,
    expand_left,
    expand_right,
    reduce_left,
    reduce_right,
    gains_left,
    gains_right,
):
    dp_size, mp_size = lax.axis_size("dp"), lax.axis_size("mp")
    mp_index = lax.axis_index("mp")
    count = patches.shape[0]
    head_width, hidden_width = D // mp_size, FF // mp_size
    head_rows_width = head_width // CHIPS
    total_patches = count * dp_size * mp_size
    earlier = -(-(SPAN - 1) // count)
    history = earlier * count
    tile = min(256, count)
    fast = dp_size == 2 * CHIPS and mp_size == 4
    device = coordinate(fast)
    grids = {
        name: piece_shape(master.shape, rows, dp_size)
        for name, master, rows in (
            ("attend", attend_master, D),
            ("output", output_master, head_width),
            ("expand", expand_master, D),
            ("reduce", reduce_master, hidden_width),
        )
    }

    stream = patches.astype(F32)
    first_rms = lax.rsqrt(jnp.mean(stream * stream, axis=1, keepdims=True) + EPSILON)
    first_hat = stream * first_rms
    first_normed = (first_hat * gains[0]).astype(BF16)

    row_labels = segments.reshape(-1)
    padded = jnp.concatenate([jnp.full((history,), -1, jnp.int32), row_labels])
    key_labels = lax.dynamic_slice_in_dim(padded, mp_index * count, history + count, 0)
    query_labels = key_labels[history:].reshape(1, count)
    key_labels = key_labels.reshape(-1, 1)
    up_one = [(i, i + 1) for i in range(mp_size - 1)]
    down_one = [(i + 1, i) for i in range(mp_size - 1)]
    half_pairs = HEADS * HD // PAIR // 2

    def count_own(all_hashes):
        own = hashes.astype(F32)
        return jnp.sum((own[:, None] == all_hashes[None, :]).astype(F32), axis=1)

    def halo(values):
        return lax.ppermute(values, "mp", up_one)

    if fast:
        attend_rows = jnp.concatenate(
            [
                rows_of_columns(to_piece(attend_master.astype(BF16), *grids["attend"][:2])),
                rows_of_rows(to_piece(output_master.astype(BF16), *grids["output"][:2])),
                hash_rows(hashes),
            ]
        )
        slice_two = pairwise(attend_rows, "mp", 2)
        slice_one = pairwise(attend_rows, "mp", 1)
        halo_source, slice_two = together(first_normed, slice_two)
        slice_three = pairwise(slice_two, "mp", 1)
        near_halo = halo(halo_source)
        attend_slices = jnp.stack([attend_rows, slice_one, slice_two, slice_three])
        sides = gather_sides(attend_slices)
        near_halo, sides = together(near_halo, sides)
        corners = gather_corner(*sides)
        shards = [near_halo, first_normed]
        for _ in range(earlier - 1):
            shards.insert(0, halo(shards[0]))
        shards[0], corners = together(shards[0], corners)
        attend_pieces = gather_end(attend_slices, *sides, *corners)
        all_hashes = jnp.concatenate(
            [rows_hash(piece[:, 4 * head_width :], count) for i, piece in enumerate(attend_pieces) if i != 6]
        )
    else:
        attend_cut = jnp.concatenate(
            [
                cut_columns(weight_by_columns(attend_master, dp_size), mp_size),
                cut_rows(weight_by_rows(output_master, head_width, dp_size), mp_size),
            ],
            axis=3,
        )
        attend_pieces = [attend_cut[chip, core] for core in range(2) for chip in range(CHIPS)]
        hidden_cut = jnp.concatenate(
            [
                cut_columns(weight_by_columns(expand_master, dp_size), mp_size),
                cut_rows(weight_by_rows(reduce_master, hidden_width, dp_size), mp_size),
            ],
            axis=3,
        )
        near_pieces, far_pieces = (
            [hidden_cut[chip, core, k : k + 2] for core in range(2) for chip in range(CHIPS)]
            for k in (0, 2)
        )
        shards = [first_normed]
        for _ in range(earlier):
            shards.insert(0, halo(shards[0]))
        all_hashes = gather_small(hashes).astype(F32)

    raw_weight = lengths.astype(F32) * lax.rsqrt(count_own(all_hashes))
    raw_total = jnp.sum(raw_weight.reshape(-1, LANES), axis=0, keepdims=True)
    grad_out = cotangent.astype(F32) * raw_weight[:, None]
    grad_low = grad_out.astype(BF16)

    if fast:
        hidden_rows = jnp.concatenate(
            [
                rows_of_columns(to_piece(expand_master.astype(BF16), *grids["expand"][:2])),
                rows_of_rows(to_piece(reduce_master.astype(BF16), *grids["reduce"][:2])),
            ]
        )
        shards[0], hidden_rows = together(shards[0], hidden_rows)
        slice_one = pairwise(hidden_rows, "mp", 1)
    attend_w, output_w, queries, keys, values, window = project(device, shards, attend_pieces)
    labels = (query_labels, key_labels)
    if fast:
        queries, slice_one, late_rows = together(queries, slice_one, hidden_rows)
        slice_two = pairwise(late_rows, "mp", 2)
        near = jnp.stack([hidden_rows, slice_one])
        sides = gather_sides(near)
    inputs = labels + (queries, keys, values)
    context_a, sums_a = attend(inputs, tile, 0, half_pairs)
    if fast:
        queries, context_a, sides, slice_two, grad_low, raw_total = together(
            queries, context_a, sides, slice_two, grad_low, raw_total
        )
        inputs = labels + (queries, keys, values)
        corners = gather_corner(*sides)
        slice_three = pairwise(slice_two, "mp", 1)
    context_b, sums_b = attend(inputs, tile, half_pairs, half_pairs)
    if fast:
        context_b, corners, slice_three = together(context_b, corners, slice_three)
        near_pieces = gather_end(near, *sides, *corners)
        total_rows = scalar_rows(raw_total)
        far = jnp.concatenate(
            [jnp.stack([slice_two, slice_three]), jnp.stack([total_rows, total_rows])], axis=1
        )
        sides = gather_sides(far)
    half = context_a.shape[1]
    middle = stream + dot(context_a, output_w[:half]) + dot(context_b, output_w[half:])

    second_rms = lax.rsqrt(jnp.mean(middle * middle, axis=1, keepdims=True) + EPSILON)
    second_hat = middle * second_rms
    second_normed = (second_hat * gains[1]).astype(BF16)
    if fast:
        second_normed, near_pieces = together(second_normed, near_pieces)
        share_a = hidden_layer(device, second_normed, grad_low, near_pieces, hidden_width, 0, 2)
        share_a, sides = together(share_a, sides)
        corners = gather_corner(*sides)
        far_pieces = gather_end(far, *sides, *corners)
        share_b = share_a
        near_grads = share_b[2:]
        near_received = pairwise(near_grads[1], "dp", 1)
        share_c = hidden_layer(device, second_normed, grad_low, far_pieces, hidden_width, 0, 2)
        totals = [
            piece[first, 3 * hidden_width : 3 * hidden_width + 8].astype(F32)
            for piece, first in zip(far_pieces, first_slices(far_pieces))
        ]
        totals = [totals[chip] + totals[CHIPS + chip] for chip in range(CHIPS)]
        totals = (totals[0] + totals[1]) + (totals[2] + totals[3])
        raw_total = (totals[2:3] + totals[1:2]) + totals[0:1]
        share_c, near_received, raw_total = together(share_c, near_received, raw_total)
        along = neighbours(raw_total, "mp", (1, 2, 3))
        far_grads = share_c[2:]
        far_received = pairwise(far_grads[1], "dp", 1)
        near_corners = send_planar(*corner_sums(near_grads[0], near_received))
        second_back = share_a[1] + share_c[1]
        results = (middle, share_a[0], share_c[0])
    else:
        share_a = hidden_layer(device, second_normed, grad_low, near_pieces, hidden_width, 0, 2)
        share_c = hidden_layer(device, second_normed, grad_low, far_pieces, hidden_width, 0, 2)
        near_grads, far_grads = share_a[2:], share_c[2:]
        raw_total = sum_small(raw_total)
        second_back = share_a[1] + share_c[1]
        activations = (middle + share_a[0] + share_c[0]).astype(BF16)


    second_scaled = second_back * gains[1]
    gain_second = jnp.sum(second_back * second_hat, axis=0)
    middle_grad = grad_out + second_rms * (
        second_scaled - second_hat * jnp.mean(second_scaled * second_hat, axis=1, keepdims=True)
    )
    middle_low = middle_grad.astype(BF16)
    grad_context = dot_back(middle_low, output_w).astype(BF16)

    def key_grads(parts):
        return dot_weight(parts[1], window).astype(BF16)

    def weight_grads(context_part, parts, keys_part):
        return [
            dot_weight(parts[0], first_normed).astype(BF16),
            keys_part,
            dot_weight(parts[2], window).astype(BF16),
            dot_weight(context_part, middle_low).astype(BF16),
        ]

    slices_half = mp_size // 2
    if fast:
        grad_context, near_corners, along = together(grad_context, near_corners, along)
        raw_total = sum_of_four(raw_total, along)
        near_sides = side_sums(near_grads[0], near_received, *near_corners)
        grad_context, near_sides = together(grad_context, near_sides)
        near_sides = send_planar(*near_sides)
    weight_scale = total_patches / jnp.sum(raw_total)
    grad_scale = weight_scale * total_patches ** (-0.5)
    backs_a = attend_back(inputs, context_a, grad_context, sums_a, tile, 0, half_pairs)
    keys_a = key_grads(backs_a)
    if fast:
        backs_a, keys_a, near_sides, far_received = together(backs_a, keys_a, near_sides, far_received)
        far_corners = corner_sums(far_grads[0], far_received)
        near_own, near_one = own_sums(near_grads[0], near_received, *near_sides)
        backs_a, far_corners, near_one = together(backs_a, far_corners, near_one)
        far_corners = send_planar(*far_corners)
        near_one = pairwise(near_one, "mp", 1)
    cut_a = cut_attend(device, weight_grads(context_a, backs_a, keys_a), slices_half)
    if fast:
        cut_a, grad_context, far_corners = together(cut_a, grad_context, far_corners)
        far_sides = side_sums(far_grads[0], far_received, *far_corners)
        cut_a, grad_context, far_sides = together(cut_a, grad_context, far_sides)
        far_sides = send_planar(*far_sides)
        received_a = pairwise(cut_a[1], "dp", 1)
    backs_b = attend_back(inputs, context_b, grad_context, sums_b, tile, half_pairs, half_pairs)
    keys_b = key_grads(backs_b)
    if fast:
        backs_b, keys_b, far_sides, received_a, near_one = together(
            backs_b, keys_b, far_sides, received_a, near_one
        )
        far_own, far_three = own_sums(far_grads[0], far_received, *far_sides)
        corners_a = corner_sums(cut_a[0], received_a)
        backs_b, far_three, corners_a = together(backs_b, far_three, corners_a)
        far_three = pairwise(far_three, "mp", 1)
        corners_a = send_planar(*corners_a)
    cut_b = cut_attend(device, weight_grads(context_b, backs_b, keys_b), slices_half)
    if fast:
        backs_b, cut_b, corners_a, far_three = together(backs_b, cut_b, corners_a, far_three)
        sides_a = side_sums(cut_a[0], received_a, *corners_a)
        far_two = (far_own + far_three.astype(F32)).astype(BF16)
        backs_b, cut_b, sides_a, far_two, results = together(backs_b, cut_b, sides_a, far_two, results)
        activations = (results[0] + results[1] + results[2]).astype(BF16)
        sides_a = send_planar(*sides_a)
        far_two = pairwise(far_two, "mp", 2)
        received_b = pairwise(cut_b[1], "dp", 1)
    shares, gain_first = project_back(backs_a, backs_b, attend_w, window)
    gain_sums = jnp.stack([gain_first[0] / gains[0], gain_second])

    def halo_back(share):
        return lax.ppermute(share.astype(BF16), "mp", down_one)

    def first_grad(carried):
        first_back = shares[-1] + carried.astype(F32)
        first_scaled = first_back * gains[0]
        return weight_scale * (
            middle_grad
            + first_rms
            * (first_scaled - first_hat * jnp.mean(first_scaled * first_hat, axis=1, keepdims=True))
        )

    if fast:
        shares, received_b, sides_a, far_two, activations = together(
            shares, received_b, sides_a, far_two, activations
        )
        corners_b = corner_sums(cut_b[0], received_b)
        own_a, one_a = own_sums(cut_a[0], received_a, *sides_a)
        shares, corners_b, one_a, far_two = together(shares, corners_b, one_a, far_two)
        corners_b = send_planar(*corners_b)
        carried = halo_back(shares[0])
        one_a = pairwise(one_a, "mp", 1)
    else:
        carried = halo_back(shares[0])
        for share in shares[1:-1]:
            carried = halo_back(share + carried.astype(F32))
        gain_sums = sum_small(gain_sums)
        input_grad = first_grad(carried)
    reduce_step, output_step = STEP_RATE * FF ** (-0.5), STEP_RATE * OUT_FAN ** (-0.5)
    expand_step = attend_step = STEP_RATE * D ** (-0.5)
    if fast:
        far_two, corners_b = together(far_two, corners_b)
        sides_b = side_sums(cut_b[0], received_b, *corners_b)
        far_two, sides_b = together(far_two, sides_b)
        sides_b = send_planar(*sides_b)
        terms = (near_own, near_one, far_two)
        reduce_out = shampoo_rows(
            terms, grad_scale, turn(reduce_master)[None], reduce_right[None], reduce_left[None],
            reduce_step, 2, True, False,
        )
        reduce_out, terms, sides_b, carried, gain_sums = together(
            reduce_out, terms, sides_b, carried, gain_sums
        )
        own_b, three_b = own_sums(cut_b[0], received_b, *sides_b)
        carried = [(share + carried.astype(F32)).astype(BF16) for share in shares[1:-1]]
        terms, three_b, carried, gain_sums = together(terms, three_b, carried, gain_sums)
        three_b = pairwise(three_b, "mp", 1)
        carried = halo_back(carried[0])
        planar = neighbours(gain_sums, "dp", (2, 4, 6))
        expand_inputs = (grad_scale, expand_master, expand_left, expand_right, expand_step, 0, True, True)
        expand_out = shampoo_rows(terms, *expand_inputs, 0, 1)
        expand_out, terms, three_b, planar = together(expand_out, terms, three_b, planar)
        gain_sums = sum_of_four(gain_sums, planar)
        two_b = (own_b + three_b.astype(F32)).astype(BF16)
        terms, two_b, gain_sums = together(terms, two_b, gain_sums)
        two_b = pairwise(two_b, "mp", 2)
        moved = pairwise(gain_sums, "dp", 1)
        expand_out = shampoo_rows(terms, *expand_inputs, 1, 2, expand_out)
        input_grad = first_grad(carried)
        expand_out, two_b, one_a, input_grad, moved = together(
            expand_out, two_b, one_a, input_grad, moved
        )
        gain_sums = gain_sums + moved
        along = neighbours(gain_sums, "mp", (1, 2, 3))
        terms = (own_a, one_a, two_b)
        attend_out = shampoo_rows(
            terms, grad_scale, attend_master, attend_left, attend_right, attend_step, 0, True, True
        )
        attend_out, terms, along = together(attend_out, terms, along)
        gain_sums = sum_of_four(gain_sums, along)
        output_out = shampoo_rows(
            terms, grad_scale, output_master[None], output_left[None], output_right[None], output_step,
            3, False, False,
        )
        alone = lambda outs: [v[0] for v in outs]
        reduce_grad, reduce_weight, right_reduce, left_reduce = alone(reduce_out)
        reduce_grad, reduce_weight = turn(reduce_grad), turn(reduce_weight)
        expand_grad, expand_weight, left_expand, right_expand = expand_out
        attend_grad, attend_weight, left_attend, right_attend = attend_out
        output_grad, output_weight, left_output, right_output = alone(output_out)
    else:
        hidden_cut = jnp.stack(
            [jnp.concatenate([near_grads[core], far_grads[core]], axis=1) for core in range(2)], axis=1
        )
        attend_cut = jnp.stack(
            [jnp.concatenate([cut_a[core], cut_b[core]], axis=1) for core in range(2)], axis=1
        )
        expand_grad = grad_scale * grad_by_columns(
            join_columns(hidden_cut[:, :, :, : 2 * hidden_width], 2), expand_master, dp_size, mp_size
        )
        reduce_grad = grad_scale * grad_by_rows(
            join_rows(hidden_cut[:, :, :, 2 * hidden_width :]),
            reduce_master,
            hidden_width,
            dp_size,
            mp_size,
        )
        output_grad = grad_scale * grad_by_rows(
            join_rows(attend_cut[:, :, :, 3 * head_width :]), output_master, head_width, dp_size, mp_size
        )
        attend_grad = grad_scale * grad_by_columns(
            join_columns(attend_cut[:, :, :, : 3 * head_width], 3), attend_master, dp_size, mp_size
        )
        reduce_weight, left_reduce, right_reduce = step_columns(
            reduce_grad, reduce_master, reduce_left, reduce_right, reduce_step, 4
        )
        expand_weight, left_expand, right_expand = step_rows(
            expand_grad, expand_master, expand_left, expand_right, expand_step, 8
        )
        output_weight, left_output, right_output = step_rows(
            output_grad, output_master, output_left, output_right, output_step, 8
        )
        attend_weight, left_attend, right_attend = step_rows(
            attend_grad, attend_master, attend_left, attend_right, attend_step, 8
        )

    gains_grad = gain_sums * grad_scale
    gains_weight, left_gains, right_gains = gain_update(gains_grad, gains, gains_left, gains_right)
    return (
        activations,
        input_grad,
        attend_grad,
        attend_weight,
        left_attend,
        right_attend,
        output_grad,
        output_weight,
        left_output,
        right_output,
        expand_grad,
        expand_weight,
        left_expand,
        right_expand,
        reduce_grad,
        reduce_weight,
        left_reduce,
        right_reduce,
        gains_grad,
        gains_weight,
        left_gains,
        right_gains,
    )


def solution(mesh):
    rows = P(("dp", "mp"), None)
    single = P(("dp", "mp"), None, None)
    stacked = P(None, ("dp", "mp"), None, None)
    return jax.shard_map(
        body,
        mesh=mesh,
        in_specs=(
            rows,
            rows,
            P(("dp", "mp")),
            P(("dp", "mp")),
            P("dp", None),
            stacked,
            single,
            stacked,
            single,
            P(),
            stacked,
            stacked,
            single,
            single,
            stacked,
            stacked,
            single,
            single,
            P(),
            P(),
        ),
        out_specs=(
            rows,
            rows,
            stacked,
            stacked,
            stacked,
            stacked,
            single,
            single,
            single,
            single,
            stacked,
            stacked,
            stacked,
            stacked,
            single,
            single,
            single,
            single,
            P(),
            P(),
            P(),
            P(),
        ),
        check_vma=False,
    )
```

```python
import functools
import math

import jax
import jax.numpy as jnp
from jax import lax
from jax.experimental import pallas as pl
from jax.experimental.pallas import tpu as pltpu
from jax.sharding import PartitionSpec as P

D = 1024
HEADS = 16
HD = 64
FF = 2816
BLK = 64
FBLK = 176
ROOTS = 6
OUT_FAN = 8
SPAN = 1024

EPSILON = 1e-05
STEP_RATE = 16.0
GAIN_RATE = 2.0
MASKED = -1e30
F32 = jnp.float32
BF16 = jnp.bfloat16
PAIR = 2 * HD


CHIPS = 4
LANES = 128


def piece_shape(blocked_shape, group_rows, dp_size):
    per_owner, height, width = blocked_shape[-3:]
    column_blocks = dp_size * per_owner // (group_rows // height)
    if per_owner % column_blocks == 0:
        rows, columns = per_owner // column_blocks, column_blocks
    else:
        rows, columns = 1, per_owner
    grid_columns = column_blocks // columns
    return rows, columns, dp_size // grid_columns, grid_columns


def to_piece(blocked, rows, columns):
    leading = blocked.shape[:-3]
    height, width = blocked.shape[-2:]
    grid = blocked.reshape(leading + (rows, columns, height, width))
    return jnp.swapaxes(grid, -3, -2).reshape(leading + (rows * height, columns * width))


def from_piece(piece, rows, columns):
    leading = piece.shape[:-2]
    height, width = piece.shape[-2] // rows, piece.shape[-1] // columns
    grid = piece.reshape(leading + (rows, height, columns, width))
    return jnp.swapaxes(grid, -3, -2).reshape(leading + (rows * columns, height, width))


def rows_of_columns(piece):
    return jnp.swapaxes(piece, -1, -2).reshape(-1, LANES)


def columns_of_rows(rows, members):
    return jnp.swapaxes(rows.reshape(members, -1, LANES), -1, -2)


def rows_of_rows(piece):
    height, width = piece.shape
    return jnp.swapaxes(piece.reshape(height, width // LANES, LANES), 0, 1).reshape(-1, LANES)


def rows_to_rows(rows, blocks):
    grid = jnp.swapaxes(rows.reshape(blocks, -1, LANES), 0, 1)
    return grid.reshape(grid.shape[0], blocks * LANES)


def together(*values):
    return lax.optimization_barrier(values)


def pairwise(values, axis, step):
    return lax.ppermute(values, axis, [(i, i ^ step) for i in range(lax.axis_size(axis))])


def gather_sides(slices):
    return pairwise(slices, "dp", 2), pairwise(slices, "dp", 4), pairwise(slices, "dp", 1)


def gather_corner(across_x, across_y, other, both=None):
    half = across_x.shape[0] // 2
    return (
        pairwise(across_y[:half], "dp", 2),
        pairwise(across_x[half:], "dp", 4),
        pairwise(jnp.concatenate([across_x, across_y]) if both is None else both, "dp", 1),
    )


def gather_end(slices, across_x, across_y, other, corner_x, corner_y, other_sides):
    corner = jnp.concatenate([corner_x, corner_y])
    return (
        slices, across_x, across_y, corner, other, other_sides, other_sides, pairwise(corner, "dp", 1)
    )


def first_slices(pieces):
    return [0] * 6 + [pieces[6].shape[0] - pieces[0].shape[0], 0]


def add_up(*refs):
    total = refs[0][...].astype(F32)
    for ref in refs[1:]:
        total = total + ref[...].astype(F32)
    return total


def add_call(kernel, slices, in_specs, out_specs, out_shape, name, *operands):
    return pl.pallas_call(
        kernel,
        grid=(slices,),
        in_specs=in_specs,
        out_specs=out_specs,
        out_shape=out_shape,
        cost_estimate=moved(sum(v.size // CHIPS for v in operands)),
        name=name,
    )(*operands)


def chip_slice(chip, rows):
    return pl.BlockSpec((1, 1, rows, LANES), lambda k: (chip, k, 0, 0))


def one_slice(rows, first=0, last=None):
    if last is None:
        return pl.BlockSpec((1, rows, LANES), lambda k: (k, 0, 0))
    return pl.BlockSpec((1, rows, LANES), lambda k: (jnp.clip(k, first, last) - first, 0, 0))


def corner_kernel(half, own, received, to_x, to_y):
    total = add_up(own, received)[0].astype(BF16)

    @pl.when(pl.program_id(0) < half)
    def _():
        to_x[...] = total

    @pl.when(pl.program_id(0) >= half)
    def _():
        to_y[...] = total


def corner_sums(own_core, received):
    slices, rows = own_core.shape[1:3]
    half = slices // 2
    shape = jax.ShapeDtypeStruct((half, rows, LANES), BF16)
    to_x, to_y = add_call(
        functools.partial(corner_kernel, half),
        slices,
        [chip_slice(3, rows)] * 2,
        [one_slice(rows, 0, half - 1), one_slice(rows, half, slices - 1)],
        [shape, shape],
        "add_corner",
        own_core,
        received,
    )
    return to_x, to_y


def send_planar(to_x, to_y):
    return pairwise(to_x, "dp", 2), pairwise(to_y, "dp", 4)


def sides_kernel(half, own_x, received_x, own_y, received_y, corner_x, corner_y, to_x, to_y):
    @pl.when(pl.program_id(0) < half)
    def _():
        to_x[...] = add_up(own_x, received_x)[0].astype(BF16)
        to_y[...] = (add_up(own_y, received_y)[0] + corner_x[...].astype(F32)).astype(BF16)

    @pl.when(pl.program_id(0) >= half)
    def _():
        to_x[...] = (add_up(own_x, received_x)[0] + corner_y[...].astype(F32)).astype(BF16)
        to_y[...] = add_up(own_y, received_y)[0].astype(BF16)


def side_sums(own_core, received, corner_x, corner_y):
    slices, rows = own_core.shape[1:3]
    half = slices // 2
    shape = jax.ShapeDtypeStruct((slices, rows, LANES), BF16)
    to_x, to_y = add_call(
        functools.partial(sides_kernel, half),
        slices,
        [chip_slice(1, rows)] * 2
        + [chip_slice(2, rows)] * 2
        + [one_slice(rows, 0, half - 1), one_slice(rows, half, slices - 1)],
        [one_slice(rows)] * 2,
        [shape, shape],
        "add_sides",
        own_core,
        received,
        own_core,
        received,
        corner_x,
        corner_y,
    )
    return to_x, to_y


def own_kernel(own, received, from_x, from_y, kept, sent):
    total = add_up(own, received)[0] + add_up(from_x, from_y)

    @pl.when(pl.program_id(0) == 0)
    def _():
        kept[...] = total

    @pl.when(pl.program_id(0) == 1)
    def _():
        sent[...] = total.astype(BF16)


def own_sums(own_core, received, from_x, from_y):
    rows = own_core.shape[2]
    kept, sent = add_call(
        own_kernel,
        2,
        [chip_slice(0, rows)] * 2 + [one_slice(rows)] * 2,
        [one_slice(rows, 0, 0)] * 2,
        [jax.ShapeDtypeStruct((1, rows, LANES), F32), jax.ShapeDtypeStruct((1, rows, LANES), BF16)],
        "add_own",
        own_core,
        received,
        from_x,
        from_y,
    )
    return kept[0], sent[0]


def coordinate(fast):
    return lax.axis_index("dp").astype(jnp.int32).reshape(1) if fast else jnp.zeros((1,), jnp.int32)


def gather_all(piece):
    return lax.all_gather(lax.all_gather(piece, "mp"), "dp")


def scatter_all(parts):
    reduced = lax.psum_scatter(parts, "dp", scatter_dimension=0, tiled=False)
    return lax.psum_scatter(reduced, "mp", scatter_dimension=0, tiled=False)


def weight_by_columns(master, dp_size):
    rows, columns, grid_rows, grid_columns = piece_shape(master.shape, D, dp_size)
    gathered = gather_all(to_piece(master.astype(BF16), rows, columns))
    mp, members, height, width = gathered.shape[1:]
    grid = gathered.reshape(grid_rows, grid_columns, mp, members, height, width)
    grid = jnp.transpose(grid, (3, 0, 4, 2, 1, 5))
    return grid.reshape(members, grid_rows * height, mp * grid_columns * width)


def weight_by_rows(master, group_rows, dp_size):
    rows, columns, grid_rows, grid_columns = piece_shape(master.shape, group_rows, dp_size)
    gathered = gather_all(to_piece(master.astype(BF16), rows, columns))
    mp, height, width = gathered.shape[1:]
    grid = gathered.reshape(grid_rows, grid_columns, mp, height, width)
    grid = jnp.transpose(grid, (2, 0, 3, 1, 4))
    return grid.reshape(mp * grid_rows * height, grid_columns * width)


def grad_by_columns(matrix, master, dp_size, mp_size):
    rows, columns, grid_rows, grid_columns = piece_shape(master.shape, D, dp_size)
    members = matrix.shape[0]
    height, width = rows * master.shape[-2], columns * master.shape[-1]
    grid = matrix.reshape(members, grid_rows, height, mp_size, grid_columns, width)
    grid = jnp.transpose(grid, (1, 4, 3, 0, 2, 5))
    parts = grid.reshape(dp_size, mp_size, members, height, width)
    return from_piece(scatter_all(parts).astype(F32), rows, columns)


def grad_by_rows(matrix, master, group_rows, dp_size, mp_size):
    rows, columns, grid_rows, grid_columns = piece_shape(master.shape, group_rows, dp_size)
    height, width = rows * master.shape[-2], columns * master.shape[-1]
    grid = matrix.reshape(mp_size, grid_rows, height, grid_columns, width)
    grid = jnp.transpose(grid, (1, 3, 0, 2, 4))
    parts = grid.reshape(dp_size, mp_size, height, width)
    return from_piece(scatter_all(parts).astype(F32), rows, columns)


def cut_columns(matrices, mp_size):
    members, _, width = matrices.shape
    grid = matrices.reshape(members, CHIPS, 2, LANES, mp_size, width // mp_size)
    return jnp.transpose(grid, (1, 2, 4, 0, 5, 3)).reshape(CHIPS, 2, mp_size, -1, LANES)


def join_columns(pieces, members):
    grid = pieces.reshape(pieces.shape[:3] + (members, -1, LANES))
    return jnp.transpose(grid, (3, 0, 1, 5, 2, 4)).reshape(members, D, -1)


def cut_rows(matrix, mp_size):
    grid = matrix.reshape(mp_size, CHIPS, matrix.shape[0] // (mp_size * CHIPS), 2, D // (2 * LANES), LANES)
    return jnp.transpose(grid, (1, 3, 0, 4, 2, 5)).reshape(CHIPS, 2, mp_size, -1, LANES)


def join_rows(pieces):
    grid = pieces.reshape(pieces.shape[:3] + (D // (2 * LANES), -1, LANES))
    return jnp.transpose(grid, (2, 0, 4, 1, 3, 5)).reshape(-1, D)


def lanes_of(device, relative):
    return pl.ds(pl.multiple_of((device ^ relative) * LANES, LANES), LANES)


def half_lanes(device, core, block):
    start = ((device & 1) ^ core) * (D // 2) + block * LANES
    return pl.ds(pl.multiple_of(start, LANES), LANES)


def rows_at(device, chip, height):
    return pl.ds(pl.multiple_of(((device >> 1) ^ chip) * height, 16), height)


def project_kernel(shard_count, device_ref, *refs):
    shards, refs = refs[:shard_count], refs[shard_count:]
    attend_ref, output_ref, query_ref, key_ref, value_ref, window_ref = refs[2 * CHIPS :]
    device = device_ref[0]
    height = attend_ref.shape[1]
    count = query_ref.shape[0]
    for core in range(2):
        for chip in range(CHIPS):
            piece = refs[core * CHIPS + chip]
            lanes = lanes_of(device, 2 * chip + core)
            for member in range(3):
                attend_ref[member, :, lanes] = piece[0, pl.ds(member * height, height), :]
            rows = rows_at(device, chip, height // CHIPS)
            for block in range(D // (2 * LANES)):
                output_ref[rows, half_lanes(device, core, block)] = piece[
                    0, pl.ds(3 * height + block * (height // CHIPS), height // CHIPS), :
                ]
    columns = pl.ds(pl.multiple_of(pl.program_id(0) * height, LANES), height)
    query_ref[...] = dot_back(shards[-1][...], attend_ref[0]).astype(BF16)
    for i, shard in enumerate(shards):
        rows = pl.ds(i * count, count)
        key_ref[rows, :] = dot_back(shard[...], attend_ref[1]).astype(BF16)
        value_ref[rows, :] = dot_back(shard[...], attend_ref[2]).astype(BF16)
        window_ref[rows, :] = shard[:, columns]


def cut_attend_kernel(device_ref, query, key, value, output, first, second):
    device = device_ref[0]
    height = query.shape[0]
    for core, pieces in enumerate((first, second)):
        for chip in range(CHIPS):
            lanes = lanes_of(device, 2 * chip + core)
            for member, matrix in enumerate((query, key, value)):
                pieces[chip, 0, pl.ds(member * height, height), :] = matrix[:, lanes]
            rows = rows_at(device, chip, height // CHIPS)
            for block in range(D // (2 * LANES)):
                pieces[chip, 0, pl.ds(3 * height + block * (height // CHIPS), height // CHIPS), :] = (
                    output[rows, half_lanes(device, core, block)]
                )


def grid_call(
    kernel, grid, in_specs, out_specs, out_shape, name, scratch=(), cost=None, aliases=None
):
    return pl.pallas_call(
        kernel,
        grid_spec=pltpu.PrefetchScalarGridSpec(
            num_scalar_prefetch=1,
            grid=grid,
            in_specs=in_specs,
            out_specs=out_specs,
            scratch_shapes=scratch,
        ),
        out_shape=out_shape,
        input_output_aliases=aliases or {},
        cost_estimate=cost,
        name=name,
    )


def moved(count):
    return pl.CostEstimate(flops=0, bytes_accessed=2 * count, transcendentals=0)


def project(device, shards, pieces):
    slices = pieces[0].shape[0]
    height = D // slices
    count = shards[0].shape[0]
    rows = count * len(shards)
    piece = lambda first: pl.BlockSpec((1, 4 * height, LANES), lambda k, d: (first + k, 0, 0))
    columns = lambda rows: pl.BlockSpec((rows, height), lambda k, d: (0, k))
    wide = lambda rows: jax.ShapeDtypeStruct((rows, D), BF16)
    return grid_call(
        functools.partial(project_kernel, len(shards)),
        (slices,),
        [pl.BlockSpec((count, D), lambda k, d: (0, 0))] * len(shards)
        + [piece(first) for first in first_slices(pieces)],
        [
            pl.BlockSpec((3, height, D), lambda k, d: (0, k, 0)),
            pl.BlockSpec((height, D), lambda k, d: (k, 0)),
            columns(count),
            columns(rows),
            columns(rows),
            columns(rows),
        ],
        [jax.ShapeDtypeStruct((3, D, D), BF16), wide(D), wide(count), wide(rows), wide(rows), wide(rows)],
        "project",
        cost=pl.CostEstimate(
            flops=2 * D * D * (2 * rows + count), bytes_accessed=16 * D * D, transcendentals=0
        ),
    )(device, *shards, *pieces)


def cut_attend(device, matrices, slices):
    height = matrices[0].shape[0] // slices
    matrix = pl.BlockSpec((height, D), lambda k, d: (k, 0))
    piece = pl.BlockSpec((CHIPS, 1, 4 * height, LANES), lambda k, d: (0, k, 0, 0))
    shape = jax.ShapeDtypeStruct((CHIPS, slices, 4 * height, LANES), BF16)
    return grid_call(
        cut_attend_kernel,
        (slices,),
        [matrix] * 4,
        [piece, piece],
        [shape, shape],
        "cut_attend",
        cost=moved(8 * slices * height * D),
    )(device, *matrices)


def hidden_kernel(
    kept, device_ref, normed_ref, grads_ref, *refs
):
    parts = refs[: 6 * CHIPS]
    result_ref, back_ref, first, second = refs[6 * CHIPS + kept : 6 * CHIPS + kept + 4]
    (
        normed_t, grads_t, w_gate, w_up, w_down, hidden_t, dgate_t, dup_t, moved_ref
    ) = refs[6 * CHIPS + kept + 4 :]
    device = device_ref[0]
    width = w_gate.shape[0]
    height = width // CHIPS
    blocks = D // (2 * LANES)

    @pl.when(pl.program_id(0) == 0)
    def _():
        normed_t[...] = normed_ref[...].T
        grads_t[...] = grads_ref[...].T
        result_ref[...] = jnp.zeros_like(result_ref)
        back_ref[...] = jnp.zeros_like(back_ref)

    for core in range(2):
        for chip in range(CHIPS):
            gate, up, down = parts[3 * (core * CHIPS + chip) : 3 * (core * CHIPS + chip + 1)]
            lanes = lanes_of(device, 2 * chip + core)
            w_gate[:, lanes] = gate[0]
            w_up[:, lanes] = up[0]
            for block in range(blocks):
                w_down[rows_at(device, chip, height), half_lanes(device, core, block)] = down[
                    0, pl.ds(block * height, height), :
                ]

    joint = 2 * height

    for j in range(width // joint):
        start = j * joint
        rows = pl.ds(start, joint)
        gate_pre = jnp.dot(w_gate[rows, :], normed_t[...], preferred_element_type=F32)
        up_pre = jnp.dot(w_up[rows, :], normed_t[...], preferred_element_type=F32)
        grad_hidden = jnp.dot(w_down[rows, :], grads_t[...], preferred_element_type=F32)
        sig = jax.nn.sigmoid(gate_pre)
        silu = gate_pre * sig
        hidden = (silu * up_pre).astype(BF16)
        dup = (grad_hidden * silu).astype(BF16)
        dgate = (grad_hidden * up_pre * sig * (1.0 + gate_pre * (1.0 - sig))).astype(BF16)
        hidden_t[rows, :] = hidden
        dup_t[rows, :] = dup
        dgate_t[rows, :] = dgate

        moved_ref[...] = jnp.dot(hidden, grads_ref[...], preferred_element_type=F32).astype(BF16)
        for part in range(2):
            chip = (device >> 1) ^ (2 * j + part)
            for core, pieces in enumerate((first, second)):
                for block in range(blocks):
                    pieces[chip, 0, pl.ds(2 * width + block * height, height), :] = moved_ref[
                        pl.ds(part * height, height), half_lanes(device, core, block)
                    ]
        for member, values in enumerate((dgate, dup)):
            moved_ref[...] = jnp.dot(values, normed_ref[...], preferred_element_type=F32).astype(BF16)
            target = pl.ds(member * width + start, joint)
            for core, pieces in enumerate((first, second)):
                for chip in range(CHIPS):
                    pieces[chip, 0, target, :] = moved_ref[:, lanes_of(device, 2 * chip + core)]

    result_ref[...] += jnp.dot(hidden_t[...].T, w_down[...], preferred_element_type=F32)
    back_ref[...] += jnp.dot(dgate_t[...].T, w_gate[...], preferred_element_type=F32)
    back_ref[...] += jnp.dot(dup_t[...].T, w_up[...], preferred_element_type=F32)


def hidden_layer(device, normed, grads, pieces, width, start, slices, earlier=()):
    count = normed.shape[0]
    whole = pl.BlockSpec((count, D), lambda k, d: (0, 0))
    piece = lambda first, part: pl.BlockSpec(
        (1, width, LANES), lambda k, d: (first + start + k, part, 0)
    )
    out_piece = pl.BlockSpec((CHIPS, 1, 3 * width, LANES), lambda k, d: (0, start + k, 0, 0))
    shape = jax.ShapeDtypeStruct((CHIPS, pieces[0].shape[0], 3 * width, LANES), BF16)
    total = jax.ShapeDtypeStruct((count, D), F32)
    first_kept = 3 + 6 * CHIPS
    return grid_call(
        functools.partial(hidden_kernel, len(earlier)),
        (slices,),
        [whole, whole]
        + [piece(first, part) for first in first_slices(pieces) for part in range(3)]
        + [pl.BlockSpec(memory_space=pl.ANY)] * len(earlier),
        [whole, whole, out_piece, out_piece],
        [total, total, shape, shape],
        "hidden_layer",
        scratch=[
            pltpu.VMEM((D, count), BF16),
            pltpu.VMEM((D, count), BF16),
            pltpu.VMEM((width, D), BF16),
            pltpu.VMEM((width, D), BF16),
            pltpu.VMEM((width, D), BF16),
            pltpu.VMEM((width, count), BF16),
            pltpu.VMEM((width, count), BF16),
            pltpu.VMEM((width, count), BF16),
            pltpu.VMEM((2 * width // CHIPS, D), BF16),
        ],
        cost=pl.CostEstimate(
            flops=18 * slices * width * D * count,
            bytes_accessed=12 * slices * width * D,
            transcendentals=0,
        ),
        aliases={first_kept + i: 2 + i for i in range(len(earlier))},
    )(device, normed, grads, *[piece for piece in pieces for _ in range(3)], *earlier)


def exchanges():
    axes = ("dp", "mp")
    size = lax.axis_size(axes)
    masks = [1 << bit for bit in range(size.bit_length() - 1)]
    if size == 32:
        masks = [3, 5, 9, 17, 7]
    return [(axes, [(i, i ^ mask) for i in range(size)]) for mask in masks]


def scalar_rows(value):
    row = lax.broadcasted_iota(jnp.int32, (32, LANES), 0)
    rows = jnp.zeros((32, LANES), F32)
    for i in range(3):
        part = lax.reduce_precision(value, 8, 7)
        rows = jnp.where(row == i, part, rows)
        value = value - part
    return rows.astype(BF16)


def neighbours(values, axis, steps):
    return [pairwise(values, axis, step) for step in steps]


def sum_of_four(values, others):
    return (values + others[0]) + (others[1] + others[2])


def hash_rows(hashes):
    digits = jnp.stack([hashes >> 14, (hashes >> 7) & 127, hashes & 127])
    rows = digits.astype(BF16).reshape(-1, LANES)
    return jnp.pad(rows, ((0, -rows.shape[0] % 32), (0, 0)))


def rows_hash(rows, count):
    used = 3 * count // LANES
    digits = rows[..., :used, :].reshape(-1, 3, count).astype(F32)
    return ((digits[:, 0] * 128.0 + digits[:, 1]) * 128.0 + digits[:, 2]).reshape(-1)


def gather_small(values):
    for axis, pairs in exchanges():
        values = jnp.concatenate([values, lax.ppermute(values, axis, pairs)], axis=0)
    return values


def sum_small(values):
    for axis, pairs in exchanges():
        values = values + lax.ppermute(values, axis, pairs)
    return values


def fill_bias(bias_ref, query_labels, key_labels, tile, tile_count, history):
    for t in range(tile_count):
        span = SPAN + tile
        key_pos = lax.broadcasted_iota(jnp.int32, (span, tile), 0) + (history - SPAN + t * tile)
        query_pos = lax.broadcasted_iota(jnp.int32, (span, tile), 1) + (history + t * tile)
        same = key_labels[pl.ds(history - SPAN + t * tile, span), :] == query_labels[:, pl.ds(t * tile, tile)]
        bias_ref[t] = jnp.where(same & (key_pos <= query_pos), 0.0, MASKED)


def head_rows(values, head):
    row = lax.broadcasted_iota(jnp.int32, values.shape, 0)
    return jnp.where((row >= head * HD) & (row < (head + 1) * HD), values, jnp.zeros_like(values))


def head_lanes(values, head):
    lane = lax.broadcasted_iota(jnp.int32, values.shape, 1)
    return jnp.where((lane >= head * HD) & (lane < (head + 1) * HD), values, jnp.zeros_like(values))


def attend_kernel(
    tile, history, query_labels, key_labels, q_ref, k_ref, v_ref, o_ref, lse_ref, bias_ref, vt_ref
):
    tile_count = q_ref.shape[0] // tile
    span = SPAN + tile

    @pl.when(pl.program_id(0) == 0)
    def _():
        fill_bias(bias_ref, query_labels, key_labels, tile, tile_count, history)

    vt_ref[...] = v_ref[...].T
    chunk = math.gcd(span, 256)
    for t in range(tile_count):
        base = history - SPAN + t * tile
        queries = (q_ref[pl.ds(t * tile, tile), :] * HD ** (-0.5)).astype(BF16).T
        outputs = []
        for head in range(2):
            rows = head_rows(queries, head)
            scores, maximum = [], None
            for start in range(0, span, chunk):
                part = (
                    jnp.dot(k_ref[pl.ds(base + start, chunk), :], rows, preferred_element_type=F32)
                    + bias_ref[t, pl.ds(start, chunk), :]
                )
                top = jnp.max(part, axis=0, keepdims=True)
                maximum = top if maximum is None else jnp.maximum(maximum, top)
                scores.append(part)
            total, weighted = 0.0, 0.0
            for i, part in enumerate(scores):
                powers = jnp.exp(part - maximum)
                total = total + jnp.sum(powers, axis=0, keepdims=True)
                weighted = weighted + jnp.dot(
                    vt_ref[pl.ds(head * HD, HD), pl.ds(base + i * chunk, chunk)],
                    powers.astype(BF16),
                    preferred_element_type=F32,
                )
            outputs.append(weighted * (1.0 / total))
            lse_ref[0, pl.ds(head, 1), pl.ds(t * tile, tile)] = maximum + jnp.log(total)
        o_ref[pl.ds(t * tile, tile), :] = jnp.concatenate(outputs, axis=0).T.astype(BF16)


def attend_back_kernel(
    tile, history, query_labels, key_labels, q_ref, k_ref, v_ref, o_ref, do_ref, lse_ref,
    dq_ref, dk_ref, dv_ref, bias_ref, kt_ref, dk_acc, dv_acc,
):
    tile_count = q_ref.shape[0] // tile
    span = SPAN + tile

    @pl.when(pl.program_id(0) == 0)
    def _():
        fill_bias(bias_ref, query_labels, key_labels, tile, tile_count, history)

    kt_ref[...] = k_ref[...].T
    dk_acc[...] = jnp.zeros_like(dk_acc)
    dv_acc[...] = jnp.zeros_like(dv_acc)
    for t in range(tile_count):
        base = history - SPAN + t * tile
        scaled = (q_ref[pl.ds(t * tile, tile), :] * HD ** (-0.5)).astype(BF16)
        grads = do_ref[pl.ds(t * tile, tile), :]
        scaled_t, grads_t = scaled.T, grads.T
        product_t = grads_t.astype(F32) * o_ref[pl.ds(t * tile, tile), :].T.astype(F32)
        keys = k_ref[pl.ds(base, span), :]
        values = v_ref[pl.ds(base, span), :]
        grad_queries = []
        for head in range(2):
            scores = (
                jnp.dot(keys, head_rows(scaled_t, head), preferred_element_type=F32) + bias_ref[t]
            )
            attention = jnp.exp(scores - lse_ref[0, pl.ds(head, 1), pl.ds(t * tile, tile)])
            row_terms = jnp.sum(product_t[head * HD : (head + 1) * HD], axis=0, keepdims=True)
            grad_attention = jnp.dot(values, head_rows(grads_t, head), preferred_element_type=F32)
            grad_scores = (attention * (grad_attention - row_terms)).astype(BF16)
            dv_acc[pl.ds(base, span), :] += jnp.dot(
                attention.astype(BF16), head_lanes(grads, head), preferred_element_type=F32
            )
            dk_acc[pl.ds(base, span), :] += jnp.dot(
                grad_scores, head_lanes(scaled, head), preferred_element_type=F32
            )
            grad_queries.append(
                jnp.dot(
                    kt_ref[pl.ds(head * HD, HD), pl.ds(base, span)],
                    grad_scores,
                    preferred_element_type=F32,
                )
            )
        dq_ref[pl.ds(t * tile, tile), :] = (
            jnp.concatenate(grad_queries, axis=0).T * HD ** (-0.5)
        ).astype(BF16)
    dk_ref[...] = dk_acc[...].astype(BF16)
    dv_ref[...] = dv_acc[...].astype(BF16)


def attention_specs(count, window, start):
    whole = lambda shape: pl.BlockSpec(shape, lambda h: (0,) * len(shape))
    specs = []
    for first in (start, 0):
        own = pl.BlockSpec((count, PAIR), lambda h, first=first: (0, first + h))
        seen = pl.BlockSpec((window, PAIR), lambda h, first=first: (0, first + h))
        specs.append((own, seen))
    sums = pl.BlockSpec((1, 2, count), lambda h: (h, 0, 0))
    labels = [whole((1, count)), whole((window, 1))]
    return labels, specs[0], specs[1], sums


def attend(inputs, tile, start, pairs):
    _, _, queries, keys, _ = inputs
    count, window = queries.shape[0], keys.shape[0]
    labels, (own, seen), (own_out, _), sums = attention_specs(count, window, start)
    work = 2 * count * (SPAN + tile) * PAIR * pairs
    return pl.pallas_call(
        functools.partial(attend_kernel, tile, window - count),
        grid=(pairs,),
        in_specs=labels + [own, seen, seen],
        out_specs=[own_out, sums],
        out_shape=[
            jax.ShapeDtypeStruct((count, pairs * PAIR), BF16),
            jax.ShapeDtypeStruct((pairs, 2, count), F32),
        ],
        scratch_shapes=[
            pltpu.VMEM((count // tile, SPAN + tile, tile), F32),
            pltpu.VMEM((PAIR, window), BF16),
        ],
        cost_estimate=pl.CostEstimate(
            flops=4 * work, bytes_accessed=4 * (window + count) * PAIR * pairs, transcendentals=0
        ),
        name="attend",
    )(*inputs)


def attend_back(inputs, context, grads, log_sums, tile, start, pairs):
    _, _, queries, keys, _ = inputs
    count, window = queries.shape[0], keys.shape[0]
    labels, (own, seen), (own_out, seen_out), sums = attention_specs(count, window, start)
    work = 2 * count * (SPAN + tile) * PAIR * pairs
    return pl.pallas_call(
        functools.partial(attend_back_kernel, tile, window - count),
        grid=(pairs,),
        in_specs=labels + [own, seen, seen, own_out, own, sums],
        out_specs=[own_out, seen_out, seen_out],
        out_shape=[
            jax.ShapeDtypeStruct((count, pairs * PAIR), BF16),
            jax.ShapeDtypeStruct((window, pairs * PAIR), BF16),
            jax.ShapeDtypeStruct((window, pairs * PAIR), BF16),
        ],
        scratch_shapes=[
            pltpu.VMEM((count // tile, SPAN + tile, tile), F32),
            pltpu.VMEM((PAIR, window), BF16),
            pltpu.VMEM((window, PAIR), F32),
            pltpu.VMEM((window, PAIR), F32),
        ],
        cost_estimate=pl.CostEstimate(
            flops=10 * work, bytes_accessed=8 * (window + count) * PAIR * pairs, transcendentals=0
        ),
        name="attend_back",
    )(*inputs, context, grads, log_sums)


def project_back_kernel(per_shard, *refs):
    queries, keys, values = refs[0:2], refs[2:4], refs[4:6]
    weights, normed = refs[6:8]
    back_refs, gain_ref, total = refs[8:-2], refs[-2], refs[-1]
    half = queries[0].shape[1]
    shard = lax.div(pl.program_id(0), per_shard)
    back = None
    for member, parts in ((1, keys), (2, values)):
        for i, part in enumerate(parts):
            term = mxu(part[...], weights[member, pl.ds(i * half, half), :])
            back = term if back is None else back + term
    total[...] = back

    @pl.when(shard == len(back_refs) - 1)
    def _():
        total[...] += mxu(queries[0][...], weights[0, pl.ds(0, half), :]) + mxu(
            queries[1][...], weights[0, pl.ds(half, half), :]
        )

    for i, ref in enumerate(back_refs):

        @pl.when(shard == i)
        def _(ref=ref):
            ref[...] = total[...].astype(ref.dtype)

    @pl.when(pl.program_id(0) == 0)
    def _():
        gain_ref[...] = jnp.zeros_like(gain_ref)

    gain_ref[...] += jnp.sum(total[...] * normed[...].astype(F32), axis=0, keepdims=True)


def project_back(first, second, weights, window):
    count, half = first[0].shape
    rows = window.shape[0]
    shards = rows // count
    tile = min(256, count)
    per_shard = count // tile
    shard_spec = lambda width, shard: pl.BlockSpec(
        (tile, width), lambda i: (jnp.clip(i - shard * per_shard, 0, per_shard - 1), 0)
    )
    own = shard_spec(half, shards - 1)
    seen = pl.BlockSpec((tile, half), lambda i: (i, 0))
    wide = pl.BlockSpec((tile, D), lambda i: (i, 0))
    shapes = [
        jax.ShapeDtypeStruct((count, D), BF16 if shard == 0 and shards > 1 else F32)
        for shard in range(shards)
    ]
    outs = pl.pallas_call(
        functools.partial(project_back_kernel, per_shard),
        grid=(rows // tile,),
        in_specs=[own, own, seen, seen, seen, seen, pl.BlockSpec((3, D, D), lambda i: (0, 0, 0)), wide],
        out_specs=[shard_spec(D, shard) for shard in range(shards)]
        + [pl.BlockSpec((1, D), lambda i: (0, 0))],
        out_shape=shapes + [jax.ShapeDtypeStruct((1, D), F32)],
        scratch_shapes=[pltpu.VMEM((tile, D), F32)],
        cost_estimate=pl.CostEstimate(
            flops=2 * D * D * (2 * rows + count), bytes_accessed=12 * rows * D, transcendentals=0
        ),
        name="project_back",
    )(first[0], second[0], first[1], second[1], first[2], second[2], weights, window)
    return outs[:-1], outs[-1]


def split(values):
    high = values.astype(BF16)
    return high, (values - high.astype(F32)).astype(BF16)


def dot_split(first, second, contract):
    dims = ((contract, contract), ((), ()))
    (a, b), (c, d) = split(first), split(second)
    multiply = lambda x, y: lax.dot_general(x, y, dims, preferred_element_type=F32)
    return multiply(a, c) + multiply(b, c) + multiply(a, d)


def total_of(values):
    return jnp.sum(jnp.sum(values, axis=0, keepdims=True), axis=1, keepdims=True)


def mxu(first, second):
    return jnp.dot(first, second, preferred_element_type=F32)


class Chain:
    def __init__(self, matrix, rows, spread):
        self.matrix, self.rows, self.spread = matrix, rows, spread

    def square(self):
        self.low = self.matrix.astype(BF16)
        height = self.rows.shape[0]
        stacked = jnp.concatenate([self.rows.astype(BF16), self.low], axis=0)
        both = mxu(stacked, self.spread(self.low))
        self.rows = 1.25 * self.rows - 0.25 * both[:height]
        self.rest = (0.0625 * both[height:] - 0.625 * self.low.astype(F32)).astype(BF16)

    def half(self):
        self.right = self.spread(self.rest)
        self.matrix = 1.5625 * self.matrix + mxu(self.low, self.right)

    def whole(self):
        self.matrix = 1.5625 * self.matrix + mxu(self.matrix.astype(BF16), self.right)

    def last(self):
        self.rows = 1.25 * self.rows - 0.25 * mxu(
            self.rows.astype(BF16), self.spread(self.matrix.astype(BF16))
        )


def run_chains(chains):
    for _ in range(ROOTS - 1):
        for chain in chains:
            chain.square()
        for chain in chains:
            chain.half()
        for chain in chains:
            chain.whole()
    for chain in chains:
        chain.last()


def quarter(norm):
    return lax.rsqrt(jnp.sqrt(norm))


def shampoo_blocks(step_size, pack, grads, shorts_old, longs_old, short_out, long_out):
    blocks = len(grads)
    short, width = grads[0].shape
    side = pack * short
    row = lax.broadcasted_iota(jnp.int32, (side, side), 0)
    lane = lax.broadcasted_iota(jnp.int32, (side, side), 1)
    mask = jnp.where(lax.div(row, short) == lax.div(lane, short), 1.0, 0.0).astype(BF16)
    eye = jnp.where(
        lax.broadcasted_iota(jnp.int32, (short, side), 0)
        == lax.rem(lax.broadcasted_iota(jnp.int32, (short, side), 1), short),
        1.0,
        0.0,
    )
    spread = lambda values: jnp.concatenate([values] * pack, axis=0) * mask
    beside = lambda values: jnp.concatenate(values, axis=1)
    alone = lambda values: values
    packed_long = width == short

    shorts, longs, scales = [], [], []
    for b, grad in enumerate(grads):
        short_new = 0.5 * shorts_old(b) + 0.5 * dot_split(grad, grad, (1,))
        grad_t = grad.T
        long_new = 0.5 * longs_old(b) + 0.5 * dot_split(grad_t, grad_t, (1,))
        short_out(b, short_new)
        long_out(b, long_new)
        short_norm = jnp.sqrt(total_of(short_new * short_new) + 1e-06)
        long_norm = jnp.sqrt(total_of(long_new * long_new) + 1e-06)
        shorts.append(short_new / short_norm)
        longs.append(long_new / long_norm)
        scales.append(step_size * quarter(short_norm) * quarter(long_norm))
    groups = [range(i, i + pack) for i in range(0, blocks, pack)]
    left = [Chain(beside([shorts[b] for b in g]), eye, spread) for g in groups]
    if packed_long:
        right = [
            Chain(beside([longs[b] for b in g]), beside([grads[b] for b in g]), spread) for g in groups
        ]
    else:
        right = [Chain(longs[b], grads[b], alone) for b in range(blocks)]
    run_chains(left + right)
    steps = []
    for i, g in enumerate(groups):
        high, low = split(left[i].rows)
        if packed_long:
            second, second_low = split(right[i].rows)
            second, second_low = spread(second), spread(second_low)
            total = mxu(high, second) + mxu(low, second) + mxu(high, second_low)
            parts = [total[:, j * short : (j + 1) * short] for j in range(pack)]
        else:
            second, second_low = split(jnp.concatenate([right[b].rows for b in g], axis=0))
            high, low = spread(high), spread(low)
            total = mxu(high, second) + mxu(low, second) + mxu(high, second_low)
            parts = [total[j * short : (j + 1) * short] for j in range(pack)]
        steps += [scales[b] * part for b, part in zip(g, parts)]
    return steps


def put(ref, lead=()):
    def store(b, values):
        ref[lead + (b,)] = values

    return store


def shampoo_kernel(
    step_size, pack, grad_ref, master_ref, short_ref, long_ref, weight_ref, short_out, long_out
):
    blocks = grad_ref.shape[0]
    steps = shampoo_blocks(
        step_size,
        pack,
        [grad_ref[b] for b in range(blocks)],
        lambda b: short_ref[b],
        lambda b: long_ref[b],
        put(short_out),
        put(long_out),
    )
    for b, step in enumerate(steps):
        weight_ref[b] = master_ref[b] - step


def shampoo_rows_kernel(
    step_size, turned, across, kept, scale_ref, own, one, two, master_ref, short_ref, long_ref, *refs
):
    grad_ref, weight_ref, short_out, long_out = refs[kept:]
    rows = own[0] + one[...].astype(F32) + two[...].astype(F32)
    rows = rows * scale_ref[0]
    groups = 4
    height = rows.shape[0] // groups
    grads = [None] * (2 * groups)
    for group in range(groups):
        slab = rows[group * height : (group + 1) * height]
        tall = slab.T if turned else None
        for half in range(2):
            b = half * groups + group if across else 2 * group + half
            lanes = slice(half * BLK, (half + 1) * BLK)
            grads[b] = tall[lanes] if turned else slab[:, lanes]
            grad_ref[0, b] = grads[b]
    steps = shampoo_blocks(
        step_size,
        4,
        grads,
        lambda b: short_ref[0, b],
        lambda b: long_ref[0, b],
        put(short_out, (0,)),
        put(long_out, (0,)),
    )
    for b, step in enumerate(steps):
        weight_ref[0, b] = master_ref[0, b] - step


def shampoo_rows(
    terms, scale, master, short_old, long_old, step_size, first, turned, across, start=0, stop=None, earlier=()
):
    members, blocks, height, width = master.shape
    stop = members if stop is None else stop
    short, long = short_old.shape[-1], long_old.shape[-1]
    rows = blocks // 2 * long
    spec = lambda *shape: pl.BlockSpec((1, blocks) + shape, lambda i: (start + i, 0, 0, 0))
    shape = lambda *dims: jax.ShapeDtypeStruct((members, blocks) + dims, F32)
    term = pl.BlockSpec((rows, LANES), lambda i: (first + start + i, 0))
    own = pl.BlockSpec((1, rows, LANES), lambda i: (0, first + start + i, 0))
    return pl.pallas_call(
        functools.partial(shampoo_rows_kernel, step_size, turned, across, len(earlier)),
        grid=(stop - start,),
        in_specs=[
            pl.BlockSpec(memory_space=pltpu.SMEM),
            own,
            term,
            term,
            spec(height, width),
            spec(short, short),
            spec(long, long),
        ]
        + [pl.BlockSpec(memory_space=pl.ANY)] * len(earlier),
        out_specs=[spec(height, width), spec(height, width), spec(short, short), spec(long, long)],
        out_shape=[shape(height, width), shape(height, width), shape(short, short), shape(long, long)],
        input_output_aliases={7 + i: i for i in range(len(earlier))},
        cost_estimate=pl.CostEstimate(
            flops=160 * (stop - start) * blocks * long * long * long,
            bytes_accessed=8 * (stop - start) * blocks * (long * long + short * short + 2 * short * long),
            transcendentals=0,
        ),
        name="shampoo_rows",
    )(scale.reshape(1), terms[0][None], terms[1], terms[2], master, short_old, long_old, *earlier)


def shampoo(gradient, master, short_old, long_old, step_size, blocks):
    count, short, width = gradient.shape
    blocks = min(blocks, count)
    pack = min(4, blocks)
    spec = lambda *shape: pl.BlockSpec((blocks,) + shape, lambda i: (i, 0, 0))
    specs = [spec(short, width), spec(short, short), spec(width, width)]
    shape = lambda *dims: jax.ShapeDtypeStruct((count,) + dims, F32)
    return pl.pallas_call(
        functools.partial(shampoo_kernel, step_size, pack),
        grid=(count // blocks,),
        in_specs=specs[:1] + specs,
        out_specs=specs,
        out_shape=[shape(short, width), shape(short, short), shape(width, width)],
        cost_estimate=pl.CostEstimate(
            flops=40 * count * width * width * width,
            bytes_accessed=8 * count * (width * width + short * short + 2 * short * width),
            transcendentals=0,
        ),
        name="shampoo",
    )(gradient, master, short_old, long_old)
def step_rows(gradient, master, left, right, step_size, blocks):
    flat = lambda values: values.reshape((-1,) + values.shape[-2:])
    outs = shampoo(flat(gradient), flat(master), flat(left), flat(right), step_size, blocks)
    return tuple(v.reshape(gradient.shape[:-2] + v.shape[-2:]) for v in outs)


def turn(values):
    return jnp.swapaxes(values, -1, -2)


def step_columns(gradient, master, left, right, step_size, blocks):
    weight, right, left = shampoo(turn(gradient), turn(master), right, left, step_size, blocks)
    return turn(weight), left, right


def two_by_two(first, second):
    (a, b), (c, d) = first
    (e, f), (g, h) = second
    return ((a * e + b * g, a * f + b * h), (c * e + d * g, c * f + d * h))


def quarter_root_pair(statistic):
    frobenius = jnp.sqrt(sum(v * v for row in statistic for v in row) + 1e-06)
    matrix = tuple(tuple(v / frobenius for v in row) for row in statistic)
    estimate = ((1.0, 0.0), (0.0, 1.0))
    for iteration in range(ROOTS):
        (a, b), (c, d) = matrix
        update = (((5.0 - a) * 0.25, -b * 0.25), (-c * 0.25, (5.0 - d) * 0.25))
        estimate = two_by_two(estimate, update)
        squared = two_by_two(update, update)
        matrix = two_by_two(two_by_two(squared, squared), matrix)
    scale = lax.rsqrt(jnp.sqrt(frobenius))
    return tuple(tuple(v * scale for v in row) for row in estimate)


def gain_kernel(grad_ref, gain_ref, left_ref, right_ref, weight_ref, left_out, right_out):
    grads = [grad_ref[pl.ds(i, 1), :] for i in range(2)]
    inner = lambda i, j: jnp.sum(grads[i] * grads[j], axis=1, keepdims=True)
    products = ((inner(0, 0), inner(0, 1)), (inner(1, 0), inner(1, 1)))
    left = tuple(
        tuple(
            0.5 * left_ref[pl.ds(i, 1), pl.ds(j, 1)] + 0.5 * products[i][j] for j in range(2)
        )
        for i in range(2)
    )
    left_out[...] = jnp.concatenate([jnp.concatenate(row, axis=1) for row in left], axis=0)
    right = 0.5 * right_ref[...] + 0.5 * (grads[0] * grads[0] + grads[1] * grads[1])
    right_out[...] = right
    root = quarter_root_pair(left)
    scale = GAIN_RATE * lax.rsqrt(jnp.sqrt(right))
    for i in range(2):
        mixed = root[i][0] * grads[0] + root[i][1] * grads[1]
        weight_ref[pl.ds(i, 1), :] = gain_ref[pl.ds(i, 1), :] - scale * mixed


def gain_update(gradient, gain_rows, left_old, right_old):
    shapes = [gain_rows.shape, left_old.shape, (1, right_old.size)]
    weight, left_new, right_new = pl.pallas_call(
        gain_kernel,
        out_shape=[jax.ShapeDtypeStruct(shape, F32) for shape in shapes],
        name="gain_update",
    )(gradient, gain_rows, left_old, right_old.reshape(1, -1))
    return weight, left_new, right_new.reshape(-1)


def dot(first, second):
    return jnp.dot(first, second, preferred_element_type=F32)


def dot_back(first, second):
    return lax.dot_general(first, second, (((1,), (1,)), ((), ())), preferred_element_type=F32)


def dot_weight(first, second):
    return lax.dot_general(first, second, (((0,), (0,)), ((), ())), preferred_element_type=F32)


def body(
    patches,
    cotangent,
    lengths,
    hashes,
    segments,
    attend_master,
    output_master,
    expand_master,
    reduce_master,
    gains,
    attend_left,
    attend_right,
    output_left,
    output_right,
    expand_left,
    expand_right,
    reduce_left,
    reduce_right,
    gains_left,
    gains_right,
):
    dp_size, mp_size = lax.axis_size("dp"), lax.axis_size("mp")
    mp_index = lax.axis_index("mp")
    count = patches.shape[0]
    head_width, hidden_width = D // mp_size, FF // mp_size
    head_rows_width = head_width // CHIPS
    total_patches = count * dp_size * mp_size
    earlier = -(-(SPAN - 1) // count)
    history = earlier * count
    tile = min(256, count)
    fast = dp_size == 2 * CHIPS and mp_size == 4
    device = coordinate(fast)
    grids = {
        name: piece_shape(master.shape, rows, dp_size)
        for name, master, rows in (
            ("attend", attend_master, D),
            ("output", output_master, head_width),
            ("expand", expand_master, D),
            ("reduce", reduce_master, hidden_width),
        )
    }

    stream = patches.astype(F32)
    first_rms = lax.rsqrt(jnp.mean(stream * stream, axis=1, keepdims=True) + EPSILON)
    first_hat = stream * first_rms
    first_normed = (first_hat * gains[0]).astype(BF16)

    row_labels = segments.reshape(-1)
    padded = jnp.concatenate([jnp.full((history,), -1, jnp.int32), row_labels])
    key_labels = lax.dynamic_slice_in_dim(padded, mp_index * count, history + count, 0)
    query_labels = key_labels[history:].reshape(1, count)
    key_labels = key_labels.reshape(-1, 1)
    up_one = [(i, i + 1) for i in range(mp_size - 1)]
    down_one = [(i + 1, i) for i in range(mp_size - 1)]
    half_pairs = HEADS * HD // PAIR // 2

    def count_own(all_hashes):
        own = hashes.astype(F32)
        return jnp.sum((own[:, None] == all_hashes[None, :]).astype(F32), axis=1)

    def halo(values):
        return lax.ppermute(values, "mp", up_one)

    if fast:
        attend_rows = jnp.concatenate(
            [
                rows_of_columns(to_piece(attend_master.astype(BF16), *grids["attend"][:2])),
                rows_of_rows(to_piece(output_master.astype(BF16), *grids["output"][:2])),
                hash_rows(hashes),
            ]
        )
        slice_two = pairwise(attend_rows, "mp", 2)
        slice_one = pairwise(attend_rows, "mp", 1)
        halo_source, slice_two = together(first_normed, slice_two)
        slice_three = pairwise(slice_two, "mp", 1)
        near_halo = halo(halo_source)
        attend_slices = jnp.stack([attend_rows, slice_one, slice_two, slice_three])
        sides = gather_sides(attend_slices)
        near_halo, sides = together(near_halo, sides)
        corners = gather_corner(*sides)
        shards = [near_halo, first_normed]
        for _ in range(earlier - 1):
            shards.insert(0, halo(shards[0]))
        shards[0], corners = together(shards[0], corners)
        attend_pieces = gather_end(attend_slices, *sides, *corners)
        all_hashes = jnp.concatenate(
            [rows_hash(piece[:, 4 * head_width :], count) for i, piece in enumerate(attend_pieces) if i != 6]
        )
    else:
        attend_cut = jnp.concatenate(
            [
                cut_columns(weight_by_columns(attend_master, dp_size), mp_size),
                cut_rows(weight_by_rows(output_master, head_width, dp_size), mp_size),
            ],
            axis=3,
        )
        attend_pieces = [attend_cut[chip, core] for core in range(2) for chip in range(CHIPS)]
        hidden_cut = jnp.concatenate(
            [
                cut_columns(weight_by_columns(expand_master, dp_size), mp_size),
                cut_rows(weight_by_rows(reduce_master, hidden_width, dp_size), mp_size),
            ],
            axis=3,
        )
        near_pieces, far_pieces = (
            [hidden_cut[chip, core, k : k + 2] for core in range(2) for chip in range(CHIPS)]
            for k in (0, 2)
        )
        shards = [first_normed]
        for _ in range(earlier):
            shards.insert(0, halo(shards[0]))
        all_hashes = gather_small(hashes).astype(F32)

    raw_weight = lengths.astype(F32) * lax.rsqrt(count_own(all_hashes))
    raw_total = jnp.sum(raw_weight.reshape(-1, LANES), axis=0, keepdims=True)
    grad_out = cotangent.astype(F32) * raw_weight[:, None]
    grad_low = grad_out.astype(BF16)

    if fast:
        hidden_rows = jnp.concatenate(
            [
                rows_of_columns(to_piece(expand_master.astype(BF16), *grids["expand"][:2])),
                rows_of_rows(to_piece(reduce_master.astype(BF16), *grids["reduce"][:2])),
            ]
        )
        shards[0], hidden_rows = together(shards[0], hidden_rows)
        slice_one = pairwise(hidden_rows, "mp", 1)
    attend_w, output_w, queries, keys, values, window = project(device, shards, attend_pieces)
    labels = (query_labels, key_labels)
    if fast:
        queries, slice_one, late_rows = together(queries, slice_one, hidden_rows)
        slice_two = pairwise(late_rows, "mp", 2)
        near = jnp.stack([hidden_rows, slice_one])
        sides = gather_sides(near)
    inputs = labels + (queries, keys, values)
    context_a, sums_a = attend(inputs, tile, 0, half_pairs)
    if fast:
        queries, context_a, sides, grad_low, raw_total = together(
            queries, context_a, sides, grad_low, raw_total
        )
        near_sides = jnp.concatenate(sides[:2])
        queries, slice_two, near_sides = together(queries, slice_two, near_sides)
        inputs = labels + (queries, keys, values)
        corners = gather_corner(*sides, near_sides)
        slice_three = pairwise(slice_two, "mp", 1)
    context_b, sums_b = attend(inputs, tile, half_pairs, half_pairs)
    if fast:
        context_b, corners, slice_three = together(context_b, corners, slice_three)
        near_pieces = gather_end(near, *sides, *corners)
        total_rows = scalar_rows(raw_total)
        far = jnp.concatenate(
            [jnp.stack([slice_two, slice_three]), jnp.stack([total_rows, total_rows])], axis=1
        )
        sides = gather_sides(far)
    half = context_a.shape[1]
    middle = stream + dot(context_a, output_w[:half]) + dot(context_b, output_w[half:])

    second_rms = lax.rsqrt(jnp.mean(middle * middle, axis=1, keepdims=True) + EPSILON)
    second_hat = middle * second_rms
    second_normed = (second_hat * gains[1]).astype(BF16)
    if fast:
        second_normed, near_pieces = together(second_normed, near_pieces)
        share_a = hidden_layer(device, second_normed, grad_low, near_pieces, hidden_width, 0, 2)
        share_a, sides = together(share_a, sides)
        corners = gather_corner(*sides)
        far_pieces = gather_end(far, *sides, *corners)
        share_b = share_a
        near_grads = share_b[2:]
        near_received = pairwise(near_grads[1], "dp", 1)
        share_c = hidden_layer(device, second_normed, grad_low, far_pieces, hidden_width, 0, 2)
        totals = [
            piece[first, 3 * hidden_width : 3 * hidden_width + 8].astype(F32)
            for piece, first in zip(far_pieces, first_slices(far_pieces))
        ]
        totals = [totals[chip] + totals[CHIPS + chip] for chip in range(CHIPS)]
        totals = (totals[0] + totals[1]) + (totals[2] + totals[3])
        raw_total = (totals[2:3] + totals[1:2]) + totals[0:1]
        share_c, near_received, raw_total = together(share_c, near_received, raw_total)
        along = neighbours(raw_total, "mp", (1, 2, 3))
        far_grads = share_c[2:]
        far_received = pairwise(far_grads[1], "dp", 1)
        near_corners = send_planar(*corner_sums(near_grads[0], near_received))
        second_back = share_a[1] + share_c[1]
        results = (middle, share_a[0], share_c[0])
    else:
        share_a = hidden_layer(device, second_normed, grad_low, near_pieces, hidden_width, 0, 2)
        share_c = hidden_layer(device, second_normed, grad_low, far_pieces, hidden_width, 0, 2)
        near_grads, far_grads = share_a[2:], share_c[2:]
        raw_total = sum_small(raw_total)
        second_back = share_a[1] + share_c[1]
        activations = (middle + share_a[0] + share_c[0]).astype(BF16)


    second_scaled = second_back * gains[1]
    gain_second = jnp.sum(second_back * second_hat, axis=0)
    middle_grad = grad_out + second_rms * (
        second_scaled - second_hat * jnp.mean(second_scaled * second_hat, axis=1, keepdims=True)
    )
    middle_low = middle_grad.astype(BF16)
    grad_context = dot_back(middle_low, output_w).astype(BF16)

    def key_grads(parts):
        return dot_weight(parts[1], window).astype(BF16)

    def weight_grads(context_part, parts, keys_part):
        return [
            dot_weight(parts[0], first_normed).astype(BF16),
            keys_part,
            dot_weight(parts[2], window).astype(BF16),
            dot_weight(context_part, middle_low).astype(BF16),
        ]

    slices_half = mp_size // 2
    if fast:
        grad_context, near_corners, along = together(grad_context, near_corners, along)
        raw_total = sum_of_four(raw_total, along)
        near_sides = side_sums(near_grads[0], near_received, *near_corners)
        grad_context, near_sides = together(grad_context, near_sides)
        near_sides = send_planar(*near_sides)
    weight_scale = total_patches / jnp.sum(raw_total)
    grad_scale = weight_scale * total_patches ** (-0.5)
    backs_a = attend_back(inputs, context_a, grad_context, sums_a, tile, 0, half_pairs)
    keys_a = key_grads(backs_a)
    if fast:
        backs_a, keys_a, near_sides, far_received = together(backs_a, keys_a, near_sides, far_received)
        far_corners = corner_sums(far_grads[0], far_received)
        near_own, near_one = own_sums(near_grads[0], near_received, *near_sides)
        backs_a, far_corners, near_one = together(backs_a, far_corners, near_one)
        far_corners = send_planar(*far_corners)
        near_one = pairwise(near_one, "mp", 1)
    cut_a = cut_attend(device, weight_grads(context_a, backs_a, keys_a), slices_half)
    if fast:
        cut_a, grad_context, far_corners = together(cut_a, grad_context, far_corners)
        far_sides = side_sums(far_grads[0], far_received, *far_corners)
        cut_a, grad_context, far_sides = together(cut_a, grad_context, far_sides)
        far_sides = send_planar(*far_sides)
        received_a = pairwise(cut_a[1], "dp", 1)
    backs_b = attend_back(inputs, context_b, grad_context, sums_b, tile, half_pairs, half_pairs)
    keys_b = key_grads(backs_b)
    if fast:
        backs_b, keys_b, far_sides, received_a, near_one = together(
            backs_b, keys_b, far_sides, received_a, near_one
        )
        far_own, far_three = own_sums(far_grads[0], far_received, *far_sides)
        corners_a = corner_sums(cut_a[0], received_a)
        backs_b, far_three, corners_a = together(backs_b, far_three, corners_a)
        far_three = pairwise(far_three, "mp", 1)
        corners_a = send_planar(*corners_a)
    cut_b = cut_attend(device, weight_grads(context_b, backs_b, keys_b), slices_half)
    if fast:
        backs_b, cut_b, corners_a, far_three = together(backs_b, cut_b, corners_a, far_three)
        sides_a = side_sums(cut_a[0], received_a, *corners_a)
        far_two = (far_own + far_three.astype(F32)).astype(BF16)
        backs_b, cut_b, sides_a, far_two, results = together(backs_b, cut_b, sides_a, far_two, results)
        activations = (results[0] + results[1] + results[2]).astype(BF16)
        sides_a = send_planar(*sides_a)
        far_two = pairwise(far_two, "mp", 2)
        received_b = pairwise(cut_b[1], "dp", 1)
    shares, gain_first = project_back(backs_a, backs_b, attend_w, window)
    gain_sums = jnp.stack([gain_first[0] / gains[0], gain_second])

    def halo_back(share):
        return lax.ppermute(share.astype(BF16), "mp", down_one)

    def first_grad(carried):
        first_back = shares[-1] + carried.astype(F32)
        first_scaled = first_back * gains[0]
        return weight_scale * (
            middle_grad
            + first_rms
            * (first_scaled - first_hat * jnp.mean(first_scaled * first_hat, axis=1, keepdims=True))
        )

    if fast:
        shares, received_b, sides_a, far_two, activations = together(
            shares, received_b, sides_a, far_two, activations
        )
        corners_b = corner_sums(cut_b[0], received_b)
        own_a, one_a = own_sums(cut_a[0], received_a, *sides_a)
        shares, corners_b, one_a, far_two = together(shares, corners_b, one_a, far_two)
        corners_b = send_planar(*corners_b)
        carried = halo_back(shares[0])
        one_a = pairwise(one_a, "mp", 1)
    else:
        carried = halo_back(shares[0])
        for share in shares[1:-1]:
            carried = halo_back(share + carried.astype(F32))
        gain_sums = sum_small(gain_sums)
        input_grad = first_grad(carried)
    reduce_step, output_step = STEP_RATE * FF ** (-0.5), STEP_RATE * OUT_FAN ** (-0.5)
    expand_step = attend_step = STEP_RATE * D ** (-0.5)
    if fast:
        far_two, corners_b = together(far_two, corners_b)
        sides_b = side_sums(cut_b[0], received_b, *corners_b)
        far_two, sides_b = together(far_two, sides_b)
        sides_b = send_planar(*sides_b)
        terms = (near_own, near_one, far_two)
        reduce_out = shampoo_rows(
            terms, grad_scale, turn(reduce_master)[None], reduce_right[None], reduce_left[None],
            reduce_step, 2, True, False,
        )
        reduce_out, terms, sides_b, carried, gain_sums = together(
            reduce_out, terms, sides_b, carried, gain_sums
        )
        own_b, three_b = own_sums(cut_b[0], received_b, *sides_b)
        carried = [(share + carried.astype(F32)).astype(BF16) for share in shares[1:-1]]
        terms, three_b, carried, gain_sums = together(terms, three_b, carried, gain_sums)
        three_b = pairwise(three_b, "mp", 1)
        carried = halo_back(carried[0])
        planar = neighbours(gain_sums, "dp", (2, 4, 6))
        expand_inputs = (grad_scale, expand_master, expand_left, expand_right, expand_step, 0, True, True)
        expand_out = shampoo_rows(terms, *expand_inputs, 0, 1)
        expand_out, terms, three_b, planar = together(expand_out, terms, three_b, planar)
        gain_sums = sum_of_four(gain_sums, planar)
        two_b = (own_b + three_b.astype(F32)).astype(BF16)
        terms, two_b, gain_sums = together(terms, two_b, gain_sums)
        two_b = pairwise(two_b, "mp", 2)
        moved = pairwise(gain_sums, "dp", 1)
        expand_out = shampoo_rows(terms, *expand_inputs, 1, 2, expand_out)
        input_grad = first_grad(carried)
        expand_out, two_b, one_a, input_grad, moved = together(
            expand_out, two_b, one_a, input_grad, moved
        )
        gain_sums = gain_sums + moved
        along = neighbours(gain_sums, "mp", (1, 2, 3))
        terms = (own_a, one_a, two_b)
        attend_out = shampoo_rows(
            terms, grad_scale, attend_master, attend_left, attend_right, attend_step, 0, True, True
        )
        attend_out, terms, along = together(attend_out, terms, along)
        gain_sums = sum_of_four(gain_sums, along)
        output_out = shampoo_rows(
            terms, grad_scale, output_master[None], output_left[None], output_right[None], output_step,
            3, False, False,
        )
        alone = lambda outs: [v[0] for v in outs]
        reduce_grad, reduce_weight, right_reduce, left_reduce = alone(reduce_out)
        reduce_grad, reduce_weight = turn(reduce_grad), turn(reduce_weight)
        expand_grad, expand_weight, left_expand, right_expand = expand_out
        attend_grad, attend_weight, left_attend, right_attend = attend_out
        output_grad, output_weight, left_output, right_output = alone(output_out)
    else:
        hidden_cut = jnp.stack(
            [jnp.concatenate([near_grads[core], far_grads[core]], axis=1) for core in range(2)], axis=1
        )
        attend_cut = jnp.stack(
            [jnp.concatenate([cut_a[core], cut_b[core]], axis=1) for core in range(2)], axis=1
        )
        expand_grad = grad_scale * grad_by_columns(
            join_columns(hidden_cut[:, :, :, : 2 * hidden_width], 2), expand_master, dp_size, mp_size
        )
        reduce_grad = grad_scale * grad_by_rows(
            join_rows(hidden_cut[:, :, :, 2 * hidden_width :]),
            reduce_master,
            hidden_width,
            dp_size,
            mp_size,
        )
        output_grad = grad_scale * grad_by_rows(
            join_rows(attend_cut[:, :, :, 3 * head_width :]), output_master, head_width, dp_size, mp_size
        )
        attend_grad = grad_scale * grad_by_columns(
            join_columns(attend_cut[:, :, :, : 3 * head_width], 3), attend_master, dp_size, mp_size
        )
        reduce_weight, left_reduce, right_reduce = step_columns(
            reduce_grad, reduce_master, reduce_left, reduce_right, reduce_step, 4
        )
        expand_weight, left_expand, right_expand = step_rows(
            expand_grad, expand_master, expand_left, expand_right, expand_step, 8
        )
        output_weight, left_output, right_output = step_rows(
            output_grad, output_master, output_left, output_right, output_step, 8
        )
        attend_weight, left_attend, right_attend = step_rows(
            attend_grad, attend_master, attend_left, attend_right, attend_step, 8
        )

    gains_grad = gain_sums * grad_scale
    gains_weight, left_gains, right_gains = gain_update(gains_grad, gains, gains_left, gains_right)
    return (
        activations,
        input_grad,
        attend_grad,
        attend_weight,
        left_attend,
        right_attend,
        output_grad,
        output_weight,
        left_output,
        right_output,
        expand_grad,
        expand_weight,
        left_expand,
        right_expand,
        reduce_grad,
        reduce_weight,
        left_reduce,
        right_reduce,
        gains_grad,
        gains_weight,
        left_gains,
        right_gains,
    )


def solution(mesh):
    rows = P(("dp", "mp"), None)
    single = P(("dp", "mp"), None, None)
    stacked = P(None, ("dp", "mp"), None, None)
    return jax.shard_map(
        body,
        mesh=mesh,
        in_specs=(
            rows,
            rows,
            P(("dp", "mp")),
            P(("dp", "mp")),
            P("dp", None),
            stacked,
            single,
            stacked,
            single,
            P(),
            stacked,
            stacked,
            single,
            single,
            stacked,
            stacked,
            single,
            single,
            P(),
            P(),
        ),
        out_specs=(
            rows,
            rows,
            stacked,
            stacked,
            stacked,
            stacked,
            single,
            single,
            single,
            single,
            stacked,
            stacked,
            stacked,
            stacked,
            single,
            single,
            single,
            single,
            P(),
            P(),
            P(),
            P(),
        ),
        check_vma=False,
    )
```
